256 devices in a mesh: section: 8 (over x, y_lo), dp: 32 (over y_hi, z, core).
Axes of the slice: x: 4, y: 4 (y_hi: 2, y_lo: 2; y = y_hi * 2 + y_lo), z: 8, core: 2. Of those that a mesh axis runs over, the one named last changes fastest.
Arguments:
- grid_latents: bfloat16 [96, 512, 512], P('dp'), may hold values from -6 to 6
- targets: bfloat16 [96, 512, 512], P('dp'), may hold values from -6 to 6
- g2m_tiles: bfloat16 [4, 128, 128], replicated, may hold values from -0.375 to 0.375
- g2m_cols: int32 [4], replicated, may hold values from 0 to 3
- m2m_tiles: bfloat16 [4, 128, 128], replicated, may hold values from -0.375 to 0.375
- m2m_cols: int32 [4], replicated, may hold values from 0 to 1
- m2g_tiles: bfloat16 [8, 128, 128], replicated, may hold values from -0.375 to 0.375
- m2g_cols: int32 [8], replicated, may hold values from 0 to 1
- w_msg: bfloat16 [8, 512, 512], P('section'), may hold values from -0.25 to 0.25
- w_up: bfloat16 [8, 512, 512], P('section'), may hold values from -0.25 to 0.25
- w_down: bfloat16 [8, 512, 512], P('section'), may hold values from -0.125 to 0.125
- gains: float32 [8, 512], P('section'), may hold values from 0.1 to 1.9
Outputs:
- weight_grads: float32 [8, 3, 512, 512], P('section')
- gain_grads: float32 [8, 512], P('section')
The draws below stay inside these ranges and needn't reach their ends.
Inputs may be any that keep to these rules, and one draw needn't show every extreme that they name: `g2m_cols`: Grid-to-mesh tiles are listed by mesh row block in order, 2 to a block; tile t belongs to row block t // 2; column indices may repeat. `m2m_cols`: mesh tiles are listed by row block in order, 2 to a block; tile t belongs to row block t // 2. `m2g_cols`: Mesh-to-grid tiles are listed by grid row block in order, 2 to a block; tile t belongs to row block t // 2.
All inputs are finite; a program needn't handle non-finite values.
Results may differ from the reference program's by a relative error of at most 0.0034.
Values may be sent and summed in bfloat16 or wider, within the bound.
A program may use at most 64 MiB of HBM per device.

```python
import math
import jax
import jax.numpy as jnp
from jax import lax

D = 512
BLOCK = 128
NODES = 256
GRID = 512
KG = 2
KM = 2
KD = 2
LAYERS = 8
SAMPLES = 96


def with_ends(result, own_key, smallest, top_value):
    extent = result.shape
    spot = [jax.random.randint(jax.random.fold_in(own_key, axis), (), 0, extent[axis]) for axis in range(len(extent))]
    result = result.at[tuple(spot)].set(smallest)
    longest = extent.index(max(extent))
    spot[longest] = (spot[longest] + 1) % extent[longest]
    return result.at[tuple(spot)].set(top_value)


def block_levels(own_key, shape, split, low, largest):
    loudness, own = 1.0, jax.random.fold_in(own_key, 6)
    for dim, shards_of in split:
        draws = jnp.exp(jax.random.uniform(jax.random.fold_in(own, dim), (shards_of,), jnp.float32, low / len(split), largest / len(split)))
        loudness = loudness * jnp.repeat(draws, shape[dim] // shards_of).reshape([-1 if axis == dim else 1 for axis in range(len(shape))])
    return loudness


def normal_values(own_key, shape, width, bound, cuts=(), dtype=jnp.bfloat16):
    loudness = block_levels(own_key, shape, cuts, -0.22, 0.18) if cuts else 1.0
    result = jax.random.normal(own_key, shape, jnp.float32) * width * loudness
    return jnp.minimum(jnp.maximum(result, -bound), bound).astype(dtype)


def setup_inputs(seed: int = 0) -> dict:
    key_of = jax.random.split(jax.random.key(seed), 13)
    return {
        "grid_latents": normal_values(key_of[0], (SAMPLES, GRID, D), 1.0, 6.0, ((0, 32),)),
        "targets": normal_values(key_of[1], (SAMPLES, GRID, D), 1.0, 6.0, ((0, 32),)),
        "g2m_tiles": normal_values(key_of[2], (NODES // BLOCK * KG, BLOCK, BLOCK), (BLOCK * KG) ** -0.5, 0.375),
        "g2m_cols": with_ends(jax.random.randint(key_of[3], (NODES // BLOCK * KG,), 0, GRID // BLOCK), jax.random.fold_in(key_of[3], 1), 0, (GRID // BLOCK) - 1).astype(jnp.int32),
        "m2m_tiles": normal_values(key_of[4], (NODES // BLOCK * KM, BLOCK, BLOCK), (BLOCK * KM) ** -0.5, 0.375),
        "m2m_cols": with_ends(jax.random.randint(key_of[5], (NODES // BLOCK * KM,), 0, NODES // BLOCK), jax.random.fold_in(key_of[5], 1), 0, (NODES // BLOCK) - 1).astype(jnp.int32),
        "m2g_tiles": normal_values(key_of[6], (GRID // BLOCK * KD, BLOCK, BLOCK), (BLOCK * KD) ** -0.5, 0.375),
        "m2g_cols": with_ends(jax.random.randint(key_of[7], (GRID // BLOCK * KD,), 0, NODES // BLOCK), jax.random.fold_in(key_of[7], 1), 0, (NODES // BLOCK) - 1).astype(jnp.int32),
        "w_msg": normal_values(key_of[8], (LAYERS, D, D), D ** -0.5, 0.25, ((0, 8),)),
        "w_up": normal_values(key_of[9], (LAYERS, D, D), D ** -0.5, 0.25, ((0, 8),)),
        "w_down": normal_values(key_of[10], (LAYERS, D, D), (4 * D) ** -0.5, 0.125, ((0, 8),)),
        "gains": jnp.clip(1.0 + 0.18 * jax.random.normal(key_of[11], (LAYERS, D), jnp.float32), 0.1, 1.9),
    }


EPSILON = 1e-05

def block_apply(tiles, cols, source, fanout):
    tile_size = tiles.shape[-1]
    features = source.shape[1]
    blocks = source.reshape(-1, tile_size, features)
    picked = jnp.take(blocks, cols.astype(jnp.int32), axis=0).astype(jnp.float32)
    groups = tiles.shape[0] // fanout
    tiles_four = tiles.astype(jnp.float32).reshape(groups, fanout, tile_size, tile_size)
    picked_four = picked.reshape(groups, fanout, tile_size, features)
    summed = jnp.einsum('rkij,rkjd->rid', tiles_four, picked_four)
    return summed.reshape(groups * tile_size, features)

def block_transpose(tiles, cols, grad, fanout, blocks_out):
    tile_size = tiles.shape[-1]
    features = grad.shape[1]
    groups = tiles.shape[0] // fanout
    tiles_four = tiles.astype(jnp.float32).reshape(groups, fanout, tile_size, tile_size)
    grad_three = grad.astype(jnp.float32).reshape(groups, tile_size, features)
    products = jnp.einsum('rkji,rjd->rkid', tiles_four, grad_three).reshape(tiles.shape[0], tile_size, features)
    summed = jax.ops.segment_sum(products, cols.astype(jnp.int32), num_segments=blocks_out)
    return summed.reshape(blocks_out * tile_size, features)

def layer_forward(inputs, weights, tiles, cols):
    w_m, w_u, w_d, gain = weights
    center = inputs - lax.optimization_barrier(jnp.mean(inputs, axis=-1, keepdims=True))
    inverse = lax.rsqrt(lax.optimization_barrier(jnp.mean(center * center, axis=-1, keepdims=True)) + EPSILON)
    normed = center * inverse
    unit = (normed * gain).astype(jnp.bfloat16)
    message = jnp.dot(unit, w_m, preferred_element_type=jnp.float32).astype(jnp.bfloat16)
    before = jnp.dot(unit, w_u, preferred_element_type=jnp.float32) + block_apply(tiles, cols, message, KM)
    active = jax.nn.silu(before).astype(jnp.bfloat16)
    output = inputs + jnp.dot(active, w_d, preferred_element_type=jnp.float32)
    return (output, (normed, inverse, unit, before, active))

def layer_backward(inputs, upstream, weights, tiles, cols, blocks_out):
    w_m, w_u, w_d, gain = weights
    unused, saved = layer_forward(inputs, weights, tiles, cols)
    normed, inverse, unit, before, active = saved
    grad_down = jnp.dot(active.T, upstream, preferred_element_type=jnp.float32)
    grad_active = jnp.dot(upstream, w_d.T, preferred_element_type=jnp.float32)
    sigma = jax.nn.sigmoid(before)
    grad_before = (grad_active * sigma * (1.0 + before * (1.0 - sigma))).astype(jnp.bfloat16)
    grad_up = jnp.dot(unit.T, grad_before, preferred_element_type=jnp.float32)
    grad_message = block_transpose(tiles, cols, grad_before, KM, blocks_out).astype(jnp.bfloat16)
    grad_msgw = jnp.dot(unit.T, grad_message, preferred_element_type=jnp.float32)
    grad_unit = jnp.dot(grad_before, w_u.T, preferred_element_type=jnp.float32) + jnp.dot(grad_message, w_m.T, preferred_element_type=jnp.float32)
    grad_gain = lax.optimization_barrier(jnp.sum(grad_unit * normed, axis=0))
    grad_normed = grad_unit * gain
    grad_inputs = upstream.astype(jnp.float32) + inverse * (grad_normed - lax.optimization_barrier(jnp.mean(grad_normed, axis=-1, keepdims=True)) - normed * lax.optimization_barrier(jnp.mean(grad_normed * normed, axis=-1, keepdims=True)))
    return (grad_inputs, (grad_msgw, grad_up, grad_down, grad_gain))

def reference(grid_latents, targets, g2m_tiles, g2m_cols, m2m_tiles, m2m_cols, m2g_tiles, m2g_cols, w_msg, w_up, w_down, gains):
    tile_size = m2m_tiles.shape[-1]
    mesh_blocks = NODES // tile_size
    loss_scale = 1.0 / math.sqrt(SAMPLES * GRID)

    def sample_step(totals, sample):
        grid_rows, target = sample
        rows = block_apply(g2m_tiles, g2m_cols, grid_rows, KG).astype(jnp.bfloat16)
        inputs = []
        for layer in range(LAYERS):
            inputs.append(rows)
            weights = (w_msg[layer], w_up[layer], w_down[layer], gains[layer])
            output, unused = layer_forward(rows.astype(jnp.float32), weights, m2m_tiles, m2m_cols)
            rows = output.astype(jnp.bfloat16)
        predicted = block_apply(m2g_tiles, m2g_cols, rows, KD)
        residual = ((predicted - target.astype(jnp.float32)) * loss_scale).astype(jnp.bfloat16)
        upstream = block_transpose(m2g_tiles, m2g_cols, residual, KD, mesh_blocks).astype(jnp.bfloat16)
        grad_m, grad_u, grad_d, grad_g = totals
        for layer in reversed(range(LAYERS)):
            weights = (w_msg[layer], w_up[layer], w_down[layer], gains[layer])
            grad_inputs, terms = layer_backward(inputs[layer].astype(jnp.float32), upstream, weights, m2m_tiles, m2m_cols, mesh_blocks)
            upstream = grad_inputs.astype(jnp.bfloat16)
            grad_m = grad_m.at[layer].add(terms[0])
            grad_u = grad_u.at[layer].add(terms[1])
            grad_d = grad_d.at[layer].add(terms[2])
            grad_g = grad_g.at[layer].add(terms[3])
        return ((grad_m, grad_u, grad_d, grad_g), None)
    square = jnp.zeros((LAYERS, D, D), jnp.float32)
    start = (square, square, square, jnp.zeros((LAYERS, D), jnp.float32))
    totals, unused = lax.scan(sample_step, start, (grid_latents, targets))
    return (jnp.stack([totals[0], totals[1], totals[2]], axis=1), totals[3])
```

```python
import functools
import math

import jax
import jax.numpy as jnp
from jax import lax
from jax.experimental import pallas as pl
from jax.experimental.pallas import tpu as pltpu
from jax.sharding import PartitionSpec as P

BLOCK = 128
NODES = 256
EPSILON = 1e-05
MESH = pl.DeviceIdType.MESH
F32 = jnp.float32
BF16 = jnp.bfloat16
CHUNKS = 2
CORES = 2
RING = 8
STEPS = RING - 1
SUBS = 2


def dot(a, b):
    return jnp.dot(a, b, preferred_element_type=F32)


def dot_nt(a, b):
    return lax.dot_general(a, b, (((1,), (1,)), ((), ())), preferred_element_type=F32)


def step_kernel(
    sections,
    halves,
    samples,
    loss_scale,
    lat_hbm,
    tgt_hbm,
    g2m_hbm,
    g2m_c,
    m2m_hbm,
    m2m_c,
    m2g_hbm,
    m2g_c,
    wm_hbm,
    wu_hbm,
    wd_hbm,
    gain_hbm,
    out,
    gain_out,
    lat,
    tgt,
    g2m,
    m2m,
    m2g,
    wm,
    wu,
    wd,
    gain_v,
    mix,
    mix_t,
    enc,
    pred,
    seed_t,
    xin,
    xout,
    gin,
    gout,
    unit_s,
    unit_t,
    act_t,
    slope_s,
    normed_s,
    inv_s,
    msg_s,
    up_s,
    gb_s,
    gm_s,
    acc,
    gacc,
    sib_buf,
    ring_buf,
    y_buf,
    g_sib,
    g_y,
    g_z,
    in_sem,
    lat_sem,
    tgt_sem,
    f_send,
    f_recv,
    b_send,
    b_recv,
    sib_send,
    sib_recv,
    rs_send,
    rs_recv,
    y_send,
    y_recv,
    ag_send,
    ag_recv,
    fw_send,
    fw_recv,
    gs_sem,
    gy_sem,
    gz_send,
    gz_recv,
):
    features = wm.shape[-1]
    s = lax.axis_index("section")
    dp = lax.axis_index("dp")
    core = lax.rem(dp, CORES)
    z = lax.rem(dp // CORES, RING)
    yh = dp // (CORES * RING)
    first = s == 0
    last = s == sections - 1
    not_first = s > 0
    not_last = s < sections - 1

    def dp_at(y_, z_, c_):
        return {"dp": (y_ * RING + z_) * CORES + c_}

    sibling = dp_at(yh, z, 1 - core)
    across = dp_at(1 - yh, z, core)
    z_next = lax.rem(z + 1, RING)
    z_prev = lax.rem(z + RING - 1, RING)

    barrier = pltpu.get_barrier_semaphore()

    def greet(where):
        pl.semaphore_signal(barrier, inc=1, device_id=where, device_id_type=MESH)

    @pl.when(not_first)
    def _():
        greet({"section": s - 1})

    @pl.when(not_last)
    def _():
        greet({"section": s + 1})

    greet(sibling)
    greet(across)
    for d in range(1, RING):
        greet(dp_at(yh, lax.rem(z + d, RING), core))

    loads = [
        pltpu.make_async_copy(a, b, in_sem.at[i])
        for i, (a, b) in enumerate(
            [
                (g2m_hbm, g2m),
                (m2m_hbm, m2m),
                (wm_hbm.at[0], wm),
                (wu_hbm.at[0], wu),
                (wd_hbm.at[0], wd),
                (gain_hbm, gain_v),
                (m2g_hbm, m2g),
            ]
        )
    ]

    def lat_load(j):
        return pltpu.make_async_copy(lat_hbm.at[j], lat.at[j], lat_sem.at[j])

    def tgt_load(j):
        return pltpu.make_async_copy(tgt_hbm.at[j], tgt.at[j], tgt_sem.at[j])

    loads[0].start()

    @pl.when(first)
    def _():
        for j in range(samples):
            lat_load(j).start()

    for load in loads[1:]:
        load.start()

    @pl.when(last)
    def _():
        for j in range(samples):
            tgt_load(j).start()

    acc[...] = jnp.zeros_like(acc)
    gacc[...] = jnp.zeros_like(gacc)

    for load in loads:
        load.wait()

    def kept_if(col, b, tile):
        return jnp.where(jnp.full(tile.shape, col, jnp.int32) == b, tile, jnp.zeros_like(tile))

    for k in range(2):
        for r in range(2):
            tile = m2m[2 * r + k]
            for b in range(2):
                kept = kept_if(m2m_c[2 * r + k], b, tile)
                mix[r * BLOCK : (r + 1) * BLOCK, (2 * k + b) * BLOCK : (2 * k + b + 1) * BLOCK] = kept
                mix_t[b * BLOCK : (b + 1) * BLOCK, (2 * k + r) * BLOCK : (2 * k + r + 1) * BLOCK] = kept.T

    @pl.when(first)
    def _():
        for t in range(4):
            for b in range(4):
                k, r = t % 2, t // 2
                kept = kept_if(g2m_c[t], b, g2m[t])
                enc[r * BLOCK : (r + 1) * BLOCK, (4 * k + b) * BLOCK : (4 * k + b + 1) * BLOCK] = kept

    @pl.when(last)
    def _():
        for t in range(8):
            tile_t = m2g[t].T
            for b in range(2):
                k, r = t % 2, t // 2
                kept = kept_if(m2g_c[t], b, m2g[t])
                pred[r * BLOCK : (r + 1) * BLOCK, (2 * k + b) * BLOCK : (2 * k + b + 1) * BLOCK] = kept
                kept = kept_if(m2g_c[t], b, tile_t)
                seed_t[b * BLOCK : (b + 1) * BLOCK, (4 * k + r) * BLOCK : (4 * k + r + 1) * BLOCK] = kept

    pl.semaphore_wait(
        barrier, RING + 1 + jnp.where(first, 0, 1) + jnp.where(last, 0, 1)
    )

    span = NODES // CHUNKS

    def rows_of(c):
        return pl.ds(c * span, span)

    def send_f(j, c):
        return pltpu.make_async_remote_copy(
            src_ref=xout.at[j, rows_of(c)],
            dst_ref=xin.at[j, rows_of(c)],
            send_sem=f_send.at[j, c],
            recv_sem=f_recv.at[j, c],
            device_id={"section": jnp.minimum(s + 1, sections - 1)},
            device_id_type=MESH,
        )

    def send_b(j, c):
        return pltpu.make_async_remote_copy(
            src_ref=gout.at[j, rows_of(c)],
            dst_ref=gin.at[j, rows_of(c)],
            send_sem=b_send.at[j, c],
            recv_sem=b_recv.at[j, c],
            device_id={"section": jnp.maximum(s - 1, 0)},
            device_id_type=MESH,
        )

    def forward(j):
        @pl.when(first)
        def _():
            lat_load(j).wait()
            grid_rows = lat.shape[1]
            xin[j] = (dot(enc[:, :grid_rows], lat[j]) + dot(enc[:, grid_rows:], lat[j])).astype(BF16)

        gain = gain_v[...]
        for c in range(CHUNKS):
            rows = rows_of(c)

            @pl.when(not_first)
            def _():
                send_f(j, c).wait_recv()

            x = xin[j, rows, :].astype(F32)
            center = x - jnp.mean(x, axis=-1, keepdims=True)
            inverse = lax.rsqrt(jnp.mean(center * center, axis=-1, keepdims=True) + EPSILON)
            normed = center * inverse
            unit = (normed * gain).astype(BF16)
            normed_s[j, rows, :] = normed
            inv_s[j, rows, :] = jnp.broadcast_to(inverse, (span, 128))
            unit_s[rows, :] = unit
            msg = dot(unit, wm[...]).astype(BF16)
            for k in range(2):
                msg_s[pl.ds(k * NODES + c * span, span), :] = msg
            up_s[rows, :] = dot(unit, wu[...])
        for c in range(CHUNKS):
            rows = rows_of(c)
            before = up_s[rows, :] + dot(mix[rows, :], msg_s[...])
            sigma = 1.0 / (1.0 + jnp.exp(-before))
            active = (before * sigma).astype(BF16)
            slope_s[j, rows, :] = sigma * (1.0 + before * (1.0 - sigma))
            gb_s[rows, :] = active
            output = xin[j, rows, :].astype(F32) + dot(active, wd[...])
            xout[j, rows, :] = output.astype(BF16)

            @pl.when(not_last)
            def _():
                send_f(j, c).start()

        unit_t[j] = unit_s[...].T
        act_t[j] = gb_s[pl.ds(0, NODES), :].T

        @pl.when(last)
        def _():
            tgt_load(j).wait()
            upstream = jnp.zeros((NODES, features), F32)
            for r in range(4):
                here = pl.ds(r * BLOCK, BLOCK)
                predicted = dot(pred[here, :NODES], xout[j]) + dot(pred[here, NODES:], xout[j])
                target = tgt[j, r * BLOCK : (r + 1) * BLOCK, :].astype(F32)
                residual = ((predicted - target) * loss_scale).astype(BF16)
                for k in range(2):
                    part = seed_t[:, (4 * k + r) * BLOCK : (4 * k + r + 1) * BLOCK]
                    upstream = upstream + dot(part, residual)
            gin[j] = upstream.astype(BF16)

    def backward(j):
        gain = gain_v[...]
        for c in range(CHUNKS):
            rows = rows_of(c)

            @pl.when(not_last)
            def _():
                send_b(j, c).wait_recv()

            grad_active = dot_nt(gin[j, rows, :], wd[...])
            grad_before = (grad_active * slope_s[j, rows, :]).astype(BF16)
            for k in range(2):
                gb_s[pl.ds(k * NODES + c * span, span), :] = grad_before
        gm_s[...] = dot(mix_t[...], gb_s[...]).astype(BF16)
        for c in range(CHUNKS):
            rows = rows_of(c)
            grad_unit = dot_nt(gb_s[rows, :], wu[...]) + dot_nt(gm_s[rows, :], wm[...])
            normed = normed_s[j, rows, :]
            product = grad_unit * normed
            gacc[...] = gacc[...] + jnp.sum(product.reshape(span // 8, 8, features), axis=0)

            @pl.when(not_first)
            def _():
                grad_normed = grad_unit * gain
                inverse = inv_s[j, rows, :][:, :1]
                grad_inputs = gin[j, rows, :].astype(F32) + inverse * (
                    grad_normed
                    - jnp.mean(grad_normed, axis=-1, keepdims=True)
                    - normed * jnp.mean(grad_normed * normed, axis=-1, keepdims=True)
                )
                gout[j, rows, :] = grad_inputs.astype(BF16)
                send_b(j, c).start()

        acc[0:features, :] += dot(unit_t[j], gm_s[...])
        acc[features : 2 * features, :] += dot(unit_t[j], gb_s[pl.ds(0, NODES), :])
        acc[2 * features :, :] += dot(act_t[j], gin[j])

    @pl.loop(0, 2 * samples)
    def _(t):
        going_back = jnp.where(last, lax.rem(t, 2), t // samples)
        j = jnp.where(last, t // 2, lax.rem(t, samples))

        @pl.when(going_back == 0)
        def _():
            forward(j)

        @pl.when(going_back == 1)
        def _():
            backward(j)

    half = acc.shape[0] // CORES
    arm = half // 2
    piece = arm // RING
    sub = piece // SUBS

    def remote(src, dst, send, recv, where):
        return pltpu.make_async_remote_copy(
            src_ref=src, dst_ref=dst, send_sem=send, recv_sem=recv, device_id=where, device_id_type=MESH
        )

    def arm_rows(c, d):
        return pl.ds(pl.multiple_of(c * half + d * arm, 8), arm)

    def sub_rows(d, chunk, u):
        return pl.ds(pl.multiple_of(core * half + d * arm + chunk * piece + u * sub, 8), sub)

    def piece_rows(d, chunk):
        return pl.ds(pl.multiple_of(core * half + d * arm + chunk * piece, 16), piece)

    def to_sib(d):
        return remote(acc.at[arm_rows(1 - core, d)], sib_buf.at[d], sib_send.at[d], sib_recv.at[d], sibling)

    g_to_sib = remote(gacc, g_sib, gs_sem.at[0], gs_sem.at[1], sibling)
    g_to_sib.start()
    for d in range(2):
        to_sib(d).start()

    def toward(d):
        return dp_at(yh, z_next if d == 0 else z_prev, core)

    def chunk_at(d, shift):
        return lax.rem(z - shift + 2 * RING, RING) if d == 0 else lax.rem(z + shift, RING)

    def rs(d, t, u):
        rows = sub_rows(d, chunk_at(d, t + 1), u)
        return remote(acc.at[rows], ring_buf.at[d, t, u], rs_send.at[d, t, u], rs_recv.at[d, t, u], toward(d))

    def y_copy(d, u):
        return remote(acc.at[sub_rows(d, z, u)], y_buf.at[d, u], y_send.at[d, u], y_recv.at[d, u], across)

    for d in range(2):
        to_sib(d).wait()
        rows = arm_rows(core, d)
        acc[rows, :] += sib_buf[d]
        for u in range(SUBS):
            rs(d, 0, u).start()

    g_to_sib.wait()
    gacc[...] += g_sib[...]
    g_to_y = remote(gacc, g_y, gy_sem.at[0], gy_sem.at[1], across)
    g_to_y.start()

    @pl.loop(0, STEPS)
    def _(t):
        for u in range(SUBS):
            for d in range(2):
                rs(d, t, u).wait_recv()
                rows = sub_rows(d, chunk_at(d, t + 2), u)
                acc[rows, :] += ring_buf[d, t, u]

                @pl.when(t < STEPS - 1)
                def _():
                    rs(d, t + 1, u).start()

                @pl.when(t == STEPS - 1)
                def _():
                    y_copy(d, u).start()

    def all_gather(d, t):
        rows = piece_rows(d, chunk_at(d, t))
        return remote(out.at[rows], out.at[rows], ag_send.at[d, t], ag_recv.at[d, t], toward(d))

    def all_gather_in(d, t):
        rows = piece_rows(d, chunk_at(d, t + 1))
        return remote(out.at[rows], out.at[rows], ag_send.at[d, t], ag_recv.at[d, t], toward(d))

    def hand_over(d, t):
        rows = piece_rows(d, chunk_at(d, t))
        return remote(out.at[rows], out.at[rows], fw_send.at[d, t], fw_recv.at[d, t], sibling)

    g_to_y.wait()
    g_z[z] = gacc[...] + g_y[...]

    def g_spread(d):
        return remote(g_z.at[z], g_z.at[z], gz_send.at[d - 1], gz_recv.at[d - 1], dp_at(yh, lax.rem(z + d, RING), core))

    def g_arrive(d):
        at = lax.rem(z - d + RING, RING)
        return remote(g_z.at[at], g_z.at[at], gz_send.at[d - 1], gz_recv.at[d - 1], dp_at(yh, at, core))

    for d in range(1, RING):
        g_spread(d).start()

    for d in range(2):
        for u in range(SUBS):
            y_copy(d, u).wait()
        total = acc[piece_rows(d, z), :] + y_buf[d].reshape(piece, features)
        out[piece_rows(d, z), :] = total.astype(BF16)
        all_gather(d, 0).start()
        hand_over(d, 0).start()

    @pl.loop(0, STEPS)
    def _(t):
        for d in range(2):
            all_gather_in(d, t).wait_recv()

            @pl.when(t < STEPS - 1)
            def _():
                all_gather(d, t + 1).start()

            hand_over(d, t + 1).start()

    for d in range(1, RING):
        g_arrive(d).wait_recv()
    total = g_z[0]
    for i in range(1, RING):
        total = total + g_z[i]
    gain_out[...] = jnp.broadcast_to(jnp.sum(total, axis=0, keepdims=True), gain_out.shape)

    def hand_over_in(d, t):
        at = pl.ds(pl.multiple_of((1 - core) * half + d * arm + chunk_at(d, t) * piece, 16), piece)
        return remote(out.at[at], out.at[at], fw_send.at[d, t], fw_recv.at[d, t], sibling)

    @pl.loop(0, RING)
    def _(t):
        for d in range(2):
            hand_over_in(d, t).wait_recv()
            hand_over(d, t).wait_send()

    @pl.loop(0, STEPS)
    def _(t):
        for d in range(2):
            all_gather(d, t).wait_send()
            for u in range(SUBS):
                rs(d, t, u).wait_send()

    for d in range(1, RING):
        g_spread(d).wait_send()

    @pl.loop(0, samples)
    def _(j):
        for c in range(CHUNKS):

            @pl.when(not_last)
            def _():
                send_f(j, c).wait_send()

            @pl.when(not_first)
            def _():
                send_b(j, c).wait_send()


def on_device(sections, replicas, *args):
    lat, tgt, g2m, g2m_c, m2m, m2m_c, m2g, m2g_c, wm, wu, wd, gains = args
    samples, grid_rows, features = lat.shape
    halves = replicas // (CORES * RING)
    loss_scale = 1.0 / math.sqrt(samples * replicas * grid_rows)
    any_spec = pl.BlockSpec(memory_space=pl.ANY)
    smem_spec = pl.BlockSpec(memory_space=pltpu.SMEM)
    vmem_spec = pl.BlockSpec(memory_space=pltpu.VMEM)
    total_rows = 3 * features
    piece = total_rows // CORES // 2 // RING
    dma = pltpu.SemaphoreType.DMA
    v = pltpu.VMEM
    tile = (BLOCK, BLOCK)
    per_sample = (samples, NODES, features)
    out, gain_out = pl.pallas_call(
        functools.partial(step_kernel, sections, halves, samples, loss_scale),
        out_shape=(
            jax.ShapeDtypeStruct((total_rows, features), BF16),
            jax.ShapeDtypeStruct((8, features), F32),
        ),
        in_specs=[any_spec, any_spec, any_spec, smem_spec, any_spec, smem_spec, any_spec, smem_spec]
        + [any_spec] * 4,
        out_specs=(vmem_spec, vmem_spec),
        scratch_shapes=[
            v((samples, grid_rows, features), BF16),
            v((samples, grid_rows, features), BF16),
            v((4,) + tile, BF16),
            v((4,) + tile, BF16),
            v((8,) + tile, BF16),
            v((features, features), BF16),
            v((features, features), BF16),
            v((features, features), BF16),
            v((1, features), F32),
            v((NODES, 2 * NODES), BF16),
            v((NODES, 2 * NODES), BF16),
            v((NODES, 2 * grid_rows), BF16),
            v((grid_rows, 2 * NODES), BF16),
            v((NODES, 2 * grid_rows), BF16),
            v(per_sample, BF16),
            v(per_sample, BF16),
            v(per_sample, BF16),
            v(per_sample, BF16),
            v((NODES, features), BF16),
            v((samples, features, NODES), BF16),
            v((samples, features, NODES), BF16),
            v(per_sample, F32),
            v(per_sample, F32),
            v((samples, NODES, 128), F32),
            v((2 * NODES, features), BF16),
            v((NODES, features), F32),
            v((2 * NODES, features), BF16),
            v((NODES, features), BF16),
            v((total_rows, features), F32),
            v((8, features), F32),
            v((2, total_rows // CORES // 2, features), F32),
            v((2, STEPS, SUBS, piece // SUBS, features), F32),
            v((2, SUBS, piece // SUBS, features), F32),
            v((8, features), F32),
            v((8, features), F32),
            v((RING, 8, features), F32),
            dma((7,)),
            dma((samples,)),
            dma((samples,)),
            dma((samples, CHUNKS)),
            dma((samples, CHUNKS)),
            dma((samples, CHUNKS)),
            dma((samples, CHUNKS)),
            dma((2,)),
            dma((2,)),
            dma((2, STEPS, SUBS)),
            dma((2, STEPS, SUBS)),
            dma((2, SUBS)),
            dma((2, SUBS)),
            dma((2, STEPS)),
            dma((2, STEPS)),
            dma((2, RING)),
            dma((2, RING)),
            dma((2,)),
            dma((2,)),
            dma((STEPS,)),
            dma((STEPS,)),
        ],
        compiler_params=pltpu.CompilerParams(
            collective_id=0, has_side_effects=True, vmem_limit_bytes=48 * 1024 * 1024
        ),
        name="train_step",
    )(*args)
    weight_grads = out.astype(F32).reshape(1, 3, features, features)
    return weight_grads, gain_out[:1]


def solution(mesh):
    placed = (
        P("dp", None, None),
        P("dp", None, None),
        P(),
        P(),
        P(),
        P(),
        P(),
        P(),
        P("section", None, None),
        P("section", None, None),
        P("section", None, None),
        P("section", None),
    )
    return jax.shard_map(
        functools.partial(on_device, mesh.shape["section"], mesh.shape["dp"]),
        mesh=mesh,
        in_specs=placed,
        out_specs=(P("section", None, None, None), P("section", None)),
        check_vma=False,
    )
```

```python
import functools
import math

import jax
import jax.numpy as jnp
from jax import lax
from jax.experimental import pallas as pl
from jax.experimental.pallas import tpu as pltpu
from jax.sharding import PartitionSpec as P

BLOCK = 128
NODES = 256
EPSILON = 1e-05
MESH = pl.DeviceIdType.MESH
F32 = jnp.float32
BF16 = jnp.bfloat16
CHUNKS = 2
LAYERS = 4
CORES = 2
RING = 8
STEPS = RING - 1
FAR = RING // 2
SUM = True


def dot(a, b):
    return jnp.dot(a, b, preferred_element_type=F32)


def dot_nt(a, b):
    return lax.dot_general(a, b, (((1,), (1,)), ((), ())), preferred_element_type=F32)


def step_kernel(
    samples,
    loss_scale,
    lat_hbm,
    tgt_hbm,
    g2m_hbm,
    g2m_c_hbm,
    m2m_hbm,
    m2m_c_hbm,
    m2g_hbm,
    m2g_c_hbm,
    wm_hbm,
    wu_hbm,
    wd_hbm,
    gain_hbm,
    out,
    gain_out,
    lat,
    tgt,
    g2m,
    m2m,
    m2g,
    g2m_c,
    m2m_c,
    m2g_c,
    w,
    gain_v,
    gains,
    mix,
    mix_t,
    enc,
    pred,
    seed_t,
    h,
    up,
    unit_s,
    act_s,
    gb_s,
    gp_s,
    slope_s,
    normed_s,
    inv_s,
    msg_s,
    up_s,
    gm_s,
    unit_t,
    act_t,
    acc,
    gacc,
    sib_buf,
    ring_buf,
    y_buf,
    g_sib,
    g_y,
    g_z,
    in_sem,
    io_sem,
    wt_send,
    wt_recv,
    ws_send,
    ws_recv,
    gn_send,
    gn_recv,
    hop_send,
    hop_recv,
    pass_send,
    pass_recv,
    sib_send,
    sib_recv,
    rs_send,
    rs_recv,
    y_send,
    y_recv,
    ag_send,
    ag_recv,
    fw_send,
    fw_recv,
    gs_sem,
    gy_sem,
    gz_send,
    gz_recv,
):
    features = w.shape[-1]
    s = lax.axis_index("section")
    dp = lax.axis_index("dp")
    core = lax.rem(dp, CORES)
    z = lax.rem(dp // CORES, RING)
    yh = dp // (CORES * RING)
    stage = s // LAYERS
    m = lax.rem(s, LAYERS)
    mx, my = m // 2, lax.rem(m, 2)
    early = stage == 0
    late = stage == 1
    j = jnp.where(early, m, 2 * (1 - mx) + my)
    busy = j < samples

    def dp_at(y_, z_, c_):
        return {"dp": (y_ * RING + z_) * CORES + c_}

    def relative(k):
        x_ = lax.rem(mx + k // 2, 2)
        y_ = lax.rem(my + k % 2, 2)
        return 2 * x_ + y_

    y_cross = lax.rem(yh + core, 2)

    def member_at(layer):
        y_ = jnp.where(lax.rem(layer, 2) == my, yh, y_cross)
        return {"section": LAYERS * stage + layer, "dp": (y_ * RING + z) * CORES + core}

    hop_to = {"section": 2 * (3 - s // 2) + lax.rem(s, 2)}
    sibling = dp_at(yh, z, 1 - core)
    across = dp_at(1 - yh, z, core)
    z_next = lax.rem(z + 1, RING)
    z_prev = lax.rem(z + RING - 1, RING)

    def remote(src, dst, send, recv, where):
        return pltpu.make_async_remote_copy(
            src_ref=src, dst_ref=dst, send_sem=send, recv_sem=recv, device_id=where, device_id_type=MESH
        )

    barrier = pltpu.get_barrier_semaphore()

    def greet(where):
        pl.semaphore_signal(barrier, inc=1, device_id=where, device_id_type=MESH)

    greet(sibling)
    for k in (1, 2, 3):
        greet(member_at(relative(k)))
    greet(hop_to)
    met = 5
    if SUM:
        greet(across)
        for d in range(1, RING):
            greet(dp_at(yh, lax.rem(z + d, RING), core))
        met += RING

    w_hbm = (wm_hbm, wu_hbm, wd_hbm)
    loads = [
        pltpu.make_async_copy(a, b, in_sem.at[i])
        for i, (a, b) in enumerate(
            [
                (g2m_c_hbm, g2m_c),
                (m2m_c_hbm, m2m_c),
                (m2g_c_hbm, m2g_c),
                (g2m_hbm, g2m),
                (m2m_hbm, m2m),
                (gain_hbm, gain_v),
                (m2g_hbm, m2g),
            ]
            + [(w_hbm[i].at[0], w.at[i, m]) for i in range(3)]
        )
    ]
    sample = jnp.minimum(j, samples - 1)
    lat_load = pltpu.make_async_copy(lat_hbm.at[sample], lat, io_sem.at[0])
    tgt_load = pltpu.make_async_copy(tgt_hbm.at[sample], tgt, io_sem.at[1])
    for load in loads:
        load.start()
    lat_load.start()
    tgt_load.start()

    def half_of(i, layer, c):
        rows = features // 2
        return w.at[i, layer, pl.ds(pl.multiple_of(c * rows, 16), rows)]

    def give(k, i):
        if k == 3:
            layer, where = relative(2), member_at(relative(1))
        else:
            layer, where = m, member_at(relative(k))
        rows = features // 2
        here = half_of(i, layer, core)
        src = here if k == 3 else w_hbm[i].at[0, pl.ds(pl.multiple_of(core * rows, 16), rows)]
        return remote(src, here, wt_send.at[k - 1, i], wt_recv.at[k - 1, i], where)

    def got(k, i):
        here = half_of(i, relative(k), core)
        return remote(here, here, wt_send.at[k - 1, i], wt_recv.at[k - 1, i], sibling)

    def share(k, i):
        here = half_of(i, relative(k), core)
        return remote(here, here, ws_send.at[k - 1, i], ws_recv.at[k - 1, i], sibling)

    def shared(k, i):
        here = half_of(i, relative(k), 1 - core)
        return remote(here, here, ws_send.at[k - 1, i], ws_recv.at[k - 1, i], sibling)

    def give_gain(k):
        return remote(gains.at[m], gains.at[m], gn_send.at[k - 1], gn_recv.at[k - 1], member_at(relative(k)))

    def got_gain(k):
        here = gains.at[relative(k)]
        return remote(here, here, gn_send.at[k - 1], gn_recv.at[k - 1], sibling)

    pl.semaphore_wait(barrier, met)
    for i in range(3):
        for k in (1, 2):
            give(k, i).start()
    for load in loads:
        load.wait()
    gains[m] = jnp.broadcast_to(gain_v[...], (8, features))
    for k in (1, 2, 3):
        give_gain(k).start()

    def kept_if(col, b, tile):
        return jnp.where(jnp.full(tile.shape, col, jnp.int32) == b, tile, jnp.zeros_like(tile))

    for k in range(2):
        for r in range(2):
            tile = m2m[2 * r + k]
            for b in range(2):
                kept = kept_if(m2m_c[2 * r + k], b, tile)
                mix[r * BLOCK : (r + 1) * BLOCK, (2 * k + b) * BLOCK : (2 * k + b + 1) * BLOCK] = kept
                mix_t[b * BLOCK : (b + 1) * BLOCK, (2 * k + r) * BLOCK : (2 * k + r + 1) * BLOCK] = kept.T

    lat_load.wait()
    tgt_load.wait()

    @pl.when(early)
    def _():
        for t in range(4):
            for b in range(4):
                k, r = t % 2, t // 2
                kept = kept_if(g2m_c[t], b, g2m[t])
                enc[r * BLOCK : (r + 1) * BLOCK, (4 * k + b) * BLOCK : (4 * k + b + 1) * BLOCK] = kept

    @pl.when(late)
    def _():
        for t in range(8):
            tile_t = m2g[t].T
            for b in range(2):
                k, r = t % 2, t // 2
                kept = kept_if(m2g_c[t], b, m2g[t])
                pred[r * BLOCK : (r + 1) * BLOCK, (2 * k + b) * BLOCK : (2 * k + b + 1) * BLOCK] = kept
                kept = kept_if(m2g_c[t], b, tile_t)
                seed_t[b * BLOCK : (b + 1) * BLOCK, (4 * k + r) * BLOCK : (4 * k + r + 1) * BLOCK] = kept

    span = NODES // CHUNKS

    def rows_of(c):
        return pl.ds(c * span, span)

    def hop_f(c):
        return remote(h.at[LAYERS, rows_of(c)], h.at[0, rows_of(c)], hop_send.at[0, c], hop_recv.at[0, c], hop_to)

    def hop_b(c):
        return remote(up.at[0, rows_of(c)], up.at[LAYERS, rows_of(c)], hop_send.at[1, c], hop_recv.at[1, c], hop_to)

    kinds = ((unit_s, 0), (act_s, 0), (up, 1), (gb_s, 0), (gp_s, 0))

    def hand_in(layer, i):
        ref, shift = kinds[i]
        return remote(
            ref.at[layer + shift], ref.at[LAYERS + shift + j], pass_send.at[layer, i], pass_recv.at[j, i], member_at(layer)
        )

    def handed_in(from_j, i):
        ref, shift = kinds[i]
        here = ref.at[LAYERS + shift + from_j]
        return remote(here, here, pass_send.at[0, i], pass_recv.at[from_j, i], sibling)

    def forward(l):
        @pl.when(early & (l == 0))
        def _():
            grid_rows = lat.shape[0]
            h[0] = (dot(enc[:, :grid_rows], lat[...]) + dot(enc[:, grid_rows:], lat[...])).astype(BF16)

        gain = gains[l, 0:1, :]
        for c in range(CHUNKS):
            rows = rows_of(c)

            @pl.when(late & (l == 0))
            def _():
                hop_f(c).wait_recv()

            x = h[l, rows, :].astype(F32)
            center = x - jnp.mean(x, axis=-1, keepdims=True)
            inverse = lax.rsqrt(jnp.mean(center * center, axis=-1, keepdims=True) + EPSILON)
            normed = center * inverse
            unit = (normed * gain).astype(BF16)
            normed_s[l, rows, :] = normed
            inv_s[l, rows, :] = jnp.broadcast_to(inverse, (span, 128))
            unit_s[l, rows, :] = unit
            msg_s[rows, :] = dot(unit, w[0, l]).astype(BF16)
            up_s[rows, :] = dot(unit, w[1, l])
        for c in range(CHUNKS):
            rows = rows_of(c)
            before = up_s[rows, :] + dot(mix[rows, :NODES], msg_s[...]) + dot(mix[rows, NODES:], msg_s[...])
            sigma = 1.0 / (1.0 + jnp.exp(-before))
            active = (before * sigma).astype(BF16)
            slope_s[l, rows, :] = sigma * (1.0 + before * (1.0 - sigma))
            act_s[l, rows, :] = active
            output = h[l, rows, :].astype(F32) + dot(active, w[2, l])
            h[l + 1, rows, :] = output.astype(BF16)

            @pl.when(early & (l == LAYERS - 1))
            def _():
                hop_f(c).start()

        @pl.when(l != m)
        def _():
            hand_in(l, 0).start()
            hand_in(l, 1).start()

        @pl.when(late & (l == LAYERS - 1))
        def _():
            upstream = jnp.zeros((NODES, features), F32)
            for r in range(4):
                here = pl.ds(r * BLOCK, BLOCK)
                predicted = dot(pred[here, :NODES], h[LAYERS]) + dot(pred[here, NODES:], h[LAYERS])
                target = tgt[r * BLOCK : (r + 1) * BLOCK, :].astype(F32)
                residual = ((predicted - target) * loss_scale).astype(BF16)
                for k in range(2):
                    part = seed_t[:, (4 * k + r) * BLOCK : (4 * k + r + 1) * BLOCK]
                    upstream = upstream + dot(part, residual)
            up[LAYERS] = upstream.astype(BF16)

    def backward(l):
        gain = gains[l, 0:1, :]
        for c in range(CHUNKS):
            rows = rows_of(c)

            @pl.when(early & (l == LAYERS - 1))
            def _():
                hop_b(c).wait_recv()

            grad_active = dot_nt(up[l + 1, rows, :], w[2, l])
            gb_s[l, rows, :] = (grad_active * slope_s[l, rows, :]).astype(BF16)

        @pl.when(l != m)
        def _():
            hand_in(l, 2).start()
            hand_in(l, 3).start()

        gm_s[...] = (dot(mix_t[:, :NODES], gb_s[l]) + dot(mix_t[:, NODES:], gb_s[l])).astype(BF16)
        for c in range(CHUNKS):
            rows = rows_of(c)
            grad_unit = dot_nt(gb_s[l, rows, :], w[1, l]) + dot_nt(gm_s[rows, :], w[0, l])
            normed = normed_s[l, rows, :]
            part = jnp.sum((grad_unit * normed).reshape(span // 8, 8, features), axis=0)
            gp_s[l] = part if c == 0 else gp_s[l] + part

            @pl.when(late | (l > 0))
            def _():
                grad_normed = grad_unit * gain
                inverse = inv_s[l, rows, :][:, :1]
                grad_inputs = up[l + 1, rows, :].astype(F32) + inverse * (
                    grad_normed
                    - jnp.mean(grad_normed, axis=-1, keepdims=True)
                    - normed * jnp.mean(grad_normed * normed, axis=-1, keepdims=True)
                )
                up[l, rows, :] = grad_inputs.astype(BF16)

            @pl.when(late & (l == 0))
            def _():
                hop_b(c).start()

        @pl.when(l != m)
        def _():
            hand_in(l, 4).start()

    def round_of(l):
        last = 0
        for i in range(LAYERS):
            far = 2 * lax.rem(i // 2 + mx, 2) + lax.rem(i % 2 + my, 2)
            last = jnp.maximum(last, jnp.where(l >= i, far, 0))
        return jnp.where(early, last, LAYERS - 1)

    @pl.loop(0, LAYERS * LAYERS)
    def _(t):
        e, l = t // LAYERS, lax.rem(t, LAYERS)

        @pl.when((e == 1) & (l == 0))
        def _():
            for k in (1, 2, 3):
                got_gain(k).wait_recv()
            for k, i in ((1, 0), (1, 1), (2, 0), (1, 2)):
                got(k, i).wait_recv()
                if k == 2:
                    give(3, i).start()
                share(k, i).start()
            for i in range(3):
                shared(1, i).wait_recv()

        @pl.when((e == 2) & (l == 0))
        def _():
            for i in (1, 2):
                got(2, i).wait_recv()
                give(3, i).start()
                share(2, i).start()
            for i in range(3):
                shared(2, i).wait_recv()

        @pl.when((e == 3) & (l == 0))
        def _():
            for i in range(3):
                got(3, i).wait_recv()
                share(3, i).start()
            for i in range(3):
                shared(3, i).wait_recv()

        @pl.when(busy & (round_of(l) == e))
        def _():
            forward(l)

    def turn():
        @pl.loop(0, samples)
        def _(i):
            mine = i == j

            @pl.when(jnp.logical_not(mine))
            def _():
                handed_in(i, 0).wait_recv()
                handed_in(i, 1).wait_recv()

            at = jnp.where(mine, m, LAYERS + i)
            unit_t[i] = unit_s[at].T
            act_t[i] = act_s[at].T

    @pl.when(early)
    def _():
        turn()

    @pl.loop(0, LAYERS)
    def _(t):
        @pl.when(busy)
        def _():
            backward(LAYERS - 1 - t)

    @pl.when(late)
    def _():
        turn()

    @pl.loop(0, samples)
    def _(t):
        i = lax.rem(j + t, samples)
        mine = i == j

        @pl.when(jnp.logical_not(mine))
        def _():
            for kind in (2, 3, 4):
                handed_in(i, kind).wait_recv()

        at = jnp.where(mine, m, LAYERS + i)
        grad_before = gb_s[at]
        gm_s[...] = (dot(mix_t[:, :NODES], grad_before) + dot(mix_t[:, NODES:], grad_before)).astype(BF16)
        parts = (
            (unit_t, lambda: gm_s[...]),
            (unit_t, lambda: gb_s[at]),
            (act_t, lambda: up[at + 1]),
        )
        for n, (left, right) in enumerate(parts):
            rows = pl.ds(n * features, features)
            product = dot(left[i], right())

            @pl.when(t == 0)
            def _():
                acc[rows, :] = product

            @pl.when(t > 0)
            def _():
                acc[rows, :] += product

        @pl.when(t == 0)
        def _():
            gacc[...] = gp_s[at]

        @pl.when(t > 0)
        def _():
            gacc[...] += gp_s[at]

    def finish_sends():
        for k in (1, 2, 3):
            give_gain(k).wait_send()
            for i in range(3):
                give(k, i).wait_send()
                share(k, i).wait_send()

        @pl.when(busy)
        def _():
            for c in range(CHUNKS):

                @pl.when(early)
                def _():
                    hop_f(c).wait_send()

                @pl.when(late)
                def _():
                    hop_b(c).wait_send()

            @pl.loop(0, LAYERS)
            def _(l):
                @pl.when(l != m)
                def _():
                    for i in range(5):
                        hand_in(l, i).wait_send()

    if not SUM:
        finish_sends()
        return

    half = acc.shape[0] // CORES
    chunk = half // RING
    piece = chunk // 2

    def toward(d):
        return dp_at(yh, z_next if d == 0 else z_prev, core)

    def owner_at(d, shift):
        return lax.rem(z + (shift if d == 0 else RING - shift), RING)

    def rows_at(c, u, owner):
        return pl.ds(pl.multiple_of(c * half + owner * chunk + u * piece, 16), piece)

    def steps(u, d):
        return FAR if u == d else FAR - 1

    flows = [(u, d) for long in (True, False) for u in range(2) for d in range(2) if (u == d) == long]

    quarter = half // 4

    def quarter_rows(c, i):
        return pl.ds(pl.multiple_of(c * half + i * quarter, 16), quarter)

    def to_sib(i):
        return remote(acc.at[quarter_rows(1 - core, i)], sib_buf.at[i], sib_send.at[i], sib_recv.at[i], sibling)

    g_to_sib = remote(gacc, g_sib, gs_sem.at[0], gs_sem.at[1], sibling)
    for i in range(4):
        to_sib(i).start()
    g_to_sib.start()

    def rs(u, d, t):
        rows = rows_at(core, u, owner_at(d, steps(u, d) - t))
        return remote(acc.at[rows], ring_buf.at[u, d, t], rs_send.at[u, d, t], rs_recv.at[u, d, t], toward(d))

    def take(u, d, t):
        rs(u, d, t).wait_recv()
        acc[rows_at(core, u, owner_at(d, steps(u, d) - t - 1)), :] += ring_buf[u, d, t]

    for i in range(4):
        to_sib(i).wait()
        acc[quarter_rows(core, i), :] += sib_buf[i]
    for u, d in flows:
        rs(u, d, 0).start()
    g_to_sib.wait()
    gacc[...] += g_sib[...]
    g_to_y = remote(gacc, g_y, gy_sem.at[0], gy_sem.at[1], across)
    g_to_y.start()
    for t in range(1, FAR):
        for u, d in flows:
            if t < steps(u, d):
                take(u, d, t - 1)
                rs(u, d, t).start()

    def y_copy(u):
        return remote(acc.at[rows_at(core, u, z)], y_buf.at[u], y_send.at[u], y_recv.at[u], across)

    for u in range(2):
        for d in (1 - u, u):
            take(u, d, steps(u, d) - 1)
        y_copy(u).start()

    g_to_y.wait()
    g_z[z] = gacc[...] + g_y[...]

    def g_spread(d):
        return remote(g_z.at[z], g_z.at[z], gz_send.at[d - 1], gz_recv.at[d - 1], dp_at(yh, lax.rem(z + d, RING), core))

    def g_arrive(d):
        at = lax.rem(z - d + RING, RING)
        return remote(g_z.at[at], g_z.at[at], gz_send.at[d - 1], gz_recv.at[d - 1], dp_at(yh, at, core))

    for d in range(1, RING):
        g_spread(d).start()

    def spread(u, d, t):
        rows = rows_at(core, u, owner_at(1 - d, t))
        return remote(out.at[rows], out.at[rows], ag_send.at[u, d, t], ag_recv.at[u, d, t], toward(d))

    def arrive(u, d, t):
        rows = rows_at(core, u, owner_at(1 - d, t + 1))
        return remote(out.at[rows], out.at[rows], ag_send.at[u, d, t], ag_recv.at[u, d, t], toward(d))

    def hand_over(u, owner):
        rows = rows_at(core, u, owner)
        return remote(out.at[rows], out.at[rows], fw_send.at[u, owner], fw_recv.at[u, owner], sibling)

    def handed_over(u, owner):
        rows = rows_at(1 - core, u, owner)
        return remote(out.at[rows], out.at[rows], fw_send.at[u, owner], fw_recv.at[u, owner], sibling)

    for u in range(2):
        y_copy(u).wait()
        rows = rows_at(core, u, z)
        out[rows, :] = acc[rows, :] + y_buf[u]
        for d in (u, 1 - u):
            spread(u, d, 0).start()
        hand_over(u, z).start()

    for t in range(FAR):
        for u, d in flows:
            if t < steps(u, d):
                arrive(u, d, t).wait_recv()
                if t + 1 < steps(u, d):
                    spread(u, d, t + 1).start()
                hand_over(u, owner_at(1 - d, t + 1)).start()

    for d in range(1, RING):
        g_arrive(d).wait_recv()
    total = g_z[0]
    for i in range(1, RING):
        total = total + g_z[i]
    gain_out[...] = jnp.broadcast_to(jnp.sum(total, axis=0, keepdims=True), gain_out.shape)

    for u in range(2):
        for i in range(RING):
            handed_over(u, i).wait_recv()
            hand_over(u, i).wait_send()
    for u, d in flows:
        for t in range(steps(u, d)):
            rs(u, d, t).wait_send()
            spread(u, d, t).wait_send()
    for d in range(1, RING):
        g_spread(d).wait_send()
    finish_sends()


def on_device(sections, replicas, *args):
    samples, grid_rows, features = args[0].shape
    loss_scale = 1.0 / math.sqrt(samples * replicas * grid_rows)
    total_rows = 3 * features
    piece = total_rows // CORES // RING // 2
    dma = pltpu.SemaphoreType.DMA
    v = pltpu.VMEM
    tile = (BLOCK, BLOCK)
    vmem_spec = pl.BlockSpec(memory_space=pltpu.VMEM)
    out, gain_out = pl.pallas_call(
        functools.partial(step_kernel, samples, loss_scale),
        out_shape=(
            jax.ShapeDtypeStruct((total_rows, features), F32),
            jax.ShapeDtypeStruct((8, features), F32),
        ),
        in_specs=[pl.BlockSpec(memory_space=pltpu.HBM)] * 12,
        out_specs=(vmem_spec, vmem_spec),
        scratch_shapes=[
            v((grid_rows, features), BF16),
            v((grid_rows, features), BF16),
            v((4,) + tile, BF16),
            v((4,) + tile, BF16),
            v((8,) + tile, BF16),
            pltpu.SMEM((4,), jnp.int32),
            pltpu.SMEM((4,), jnp.int32),
            pltpu.SMEM((8,), jnp.int32),
            v((3, LAYERS, features, features), BF16),
            v((1, features), F32),
            v((LAYERS, 8, features), F32),
            v((NODES, 2 * NODES), BF16),
            v((NODES, 2 * NODES), BF16),
            v((NODES, 2 * grid_rows), BF16),
            v((grid_rows, 2 * NODES), BF16),
            v((NODES, 2 * grid_rows), BF16),
            v((LAYERS + 1, NODES, features), BF16),
            v((LAYERS + 1 + samples, NODES, features), BF16),
            v((LAYERS + samples, NODES, features), BF16),
            v((LAYERS + samples, NODES, features), BF16),
            v((LAYERS + samples, NODES, features), BF16),
            v((LAYERS + samples, 8, features), F32),
            v((LAYERS, NODES, features), F32),
            v((LAYERS, NODES, features), F32),
            v((LAYERS, NODES, 128), F32),
            v((NODES, features), BF16),
            v((NODES, features), F32),
            v((NODES, features), BF16),
            v((samples, features, NODES), BF16),
            v((samples, features, NODES), BF16),
            v((total_rows, features), F32),
            v((8, features), F32),
            v((4, total_rows // CORES // 4, features), F32),
            v((2, 2, FAR, piece, features), F32),
            v((2, piece, features), F32),
            v((8, features), F32),
            v((8, features), F32),
            v((RING, 8, features), F32),
            dma((10,)),
            dma((2,)),
            dma((3, 3)),
            dma((3, 3)),
            dma((3, 3)),
            dma((3, 3)),
            dma((3,)),
            dma((3,)),
            dma((2, CHUNKS)),
            dma((2, CHUNKS)),
            dma((LAYERS, 5)),
            dma((samples, 5)),
            dma((4,)),
            dma((4,)),
            dma((2, 2, FAR)),
            dma((2, 2, FAR)),
            dma((2,)),
            dma((2,)),
            dma((2, 2, FAR)),
            dma((2, 2, FAR)),
            dma((2, RING)),
            dma((2, RING)),
            dma((2,)),
            dma((2,)),
            dma((STEPS,)),
            dma((STEPS,)),
        ],
        compiler_params=pltpu.CompilerParams(
            collective_id=0, has_side_effects=True, vmem_limit_bytes=64 * 1024 * 1024 - 4096
        ),
        name="train_step",
    )(*args)
    return out.reshape(1, 3, features, features), gain_out[:1]


def solution(mesh):
    placed = (
        P("dp", None, None),
        P("dp", None, None),
        P(),
        P(),
        P(),
        P(),
        P(),
        P(),
        P("section", None, None),
        P("section", None, None),
        P("section", None, None),
        P("section", None),
    )
    return jax.shard_map(
        functools.partial(on_device, mesh.shape["section"], mesh.shape["dp"]),
        mesh=mesh,
        in_specs=placed,
        out_specs=(P("section", None, None, None), P("section", None)),
        check_vma=False,
    )
```

```python
import functools
import math

import jax
import jax.numpy as jnp
from jax import lax
from jax.experimental import pallas as pl
from jax.experimental.pallas import tpu as pltpu
from jax.sharding import PartitionSpec as P

BLOCK = 128
NODES = 256
EPSILON = 1e-05
MESH = pl.DeviceIdType.MESH
F32 = jnp.float32
BF16 = jnp.bfloat16
CHUNKS = 2
LAYERS = 4
CORES = 2
RING = 8
STEPS = RING - 1
FAR = RING // 2
SUM = True


def dot(a, b):
    return jnp.dot(a, b, preferred_element_type=F32)


def dot_nt(a, b):
    return lax.dot_general(a, b, (((1,), (1,)), ((), ())), preferred_element_type=F32)


def step_kernel(
    samples,
    loss_scale,
    lat_hbm,
    tgt_hbm,
    g2m_hbm,
    g2m_c_hbm,
    m2m_hbm,
    m2m_c_hbm,
    m2g_hbm,
    m2g_c_hbm,
    wm_hbm,
    wu_hbm,
    wd_hbm,
    gain_hbm,
    out,
    gain_out,
    lat,
    tgt,
    g2m,
    m2m,
    m2g,
    g2m_c,
    m2m_c,
    m2g_c,
    w,
    gain_v,
    gains,
    mix,
    mix_t,
    enc,
    pred,
    seed_t,
    h,
    up,
    unit_s,
    act_s,
    gb_s,
    slope_s,
    normed_s,
    inv_s,
    msg_s,
    up_s,
    gm_s,
    acc,
    gacc,
    sib_buf,
    ring_buf,
    y_buf,
    g_sib,
    g_y,
    g_z,
    in_sem,
    io_sem,
    wt_send,
    wt_recv,
    ws_send,
    ws_recv,
    gn_send,
    gn_recv,
    hop_send,
    hop_recv,
    pass_send,
    pass_recv,
    sib_send,
    sib_recv,
    rs_send,
    rs_recv,
    y_send,
    y_recv,
    ag_send,
    ag_recv,
    fw_send,
    fw_recv,
    gs_sem,
    gy_sem,
    gz_send,
    gz_recv,
):
    features = w.shape[-1]
    s = lax.axis_index("section")
    dp = lax.axis_index("dp")
    core = lax.rem(dp, CORES)
    z = lax.rem(dp // CORES, RING)
    yh = dp // (CORES * RING)
    stage = s // LAYERS
    m = lax.rem(s, LAYERS)
    mx, my = m // 2, lax.rem(m, 2)
    early = stage == 0
    late = stage == 1
    j = jnp.where(early, m, 2 * (1 - mx) + my)
    busy = j < samples

    def dp_at(y_, z_, c_):
        return {"dp": (y_ * RING + z_) * CORES + c_}

    def relative(k):
        x_ = lax.rem(mx + k // 2, 2)
        y_ = lax.rem(my + k % 2, 2)
        return 2 * x_ + y_

    y_cross = lax.rem(yh + core, 2)

    def member_at(layer):
        y_ = jnp.where(lax.rem(layer, 2) == my, yh, y_cross)
        return {"section": LAYERS * stage + layer, "dp": (y_ * RING + z) * CORES + core}

    hop_to = {"section": 2 * (3 - s // 2) + lax.rem(s, 2)}
    sibling = dp_at(yh, z, 1 - core)
    across = dp_at(1 - yh, z, core)
    z_next = lax.rem(z + 1, RING)
    z_prev = lax.rem(z + RING - 1, RING)

    def remote(src, dst, send, recv, where):
        return pltpu.make_async_remote_copy(
            src_ref=src, dst_ref=dst, send_sem=send, recv_sem=recv, device_id=where, device_id_type=MESH
        )

    barrier = pltpu.get_barrier_semaphore()

    def greet(where):
        pl.semaphore_signal(barrier, inc=1, device_id=where, device_id_type=MESH)

    greet(sibling)
    for k in (1, 2, 3):
        greet(member_at(relative(k)))
    greet(hop_to)
    met = 5
    if SUM:
        greet(across)
        for d in range(1, RING):
            greet(dp_at(yh, lax.rem(z + d, RING), core))
        met += RING

    w_hbm = (wm_hbm, wu_hbm, wd_hbm)
    loads = [
        pltpu.make_async_copy(a, b, in_sem.at[i])
        for i, (a, b) in enumerate(
            [
                (g2m_c_hbm, g2m_c),
                (m2m_c_hbm, m2m_c),
                (m2g_c_hbm, m2g_c),
                (g2m_hbm, g2m),
                (m2m_hbm, m2m),
                (gain_hbm, gain_v),
                (m2g_hbm, m2g),
            ]
            + [(w_hbm[i].at[0], w.at[i, m]) for i in range(3)]
        )
    ]
    sample = jnp.minimum(j, samples - 1)
    lat_load = pltpu.make_async_copy(lat_hbm.at[sample], lat, io_sem.at[0])
    tgt_load = pltpu.make_async_copy(tgt_hbm.at[sample], tgt, io_sem.at[1])
    for load in loads:
        load.start()
    lat_load.start()
    tgt_load.start()

    def half_of(i, layer, c):
        rows = features // 2
        return w.at[i, layer, pl.ds(pl.multiple_of(c * rows, 16), rows)]

    def give(k, i):
        if k == 3:
            layer, where = relative(2), member_at(relative(1))
        else:
            layer, where = m, member_at(relative(k))
        rows = features // 2
        here = half_of(i, layer, core)
        src = here if k == 3 else w_hbm[i].at[0, pl.ds(pl.multiple_of(core * rows, 16), rows)]
        return remote(src, here, wt_send.at[k - 1, i], wt_recv.at[k - 1, i], where)

    def got(k, i):
        here = half_of(i, relative(k), core)
        return remote(here, here, wt_send.at[k - 1, i], wt_recv.at[k - 1, i], sibling)

    def share(k, i):
        here = half_of(i, relative(k), core)
        return remote(here, here, ws_send.at[k - 1, i], ws_recv.at[k - 1, i], sibling)

    def shared(k, i):
        here = half_of(i, relative(k), 1 - core)
        return remote(here, here, ws_send.at[k - 1, i], ws_recv.at[k - 1, i], sibling)

    def give_gain(k):
        return remote(gains.at[m], gains.at[m], gn_send.at[k - 1], gn_recv.at[k - 1], member_at(relative(k)))

    def got_gain(k):
        here = gains.at[relative(k)]
        return remote(here, here, gn_send.at[k - 1], gn_recv.at[k - 1], sibling)

    pl.semaphore_wait(barrier, met)
    give(1, 0).start()
    give(2, 0).start()
    for load in loads:
        load.wait()
    gains[m] = jnp.broadcast_to(gain_v[...], (8, features))
    for k in (1, 2, 3):
        give_gain(k).start()

    def kept_if(col, b, tile):
        return jnp.where(jnp.full(tile.shape, col, jnp.int32) == b, tile, jnp.zeros_like(tile))

    for k in range(2):
        for r in range(2):
            tile = m2m[2 * r + k]
            for b in range(2):
                kept = kept_if(m2m_c[2 * r + k], b, tile)
                mix[r * BLOCK : (r + 1) * BLOCK, (2 * k + b) * BLOCK : (2 * k + b + 1) * BLOCK] = kept
                mix_t[b * BLOCK : (b + 1) * BLOCK, (2 * k + r) * BLOCK : (2 * k + r + 1) * BLOCK] = kept.T

    lat_load.wait()
    tgt_load.wait()

    @pl.when(early)
    def _():
        for t in range(4):
            for b in range(4):
                k, r = t % 2, t // 2
                kept = kept_if(g2m_c[t], b, g2m[t])
                enc[r * BLOCK : (r + 1) * BLOCK, (4 * k + b) * BLOCK : (4 * k + b + 1) * BLOCK] = kept

    @pl.when(late)
    def _():
        for t in range(8):
            tile_t = m2g[t].T
            for b in range(2):
                k, r = t % 2, t // 2
                kept = kept_if(m2g_c[t], b, m2g[t])
                pred[r * BLOCK : (r + 1) * BLOCK, (2 * k + b) * BLOCK : (2 * k + b + 1) * BLOCK] = kept
                kept = kept_if(m2g_c[t], b, tile_t)
                seed_t[b * BLOCK : (b + 1) * BLOCK, (4 * k + r) * BLOCK : (4 * k + r + 1) * BLOCK] = kept

    give(1, 0).wait_send()
    give(1, 1).start()
    give(1, 2).start()
    give(2, 0).wait_send()
    give(2, 1).start()

    span = NODES // CHUNKS

    def rows_of(c):
        return pl.ds(c * span, span)

    def hop_f(c):
        return remote(h.at[LAYERS, rows_of(c)], h.at[0, rows_of(c)], hop_send.at[0, c], hop_recv.at[0, c], hop_to)

    def hop_b(c):
        return remote(up.at[0, rows_of(c)], up.at[LAYERS, rows_of(c)], hop_send.at[1, c], hop_recv.at[1, c], hop_to)

    def hand_in(layer, kind):
        ref, at = ((h, layer), (up, layer + 1))[kind]
        return remote(
            ref.at[at], ref.at[LAYERS + 1 + j], pass_send.at[layer, kind], pass_recv.at[j, kind], member_at(layer)
        )

    def handed_in(i, kind):
        here = (h, up)[kind].at[LAYERS + 1 + i]
        return remote(here, here, pass_send.at[0, kind], pass_recv.at[i, kind], sibling)

    def forward(q, layer, own):
        at = q if own else q + 1
        gain = gains[layer, 0:1, :]
        for c in range(CHUNKS):
            rows = rows_of(c)
            if own:

                @pl.when(late & (q == 0))
                def _():
                    hop_f(c).wait_recv()

            x = h[at, rows, :].astype(F32)
            center = x - jnp.mean(x, axis=-1, keepdims=True)
            inverse = lax.rsqrt(jnp.mean(center * center, axis=-1, keepdims=True) + EPSILON)
            normed = center * inverse
            unit = (normed * gain).astype(BF16)
            normed_s[q, rows, :] = normed
            if own:
                inv_s[q, rows, :] = jnp.broadcast_to(inverse, (span, 128))
            unit_s[q, rows, :] = unit
            msg_s[rows, :] = dot(unit, w[0, layer]).astype(BF16)
            up_s[rows, :] = dot(unit, w[1, layer])
        for c in range(CHUNKS):
            rows = rows_of(c)
            before = up_s[rows, :] + dot(mix[rows, :NODES], msg_s[...]) + dot(mix[rows, NODES:], msg_s[...])
            sigma = 1.0 / (1.0 + jnp.exp(-before))
            active = (before * sigma).astype(BF16)
            slope_s[q, rows, :] = sigma * (1.0 + before * (1.0 - sigma))
            act_s[q, rows, :] = active
            if own:
                output = h[q, rows, :].astype(F32) + dot(active, w[2, layer])
                h[q + 1, rows, :] = output.astype(BF16)

                @pl.when(early & (q == LAYERS - 1))
                def _():
                    hop_f(c).start()

    def encode():
        grid_rows = lat.shape[0]
        h[0] = (dot(enc[:, :grid_rows], lat[...]) + dot(enc[:, grid_rows:], lat[...])).astype(BF16)

    def decode():
        upstream = jnp.zeros((NODES, features), F32)
        for r in range(4):
            here = pl.ds(r * BLOCK, BLOCK)
            predicted = dot(pred[here, :NODES], h[LAYERS]) + dot(pred[here, NODES:], h[LAYERS])
            target = tgt[r * BLOCK : (r + 1) * BLOCK, :].astype(F32)
            residual = ((predicted - target) * loss_scale).astype(BF16)
            for k in range(2):
                part = seed_t[:, (4 * k + r) * BLOCK : (4 * k + r + 1) * BLOCK]
                upstream = upstream + dot(part, residual)
        up[LAYERS] = upstream.astype(BF16)

    def backward(q, layer, own):
        gain = gains[layer, 0:1, :]
        gb_s[q] = (dot_nt(up[q + 1], w[2, layer]) * slope_s[q]).astype(BF16)
        gm_s[q] = (dot(mix_t[:, :NODES], gb_s[q]) + dot(mix_t[:, NODES:], gb_s[q])).astype(BF16)
        up_s[...] = dot_nt(gb_s[q], w[1, layer]) + dot_nt(gm_s[q], w[0, layer])

        @pl.when(layer == m)
        def _():
            gacc[...] += jnp.sum((up_s[...] * normed_s[q]).reshape(NODES // 8, 8, features), axis=0)

        if own:

            @pl.when(late | (q > 0))
            def _():
                for c in range(CHUNKS):
                    rows = rows_of(c)
                    grad_normed = up_s[rows, :] * gain
                    normed = normed_s[q, rows, :]
                    inverse = inv_s[q, rows, :][:, :1]
                    grad_inputs = up[q + 1, rows, :].astype(F32) + inverse * (
                        grad_normed
                        - jnp.mean(grad_normed, axis=-1, keepdims=True)
                        - normed * jnp.mean(grad_normed * normed, axis=-1, keepdims=True)
                    )
                    up[q, rows, :] = grad_inputs.astype(BF16)

                    @pl.when(late & (q == 0))
                    def _():
                        hop_b(c).start()

    def add_weight_grads(q):
        for n, (left, right) in enumerate(((unit_s, gm_s), (unit_s, gb_s), (act_s, None))):
            rows = pl.ds(n * features, features)
            acc[rows, :] += dot(left[q].T, up[q + 1] if right is None else right[q])

    def round_of(l):
        last = 0
        for i in range(LAYERS):
            far = 2 * lax.rem(i // 2 + mx, 2) + lax.rem(i % 2 + my, 2)
            last = jnp.maximum(last, jnp.where(l >= i, far, 0))
        return jnp.where(early, last, LAYERS - 1)

    @pl.loop(0, LAYERS * LAYERS)
    def _(t):
        e, l = t // LAYERS, lax.rem(t, LAYERS)

        @pl.when((e == 1) & (l == 0))
        def _():
            for k in (1, 2, 3):
                got_gain(k).wait_recv()
            for k, i in ((1, 0), (2, 0), (1, 1), (1, 2)):
                got(k, i).wait_recv()
                if k == 2:
                    give(3, i).start()
                share(k, i).start()
            give(2, 1).wait_send()
            give(2, 2).start()
            for i in range(3):
                shared(1, i).wait_recv()

        @pl.when((e == 2) & (l == 0))
        def _():
            for i in (1, 2):
                got(2, i).wait_recv()
                give(3, i).start()
                share(2, i).start()
            for i in range(3):
                shared(2, i).wait_recv()

        @pl.when((e == 3) & (l == 0))
        def _():
            for i in range(3):
                got(3, i).wait_recv()
                share(3, i).start()
            for i in range(3):
                shared(3, i).wait_recv()

        @pl.when(busy & (round_of(l) == e))
        def _():
            @pl.when(early & (l == 0))
            def _():
                encode()

            @pl.when(late & (l != m))
            def _():
                @pl.when(l > 0)
                def _():
                    hand_in(l, 0).start()

            forward(l, l, True)

    @pl.when(busy & late)
    def _():
        decode()

    @pl.when(busy)
    def _():
        @pl.loop(0, LAYERS)
        def _(l):
            @pl.when((l != m) & (early | (l == 0)))
            def _():
                hand_in(l, 0).start()

        @pl.when(m != LAYERS - 1)
        def _():
            @pl.when(late)
            def _():
                hand_in(LAYERS - 1, 1).start()

    acc[...] = jnp.zeros_like(acc)
    gacc[...] = jnp.zeros_like(gacc)

    @pl.loop(0, LAYERS + samples)
    def _(t):
        other = jnp.where(early, t, t - LAYERS)
        l = LAYERS - 1 - jnp.where(early, t - samples, t)

        @pl.when((other >= 0) & (other < samples) & (other != j))
        def _():
            handed_in(other, 0).wait_recv()
            forward(LAYERS + other, m, False)

        @pl.when(busy & (l >= 0) & (l < LAYERS))
        def _():
            @pl.when(early & (l == LAYERS - 1))
            def _():
                for c in range(CHUNKS):
                    hop_b(c).wait_recv()

                @pl.when(m != LAYERS - 1)
                def _():
                    hand_in(LAYERS - 1, 1).start()

            @pl.when(late | (l > 0) | (m == 0))
            def _():
                backward(l, l, True)

            @pl.when((l > 0) & (l - 1 != m))
            def _():
                hand_in(l - 1, 1).start()

    @pl.loop(0, samples)
    def _(t):
        i = lax.rem(j + t, samples)
        mine = i == j

        @pl.when(jnp.logical_not(mine))
        def _():
            handed_in(i, 1).wait_recv()
            backward(LAYERS + i, m, False)

        add_weight_grads(jnp.where(mine, m, LAYERS + i))

    def finish_sends():
        for k in (1, 2, 3):
            give_gain(k).wait_send()
            for i in range(3):
                if (k, i) not in ((1, 0), (2, 0), (2, 1)):
                    give(k, i).wait_send()
                share(k, i).wait_send()

        @pl.when(busy)
        def _():
            for c in range(CHUNKS):

                @pl.when(early)
                def _():
                    hop_f(c).wait_send()

                @pl.when(late)
                def _():
                    hop_b(c).wait_send()

            @pl.loop(0, LAYERS)
            def _(l):
                @pl.when(l != m)
                def _():
                    for kind in range(2):
                        hand_in(l, kind).wait_send()

    if not SUM:
        finish_sends()
        return

    half = acc.shape[0] // CORES
    chunk = half // RING
    piece = chunk // 2

    def toward(d):
        return dp_at(yh, z_next if d == 0 else z_prev, core)

    def owner_at(d, shift):
        return lax.rem(z + (shift if d == 0 else RING - shift), RING)

    def rows_at(c, u, owner):
        return pl.ds(pl.multiple_of(c * half + owner * chunk + u * piece, 16), piece)

    def steps(u, d):
        return FAR if u == d else FAR - 1

    flows = [(u, d) for long in (True, False) for u in range(2) for d in range(2) if (u == d) == long]

    quarter = half // 4

    def quarter_rows(c, i):
        return pl.ds(pl.multiple_of(c * half + i * quarter, 16), quarter)

    def to_sib(i):
        return remote(acc.at[quarter_rows(1 - core, i)], sib_buf.at[i], sib_send.at[i], sib_recv.at[i], sibling)

    g_to_sib = remote(gacc, g_sib, gs_sem.at[0], gs_sem.at[1], sibling)
    for i in range(4):
        to_sib(i).start()
    g_to_sib.start()

    def rs(u, d, t):
        rows = rows_at(core, u, owner_at(d, steps(u, d) - t))
        return remote(acc.at[rows], ring_buf.at[u, d, t], rs_send.at[u, d, t], rs_recv.at[u, d, t], toward(d))

    def take(u, d, t):
        rs(u, d, t).wait_recv()
        acc[rows_at(core, u, owner_at(d, steps(u, d) - t - 1)), :] += ring_buf[u, d, t]

    for i in range(4):
        to_sib(i).wait()
        acc[quarter_rows(core, i), :] += sib_buf[i]
    for u, d in flows:
        rs(u, d, 0).start()
    g_to_sib.wait()
    gacc[...] += g_sib[...]
    g_to_y = remote(gacc, g_y, gy_sem.at[0], gy_sem.at[1], across)
    g_to_y.start()
    for t in range(1, FAR):
        for u, d in flows:
            if t < steps(u, d):
                take(u, d, t - 1)
                rs(u, d, t).start()

    def y_copy(u):
        return remote(acc.at[rows_at(core, u, z)], y_buf.at[u], y_send.at[u], y_recv.at[u], across)

    for u in range(2):
        for d in (1 - u, u):
            take(u, d, steps(u, d) - 1)
        y_copy(u).start()

    g_to_y.wait()
    g_z[z] = gacc[...] + g_y[...]

    def g_spread(d):
        return remote(g_z.at[z], g_z.at[z], gz_send.at[d - 1], gz_recv.at[d - 1], dp_at(yh, lax.rem(z + d, RING), core))

    def g_arrive(d):
        at = lax.rem(z - d + RING, RING)
        return remote(g_z.at[at], g_z.at[at], gz_send.at[d - 1], gz_recv.at[d - 1], dp_at(yh, at, core))

    for d in range(1, RING):
        g_spread(d).start()

    def spread(u, d, t):
        rows = rows_at(core, u, owner_at(1 - d, t))
        return remote(out.at[rows], out.at[rows], ag_send.at[u, d, t], ag_recv.at[u, d, t], toward(d))

    def arrive(u, d, t):
        rows = rows_at(core, u, owner_at(1 - d, t + 1))
        return remote(out.at[rows], out.at[rows], ag_send.at[u, d, t], ag_recv.at[u, d, t], toward(d))

    def hand_over(u, owner):
        rows = rows_at(core, u, owner)
        return remote(out.at[rows], out.at[rows], fw_send.at[u, owner], fw_recv.at[u, owner], sibling)

    def handed_over(u, owner):
        rows = rows_at(1 - core, u, owner)
        return remote(out.at[rows], out.at[rows], fw_send.at[u, owner], fw_recv.at[u, owner], sibling)

    for u in range(2):
        y_copy(u).wait()
        rows = rows_at(core, u, z)
        out[rows, :] = acc[rows, :] + y_buf[u]
        for d in (u, 1 - u):
            spread(u, d, 0).start()
        hand_over(u, z).start()

    for t in range(FAR):
        for u, d in flows:
            if t < steps(u, d):
                arrive(u, d, t).wait_recv()
                if t + 1 < steps(u, d):
                    spread(u, d, t + 1).start()
                hand_over(u, owner_at(1 - d, t + 1)).start()

    for d in range(1, RING):
        g_arrive(d).wait_recv()
    total = g_z[0]
    for i in range(1, RING):
        total = total + g_z[i]
    gain_out[...] = jnp.sum(total, axis=0, keepdims=True)

    for u in range(2):
        for i in range(RING):
            handed_over(u, i).wait_recv()
            hand_over(u, i).wait_send()
    for u, d in flows:
        for t in range(steps(u, d)):
            rs(u, d, t).wait_send()
            spread(u, d, t).wait_send()
    for d in range(1, RING):
        g_spread(d).wait_send()
    finish_sends()


def on_device(sections, replicas, *args):
    samples, grid_rows, features = args[0].shape
    loss_scale = 1.0 / math.sqrt(samples * replicas * grid_rows)
    total_rows = 3 * features
    piece = total_rows // CORES // RING // 2
    dma = pltpu.SemaphoreType.DMA
    v = pltpu.VMEM
    tile = (BLOCK, BLOCK)
    vmem_spec = pl.BlockSpec(memory_space=pltpu.VMEM)
    out, gain_out = pl.pallas_call(
        functools.partial(step_kernel, samples, loss_scale),
        out_shape=(
            jax.ShapeDtypeStruct((total_rows, features), F32),
            jax.ShapeDtypeStruct((1, features), F32),
        ),
        in_specs=[pl.BlockSpec(memory_space=pltpu.HBM)] * 12,
        out_specs=(vmem_spec, vmem_spec),
        scratch_shapes=[
            v((grid_rows, features), BF16),
            v((grid_rows, features), BF16),
            v((4,) + tile, BF16),
            v((4,) + tile, BF16),
            v((8,) + tile, BF16),
            pltpu.SMEM((4,), jnp.int32),
            pltpu.SMEM((4,), jnp.int32),
            pltpu.SMEM((8,), jnp.int32),
            v((3, LAYERS, features, features), BF16),
            v((1, features), F32),
            v((LAYERS, 8, features), F32),
            v((NODES, 2 * NODES), BF16),
            v((NODES, 2 * NODES), BF16),
            v((NODES, 2 * grid_rows), BF16),
            v((grid_rows, 2 * NODES), BF16),
            v((NODES, 2 * grid_rows), BF16),
            v((LAYERS + 1 + samples, NODES, features), BF16),
            v((LAYERS + 1 + samples, NODES, features), BF16),
            v((LAYERS + samples, NODES, features), BF16),
            v((LAYERS + samples, NODES, features), BF16),
            v((LAYERS + samples, NODES, features), BF16),
            v((LAYERS + samples, NODES, features), F32),
            v((LAYERS + samples, NODES, features), F32),
            v((LAYERS, NODES, 128), F32),
            v((NODES, features), BF16),
            v((NODES, features), F32),
            v((LAYERS + samples, NODES, features), BF16),
            v((total_rows, features), F32),
            v((8, features), F32),
            v((4, total_rows // CORES // 4, features), F32),
            v((2, 2, FAR, piece, features), F32),
            v((2, piece, features), F32),
            v((8, features), F32),
            v((8, features), F32),
            v((RING, 8, features), F32),
            dma((10,)),
            dma((2,)),
            dma((3, 3)),
            dma((3, 3)),
            dma((3, 3)),
            dma((3, 3)),
            dma((3,)),
            dma((3,)),
            dma((2, CHUNKS)),
            dma((2, CHUNKS)),
            dma((LAYERS, 2)),
            dma((samples, 2)),
            dma((4,)),
            dma((4,)),
            dma((2, 2, FAR)),
            dma((2, 2, FAR)),
            dma((2,)),
            dma((2,)),
            dma((2, 2, FAR)),
            dma((2, 2, FAR)),
            dma((2, RING)),
            dma((2, RING)),
            dma((2,)),
            dma((2,)),
            dma((STEPS,)),
            dma((STEPS,)),
        ],
        compiler_params=pltpu.CompilerParams(
            collective_id=0, has_side_effects=True, vmem_limit_bytes=44 * 1024 * 1024
        ),
        name="train_step",
    )(*[pltpu.with_memory_space_constraint(a, pltpu.HBM) for a in args])
    return out.reshape(1, 3, features, features), gain_out


def solution(mesh):
    placed = (
        P("dp", None, None),
        P("dp", None, None),
        P(),
        P(),
        P(),
        P(),
        P(),
        P(),
        P("section", None, None),
        P("section", None, None),
        P("section", None, None),
        P("section", None),
    )
    return jax.shard_map(
        functools.partial(on_device, mesh.shape["section"], mesh.shape["dp"]),
        mesh=mesh,
        in_specs=placed,
        out_specs=(P("section", None, None, None), P("section", None)),
        check_vma=False,
    )
```

```python
import functools
import math

import jax
import jax.numpy as jnp
from jax import lax
from jax.experimental import pallas as pl
from jax.experimental.pallas import tpu as pltpu
from jax.sharding import PartitionSpec as P

BLOCK = 128
NODES = 256
EPSILON = 1e-05
MESH = pl.DeviceIdType.MESH
F32 = jnp.float32
BF16 = jnp.bfloat16
CHUNKS = 2
LAYERS = 4
CORES = 2
RING = 8
STEPS = RING - 1
FAR = RING // 2
STREAMS = 4
SUM = True


def dot(a, b):
    return jnp.dot(a, b, preferred_element_type=F32)


def dot_nt(a, b):
    return lax.dot_general(a, b, (((1,), (1,)), ((), ())), preferred_element_type=F32)


def step_kernel(
    samples,
    loss_scale,
    lat_hbm,
    tgt_hbm,
    g2m_hbm,
    g2m_c_hbm,
    m2m_hbm,
    m2m_c_hbm,
    m2g_hbm,
    m2g_c_hbm,
    wm_hbm,
    wu_hbm,
    wd_hbm,
    gain_hbm,
    out,
    gain_out,
    lat,
    tgt,
    g2m,
    m2m,
    m2g,
    g2m_c,
    m2m_c,
    m2g_c,
    w,
    gain_v,
    gains,
    mix,
    mix_t,
    enc,
    pred,
    seed_t,
    h,
    up,
    unit_s,
    act_s,
    gb_s,
    slope_s,
    normed_s,
    inv_s,
    msg_s,
    up_s,
    gm_s,
    acc,
    gacc,
    sib_buf,
    ring_buf,
    y_buf,
    g_sib,
    g_y,
    g_z,
    in_sem,
    io_sem,
    wt_send,
    wt_recv,
    ws_send,
    ws_recv,
    gn_send,
    gn_recv,
    hop_send,
    hop_recv,
    pass_send,
    pass_recv,
    sib_send,
    sib_recv,
    rs_send,
    rs_recv,
    y_send,
    y_recv,
    ag_send,
    ag_recv,
    fw_send,
    fw_recv,
    gs_sem,
    gy_sem,
    gz_send,
    gz_recv,
):
    features = w.shape[-1]
    s = lax.axis_index("section")
    dp = lax.axis_index("dp")
    core = lax.rem(dp, CORES)
    z = lax.rem(dp // CORES, RING)
    yh = dp // (CORES * RING)
    stage = s // LAYERS
    m = lax.rem(s, LAYERS)
    mx, my = m // 2, lax.rem(m, 2)
    early = stage == 0
    late = stage == 1
    j = jnp.where(early, m, 2 * (1 - mx) + my)
    busy = j < samples

    def dp_at(y_, z_, c_):
        return {"dp": (y_ * RING + z_) * CORES + c_}

    def relative(k):
        x_ = lax.rem(mx + k // 2, 2)
        y_ = lax.rem(my + k % 2, 2)
        return 2 * x_ + y_

    y_cross = lax.rem(yh + core, 2)

    def member_at(layer):
        y_ = jnp.where(lax.rem(layer, 2) == my, yh, y_cross)
        return {"section": LAYERS * stage + layer, "dp": (y_ * RING + z) * CORES + core}

    hop_to = {"section": 2 * (3 - s // 2) + lax.rem(s, 2)}
    sibling = dp_at(yh, z, 1 - core)
    across = dp_at(1 - yh, z, core)
    z_next = lax.rem(z + 1, RING)
    z_prev = lax.rem(z + RING - 1, RING)

    def remote(src, dst, send, recv, where):
        return pltpu.make_async_remote_copy(
            src_ref=src, dst_ref=dst, send_sem=send, recv_sem=recv, device_id=where, device_id_type=MESH
        )

    barrier = pltpu.get_barrier_semaphore()

    def greet(where):
        pl.semaphore_signal(barrier, inc=1, device_id=where, device_id_type=MESH)

    greet(sibling)
    for k in (1, 2, 3):
        greet(member_at(relative(k)))
    greet(hop_to)
    met = 5
    if SUM:
        greet(across)
        for d in range(1, RING):
            greet(dp_at(yh, lax.rem(z + d, RING), core))
        met += RING

    w_hbm = (wm_hbm, wu_hbm, wd_hbm)
    loads = [
        pltpu.make_async_copy(a, b, in_sem.at[i])
        for i, (a, b) in enumerate(
            [
                (g2m_c_hbm, g2m_c),
                (m2m_c_hbm, m2m_c),
                (m2g_c_hbm, m2g_c),
                (g2m_hbm, g2m),
                (m2m_hbm, m2m),
                (gain_hbm, gain_v),
                (m2g_hbm, m2g),
            ]
            + [(w_hbm[i].at[0], w.at[i, m]) for i in range(3)]
        )
    ]
    sample = jnp.minimum(j, samples - 1)
    lat_load = pltpu.make_async_copy(lat_hbm.at[sample], lat, io_sem.at[0])
    tgt_load = pltpu.make_async_copy(tgt_hbm.at[sample], tgt, io_sem.at[1])
    for load in loads:
        load.start()
    lat_load.start()
    tgt_load.start()

    def half_of(i, layer, c):
        rows = features // 2
        return w.at[i, layer, pl.ds(pl.multiple_of(c * rows, 16), rows)]

    def give(k, i):
        if k == 3:
            layer, where = relative(2), member_at(relative(1))
        else:
            layer, where = m, member_at(relative(k))
        rows = features // 2
        here = half_of(i, layer, core)
        src = here if k == 3 else w_hbm[i].at[0, pl.ds(pl.multiple_of(core * rows, 16), rows)]
        return remote(src, here, wt_send.at[k - 1, i], wt_recv.at[k - 1, i], where)

    def got(k, i):
        here = half_of(i, relative(k), core)
        return remote(here, here, wt_send.at[k - 1, i], wt_recv.at[k - 1, i], sibling)

    def share(k, i):
        here = half_of(i, relative(k), core)
        return remote(here, here, ws_send.at[k - 1, i], ws_recv.at[k - 1, i], sibling)

    def shared(k, i):
        here = half_of(i, relative(k), 1 - core)
        return remote(here, here, ws_send.at[k - 1, i], ws_recv.at[k - 1, i], sibling)

    def give_gain(k):
        return remote(gains.at[m], gains.at[m], gn_send.at[k - 1], gn_recv.at[k - 1], member_at(relative(k)))

    def got_gain(k):
        here = gains.at[relative(k)]
        return remote(here, here, gn_send.at[k - 1], gn_recv.at[k - 1], sibling)

    pl.semaphore_wait(barrier, met)
    give(1, 0).start()
    give(2, 0).start()
    for load in loads:
        load.wait()
    gains[m] = jnp.broadcast_to(gain_v[...], (8, features))
    for k in (1, 2, 3):
        give_gain(k).start()

    def kept_if(col, b, tile):
        return jnp.where(jnp.full(tile.shape, col, jnp.int32) == b, tile, jnp.zeros_like(tile))

    for k in range(2):
        for r in range(2):
            tile = m2m[2 * r + k]
            for b in range(2):
                kept = kept_if(m2m_c[2 * r + k], b, tile)
                mix[r * BLOCK : (r + 1) * BLOCK, (2 * k + b) * BLOCK : (2 * k + b + 1) * BLOCK] = kept
                mix_t[b * BLOCK : (b + 1) * BLOCK, (2 * k + r) * BLOCK : (2 * k + r + 1) * BLOCK] = kept.T

    lat_load.wait()
    tgt_load.wait()

    @pl.when(early)
    def _():
        for t in range(4):
            for b in range(4):
                k, r = t % 2, t // 2
                kept = kept_if(g2m_c[t], b, g2m[t])
                enc[r * BLOCK : (r + 1) * BLOCK, (4 * k + b) * BLOCK : (4 * k + b + 1) * BLOCK] = kept

    @pl.when(late)
    def _():
        for t in range(8):
            tile_t = m2g[t].T
            for b in range(2):
                k, r = t % 2, t // 2
                kept = kept_if(m2g_c[t], b, m2g[t])
                pred[r * BLOCK : (r + 1) * BLOCK, (2 * k + b) * BLOCK : (2 * k + b + 1) * BLOCK] = kept
                kept = kept_if(m2g_c[t], b, tile_t)
                seed_t[b * BLOCK : (b + 1) * BLOCK, (4 * k + r) * BLOCK : (4 * k + r + 1) * BLOCK] = kept

    give(1, 0).wait_send()
    give(1, 1).start()
    give(1, 2).start()
    give(2, 0).wait_send()
    give(2, 1).start()

    span = NODES // CHUNKS

    def rows_of(c):
        return pl.ds(c * span, span)

    def hop_f(c):
        return remote(h.at[LAYERS, rows_of(c)], h.at[0, rows_of(c)], hop_send.at[0, c], hop_recv.at[0, c], hop_to)

    def hop_b(c):
        return remote(up.at[0, rows_of(c)], up.at[LAYERS, rows_of(c)], hop_send.at[1, c], hop_recv.at[1, c], hop_to)

    def hand_in(layer, kind):
        ref, at = ((h, layer), (up, layer + 1))[kind]
        return remote(
            ref.at[at], ref.at[LAYERS + 1 + j], pass_send.at[layer, kind], pass_recv.at[j, kind], member_at(layer)
        )

    def handed_in(i, kind):
        here = (h, up)[kind].at[LAYERS + 1 + i]
        return remote(here, here, pass_send.at[0, kind], pass_recv.at[i, kind], sibling)

    def forward(q, layer, own):
        at = q if own else q + 1
        gain = gains[layer, 0:1, :]
        if own:

            @pl.when(late & (q == 0))
            def _():
                for c in range(CHUNKS):
                    hop_f(c).wait_recv()

        for c in range(CHUNKS):
            rows = rows_of(c)
            x = h[at, rows, :].astype(F32)
            center = x - jnp.mean(x, axis=-1, keepdims=True)
            inverse = lax.rsqrt(jnp.mean(center * center, axis=-1, keepdims=True) + EPSILON)
            normed = center * inverse
            unit = (normed * gain).astype(BF16)
            normed_s[q, rows, :] = normed
            if own:
                inv_s[q, rows, :] = jnp.broadcast_to(inverse, (span, 128))
            unit_s[q, rows, :] = unit
            msg_s[rows, :] = dot(unit, w[0, layer]).astype(BF16)
            up_s[rows, :] = dot(unit, w[1, layer])
        for c in range(CHUNKS):
            rows = rows_of(c)
            before = up_s[rows, :] + dot(mix[rows, :NODES], msg_s[...]) + dot(mix[rows, NODES:], msg_s[...])
            sigma = 1.0 / (1.0 + jnp.exp(-before))
            active = (before * sigma).astype(BF16)
            slope_s[q, rows, :] = sigma * (1.0 + before * (1.0 - sigma))
            act_s[q, rows, :] = active
            if own:
                output = h[q, rows, :].astype(F32) + dot(active, w[2, layer])
                h[q + 1, rows, :] = output.astype(BF16)
        if own:

            @pl.when(early & (q == LAYERS - 1))
            def _():
                for c in range(CHUNKS):
                    hop_f(c).start()

    def encode():
        grid_rows = lat.shape[0]
        h[0] = (dot(enc[:, :grid_rows], lat[...]) + dot(enc[:, grid_rows:], lat[...])).astype(BF16)

    def decode():
        upstream = jnp.zeros((NODES, features), F32)
        for r in range(4):
            here = pl.ds(r * BLOCK, BLOCK)
            predicted = dot(pred[here, :NODES], h[LAYERS]) + dot(pred[here, NODES:], h[LAYERS])
            target = tgt[r * BLOCK : (r + 1) * BLOCK, :].astype(F32)
            residual = ((predicted - target) * loss_scale).astype(BF16)
            for k in range(2):
                part = seed_t[:, (4 * k + r) * BLOCK : (4 * k + r + 1) * BLOCK]
                upstream = upstream + dot(part, residual)
        up[LAYERS] = upstream.astype(BF16)

    def backward(q, layer, own):
        gain = gains[layer, 0:1, :]
        gb_s[q] = (dot_nt(up[q + 1], w[2, layer]) * slope_s[q]).astype(BF16)
        gm_s[q] = (dot(mix_t[:, :NODES], gb_s[q]) + dot(mix_t[:, NODES:], gb_s[q])).astype(BF16)
        up_s[...] = dot_nt(gb_s[q], w[1, layer]) + dot_nt(gm_s[q], w[0, layer])

        @pl.when(layer == m)
        def _():
            gacc[...] += jnp.sum((up_s[...] * normed_s[q]).reshape(NODES // 8, 8, features), axis=0)

        if own:

            @pl.when(late | (q > 0))
            def _():
                for c in range(CHUNKS):
                    rows = rows_of(c)
                    grad_normed = up_s[rows, :] * gain
                    normed = normed_s[q, rows, :]
                    inverse = inv_s[q, rows, :][:, :1]
                    grad_inputs = up[q + 1, rows, :].astype(F32) + inverse * (
                        grad_normed
                        - jnp.mean(grad_normed, axis=-1, keepdims=True)
                        - normed * jnp.mean(grad_normed * normed, axis=-1, keepdims=True)
                    )
                    up[q, rows, :] = grad_inputs.astype(BF16)

            @pl.when(late & (q == 0))
            def _():
                for c in range(CHUNKS):
                    hop_b(c).start()

    def add_weight_grads(q):
        for n, (left, right) in enumerate(((unit_s, gm_s), (unit_s, gb_s), (act_s, None))):
            rows = pl.ds(n * features, features)
            acc[rows, :] += dot(left[q].T, up[q + 1] if right is None else right[q])

    def round_of(l):
        last = 0
        for i in range(LAYERS):
            far = 2 * lax.rem(i // 2 + mx, 2) + lax.rem(i % 2 + my, 2)
            last = jnp.maximum(last, jnp.where(l >= i, far, 0))
        return jnp.where(early, last, LAYERS - 1)

    @pl.loop(0, LAYERS * LAYERS)
    def _(t):
        e, l = t // LAYERS, lax.rem(t, LAYERS)

        @pl.when((e == 1) & (l == 0))
        def _():
            for k in (1, 2, 3):
                got_gain(k).wait_recv()
            for k, i in ((1, 0), (2, 0), (1, 1), (1, 2)):
                got(k, i).wait_recv()
                if k == 2:
                    give(3, i).start()
                share(k, i).start()
            give(2, 1).wait_send()
            give(2, 2).start()
            for i in range(3):
                shared(1, i).wait_recv()

        @pl.when((e == 2) & (l == 0))
        def _():
            for i in (1, 2):
                got(2, i).wait_recv()
                give(3, i).start()
                share(2, i).start()
            for i in range(3):
                shared(2, i).wait_recv()

        @pl.when((e == 3) & (l == 0))
        def _():
            for i in range(3):
                got(3, i).wait_recv()
                share(3, i).start()
            for i in range(3):
                shared(3, i).wait_recv()

        @pl.when(busy & (round_of(l) == e))
        def _():
            @pl.when(early & (l == 0))
            def _():
                encode()

            @pl.when(late & (l != m))
            def _():
                @pl.when(l > 0)
                def _():
                    hand_in(l, 0).start()

            forward(l, l, True)

    @pl.when(busy & late)
    def _():
        decode()

    @pl.when(busy)
    def _():
        @pl.loop(0, LAYERS)
        def _(l):
            @pl.when((l != m) & (early | (l == 0)))
            def _():
                hand_in(l, 0).start()

        @pl.when(m != LAYERS - 1)
        def _():
            @pl.when(late)
            def _():
                hand_in(LAYERS - 1, 1).start()

    acc[...] = jnp.zeros_like(acc)
    gacc[...] = jnp.zeros_like(gacc)

    @pl.loop(0, LAYERS + samples)
    def _(t):
        other = jnp.where(early, t, t - LAYERS)
        l = LAYERS - 1 - jnp.where(early, t - samples, t)

        @pl.when((other >= 0) & (other < samples) & (other != j))
        def _():
            handed_in(other, 0).wait_recv()
            forward(LAYERS + other, m, False)

        @pl.when(busy & (l >= 0) & (l < LAYERS))
        def _():
            @pl.when(early & (l == LAYERS - 1))
            def _():
                for c in range(CHUNKS):
                    hop_b(c).wait_recv()

                @pl.when(m != LAYERS - 1)
                def _():
                    hand_in(LAYERS - 1, 1).start()

            @pl.when(late | (l > 0) | (m == 0))
            def _():
                backward(l, l, True)

            @pl.when((l > 0) & (l - 1 != m))
            def _():
                hand_in(l - 1, 1).start()

    @pl.loop(0, samples)
    def _(t):
        i = lax.rem(j + t, samples)
        mine = i == j

        @pl.when(jnp.logical_not(mine))
        def _():
            handed_in(i, 1).wait_recv()
            backward(LAYERS + i, m, False)

        add_weight_grads(jnp.where(mine, m, LAYERS + i))

    def finish_sends():
        for k in (1, 2, 3):
            give_gain(k).wait_send()
            for i in range(3):
                if (k, i) not in ((1, 0), (2, 0), (2, 1)):
                    give(k, i).wait_send()
                share(k, i).wait_send()

        @pl.when(busy)
        def _():
            for c in range(CHUNKS):

                @pl.when(early)
                def _():
                    hop_f(c).wait_send()

                @pl.when(late)
                def _():
                    hop_b(c).wait_send()

            @pl.loop(0, LAYERS)
            def _(l):
                @pl.when(l != m)
                def _():
                    for kind in range(2):
                        hand_in(l, kind).wait_send()

    if not SUM:
        finish_sends()
        return

    half = acc.shape[0] // CORES
    chunk = half // RING
    piece = chunk // STREAMS

    def toward(d):
        return dp_at(yh, z_next if d == 0 else z_prev, core)

    def owner_at(d, shift):
        return lax.rem(z + (shift if d == 0 else RING - shift), RING)

    def rows_at(c, u, owner):
        return pl.ds(pl.multiple_of(c * half + owner * chunk + u * piece, 8), piece)

    def steps(u, d):
        return FAR if u % 2 == d else FAR - 1

    pairs = [((u, 0), (u + 1, 1)) for u in range(0, STREAMS, 2)] + [((u + 1, 0), (u, 1)) for u in range(0, STREAMS, 2)]
    flows = [flow for pair in pairs for flow in pair]

    def chunk_rows(c, shift):
        return pl.ds(pl.multiple_of(c * half + lax.rem(z + shift, RING) * chunk, 8), chunk)

    def to_sib(shift):
        rows = chunk_rows(1 - core, shift)
        return remote(acc.at[rows], sib_buf.at[shift], sib_send.at[shift], sib_recv.at[shift], sibling)

    def from_sib(*shifts):
        for shift in shifts:
            to_sib(shift).wait_recv()
            acc[chunk_rows(core, shift), :] += sib_buf[shift]

    g_to_sib = remote(gacc, g_sib, gs_sem.at[0], gs_sem.at[1], sibling)
    for shift in (4, 3, 5, 2, 6, 1, 7, 0):
        to_sib(shift).start()
    g_to_sib.start()

    def rs(u, d, t):
        rows = rows_at(core, u, owner_at(d, steps(u, d) - t))
        return remote(acc.at[rows], ring_buf.at[u, d, t], rs_send.at[u, d, t], rs_recv.at[u, d, t], toward(d))

    def take(u, d, t):
        rs(u, d, t).wait_recv()
        acc[rows_at(core, u, owner_at(d, steps(u, d) - t - 1)), :] += ring_buf[u, d, t]

    def start_pair(n):
        if n > 0:
            for u, d in pairs[n - 1]:
                rs(u, d, 0).wait_send()
        for u, d in pairs[n]:
            rs(u, d, 0).start()

    from_sib(4)
    start_pair(0)
    from_sib(3, 5)
    start_pair(1)
    from_sib(2, 6)
    start_pair(2)
    from_sib(1, 7)
    start_pair(3)
    from_sib(0)
    g_to_sib.wait()
    gacc[...] += g_sib[...]
    g_to_y = remote(gacc, g_y, gy_sem.at[0], gy_sem.at[1], across)
    g_to_y.start()
    for t in range(1, FAR):
        for u, d in flows:
            if t < steps(u, d):
                take(u, d, t - 1)
                rs(u, d, t).start()

    def y_copy(u):
        return remote(acc.at[rows_at(core, u, z)], y_buf.at[u], y_send.at[u], y_recv.at[u], across)

    for u in range(STREAMS):
        for d in (1 - u % 2, u % 2):
            take(u, d, steps(u, d) - 1)
        y_copy(u).start()

    g_to_y.wait()
    g_z[z] = gacc[...] + g_y[...]

    def g_spread(d):
        return remote(g_z.at[z], g_z.at[z], gz_send.at[d - 1], gz_recv.at[d - 1], dp_at(yh, lax.rem(z + d, RING), core))

    def g_arrive(d):
        at = lax.rem(z - d + RING, RING)
        return remote(g_z.at[at], g_z.at[at], gz_send.at[d - 1], gz_recv.at[d - 1], dp_at(yh, at, core))

    for d in range(1, RING):
        g_spread(d).start()

    def spread(u, d, t):
        rows = rows_at(core, u, owner_at(1 - d, t))
        return remote(out.at[rows], out.at[rows], ag_send.at[u, d, t], ag_recv.at[u, d, t], toward(d))

    def arrive(u, d, t):
        rows = rows_at(core, u, owner_at(1 - d, t + 1))
        return remote(out.at[rows], out.at[rows], ag_send.at[u, d, t], ag_recv.at[u, d, t], toward(d))

    def hand_over(u, owner):
        rows = rows_at(core, u, owner)
        return remote(out.at[rows], out.at[rows], fw_send.at[u, owner], fw_recv.at[u, owner], sibling)

    def handed_over(u, owner):
        rows = rows_at(1 - core, u, owner)
        return remote(out.at[rows], out.at[rows], fw_send.at[u, owner], fw_recv.at[u, owner], sibling)

    for u in range(STREAMS):
        y_copy(u).wait()
        rows = rows_at(core, u, z)
        out[rows, :] = acc[rows, :] + y_buf[u]
        for d in (u % 2, 1 - u % 2):
            spread(u, d, 0).start()
        hand_over(u, z).start()

    for t in range(FAR):
        for u, d in flows:
            if t < steps(u, d):
                arrive(u, d, t).wait_recv()
                if t + 1 < steps(u, d):
                    spread(u, d, t + 1).start()
                hand_over(u, owner_at(1 - d, t + 1)).start()

    for d in range(1, RING):
        g_arrive(d).wait_recv()
    total = g_z[0]
    for i in range(1, RING):
        total = total + g_z[i]
    gain_out[...] = jnp.sum(total, axis=0, keepdims=True)

    for shift in range(RING):
        to_sib(shift).wait_send()
    for u in range(STREAMS):
        for i in range(RING):
            handed_over(u, i).wait_recv()
            hand_over(u, i).wait_send()
    for u, d in flows:
        for t in range(steps(u, d)):
            if t > 0 or (u, d) in pairs[-1]:
                rs(u, d, t).wait_send()
            spread(u, d, t).wait_send()
    for d in range(1, RING):
        g_spread(d).wait_send()
    finish_sends()


def on_device(sections, replicas, *args):
    samples, grid_rows, features = args[0].shape
    loss_scale = 1.0 / math.sqrt(samples * replicas * grid_rows)
    total_rows = 3 * features
    chunk = total_rows // CORES // RING
    piece = chunk // STREAMS
    dma = pltpu.SemaphoreType.DMA
    v = pltpu.VMEM
    tile = (BLOCK, BLOCK)
    vmem_spec = pl.BlockSpec(memory_space=pltpu.VMEM)
    out, gain_out = pl.pallas_call(
        functools.partial(step_kernel, samples, loss_scale),
        out_shape=(
            jax.ShapeDtypeStruct((total_rows, features), F32),
            jax.ShapeDtypeStruct((1, features), F32),
        ),
        in_specs=[pl.BlockSpec(memory_space=pltpu.HBM)] * 12,
        out_specs=(vmem_spec, vmem_spec),
        scratch_shapes=[
            v((grid_rows, features), BF16),
            v((grid_rows, features), BF16),
            v((4,) + tile, BF16),
            v((4,) + tile, BF16),
            v((8,) + tile, BF16),
            pltpu.SMEM((4,), jnp.int32),
            pltpu.SMEM((4,), jnp.int32),
            pltpu.SMEM((8,), jnp.int32),
            v((3, LAYERS, features, features), BF16),
            v((1, features), F32),
            v((LAYERS, 8, features), F32),
            v((NODES, 2 * NODES), BF16),
            v((NODES, 2 * NODES), BF16),
            v((NODES, 2 * grid_rows), BF16),
            v((grid_rows, 2 * NODES), BF16),
            v((NODES, 2 * grid_rows), BF16),
            v((LAYERS + 1 + samples, NODES, features), BF16),
            v((LAYERS + 1 + samples, NODES, features), BF16),
            v((LAYERS + samples, NODES, features), BF16),
            v((LAYERS + samples, NODES, features), BF16),
            v((LAYERS + samples, NODES, features), BF16),
            v((LAYERS + samples, NODES, features), F32),
            v((LAYERS + samples, NODES, features), F32),
            v((LAYERS, NODES, 128), F32),
            v((NODES, features), BF16),
            v((NODES, features), F32),
            v((LAYERS + samples, NODES, features), BF16),
            v((total_rows, features), F32),
            v((8, features), F32),
            v((RING, chunk, features), F32),
            v((STREAMS, 2, FAR, piece, features), F32),
            v((STREAMS, piece, features), F32),
            v((8, features), F32),
            v((8, features), F32),
            v((RING, 8, features), F32),
            dma((10,)),
            dma((2,)),
            dma((3, 3)),
            dma((3, 3)),
            dma((3, 3)),
            dma((3, 3)),
            dma((3,)),
            dma((3,)),
            dma((2, CHUNKS)),
            dma((2, CHUNKS)),
            dma((LAYERS, 2)),
            dma((samples, 2)),
            dma((RING,)),
            dma((RING,)),
            dma((STREAMS, 2, FAR)),
            dma((STREAMS, 2, FAR)),
            dma((STREAMS,)),
            dma((STREAMS,)),
            dma((STREAMS, 2, FAR)),
            dma((STREAMS, 2, FAR)),
            dma((STREAMS, RING)),
            dma((STREAMS, RING)),
            dma((2,)),
            dma((2,)),
            dma((STEPS,)),
            dma((STEPS,)),
        ],
        compiler_params=pltpu.CompilerParams(
            collective_id=0, has_side_effects=True, vmem_limit_bytes=44 * 1024 * 1024
        ),
        name="train_step",
    )(*[pltpu.with_memory_space_constraint(a, pltpu.HBM) for a in args])
    return out.reshape(1, 3, features, features), gain_out


def solution(mesh):
    placed = (
        P("dp", None, None),
        P("dp", None, None),
        P(),
        P(),
        P(),
        P(),
        P(),
        P(),
        P("section", None, None),
        P("section", None, None),
        P("section", None, None),
        P("section", None),
    )
    return jax.shard_map(
        functools.partial(on_device, mesh.shape["section"], mesh.shape["dp"]),
        mesh=mesh,
        in_specs=placed,
        out_specs=(P("section", None, None, None), P("section", None)),
        check_vma=False,
    )
```

```python
import functools
import math

import jax
import jax.numpy as jnp
from jax import lax
from jax.experimental import pallas as pl
from jax.experimental.pallas import tpu as pltpu
from jax.sharding import PartitionSpec as P

BLOCK = 128
NODES = 256
EPSILON = 1e-05
MESH = pl.DeviceIdType.MESH
F32 = jnp.float32
BF16 = jnp.bfloat16
CHUNKS = 2
GUEST = 2
LAYERS = 4
CORES = 2
RING = 8
STEPS = RING - 1
FAR = RING // 2
STREAMS = 4
SUM = True


def dot(a, b):
    return jnp.dot(a, b, preferred_element_type=F32)


def dot_nt(a, b):
    return lax.dot_general(a, b, (((1,), (1,)), ((), ())), preferred_element_type=F32)


def step_kernel(
    samples,
    loss_scale,
    lat_hbm,
    tgt_hbm,
    g2m_hbm,
    g2m_c_hbm,
    m2m_hbm,
    m2m_c_hbm,
    m2g_hbm,
    m2g_c_hbm,
    wm_hbm,
    wu_hbm,
    wd_hbm,
    gain_hbm,
    out,
    gain_out,
    lat,
    tgt,
    g2m,
    m2m,
    m2g,
    g2m_c,
    m2m_c,
    m2g_c,
    w,
    gain_v,
    gains,
    mix,
    mix_t,
    enc,
    pred,
    seed_t,
    h,
    up,
    unit_s,
    act_s,
    gb_s,
    slope_s,
    normed_s,
    inv_s,
    msg_s,
    up_s,
    gm_s,
    acc,
    gacc,
    sib_buf,
    ring_buf,
    y_buf,
    g_sib,
    g_y,
    g_z,
    in_sem,
    io_sem,
    wt_send,
    wt_recv,
    ws_send,
    ws_recv,
    gn_send,
    gn_recv,
    hop_send,
    hop_recv,
    guest_send,
    guest_recv,
    pass_send,
    pass_recv,
    sib_send,
    sib_recv,
    rs_send,
    rs_recv,
    y_send,
    y_recv,
    ag_send,
    ag_recv,
    fw_send,
    fw_recv,
    gs_sem,
    gy_sem,
    gz_send,
    gz_recv,
):
    features = w.shape[-1]
    s = lax.axis_index("section")
    dp = lax.axis_index("dp")
    core = lax.rem(dp, CORES)
    z = lax.rem(dp // CORES, RING)
    yh = dp // (CORES * RING)
    stage = s // LAYERS
    m = lax.rem(s, LAYERS)
    mx, my = m // 2, lax.rem(m, 2)
    early = stage == 0
    late = stage == 1
    j = jnp.where(early, m, 2 * (1 - mx) + my)
    busy = j < samples
    host = early & (m == 0)
    guest = early & (m == 2)

    def dp_at(y_, z_, c_):
        return {"dp": (y_ * RING + z_) * CORES + c_}

    def relative(k):
        x_ = lax.rem(mx + k // 2, 2)
        y_ = lax.rem(my + k % 2, 2)
        return 2 * x_ + y_

    y_cross = lax.rem(yh + core, 2)

    def member_at(layer):
        y_ = jnp.where(lax.rem(layer, 2) == my, yh, y_cross)
        return {"section": LAYERS * stage + layer, "dp": (y_ * RING + z) * CORES + core}

    hop_to = {"section": 2 * (3 - s // 2) + lax.rem(s, 2)}
    sibling = dp_at(yh, z, 1 - core)
    across = dp_at(1 - yh, z, core)
    z_next = lax.rem(z + 1, RING)
    z_prev = lax.rem(z + RING - 1, RING)

    def remote(src, dst, send, recv, where):
        return pltpu.make_async_remote_copy(
            src_ref=src, dst_ref=dst, send_sem=send, recv_sem=recv, device_id=where, device_id_type=MESH
        )

    barrier = pltpu.get_barrier_semaphore()

    def greet(where):
        pl.semaphore_signal(barrier, inc=1, device_id=where, device_id_type=MESH)

    greet(sibling)
    for k in (1, 2, 3):
        greet(member_at(relative(k)))
    greet(hop_to)
    met = 5
    if SUM:
        greet(across)
        for d in range(1, RING):
            greet(dp_at(yh, lax.rem(z + d, RING), core))
        met += RING

    w_hbm = (wm_hbm, wu_hbm, wd_hbm)
    loads = [
        pltpu.make_async_copy(a, b, in_sem.at[i])
        for i, (a, b) in enumerate(
            [
                (g2m_c_hbm, g2m_c),
                (m2m_c_hbm, m2m_c),
                (m2g_c_hbm, m2g_c),
                (g2m_hbm, g2m),
                (m2m_hbm, m2m),
                (gain_hbm, gain_v),
                (m2g_hbm, m2g),
            ]
            + [(w_hbm[i].at[0], w.at[i, m]) for i in range(3)]
        )
    ]
    sample = jnp.minimum(j, samples - 1)
    lat_load = pltpu.make_async_copy(lat_hbm.at[sample], lat.at[0], io_sem.at[0])
    guest_load = pltpu.make_async_copy(lat_hbm.at[GUEST], lat.at[1], io_sem.at[2])
    tgt_load = pltpu.make_async_copy(tgt_hbm.at[sample], tgt, io_sem.at[1])
    for load in loads:
        load.start()
    lat_load.start()
    guest_load.start()
    tgt_load.start()

    def half_of(i, layer, c):
        rows = features // 2
        return w.at[i, layer, pl.ds(pl.multiple_of(c * rows, 16), rows)]

    def give(k, i):
        if k == 3:
            layer, where = relative(2), member_at(relative(1))
        else:
            layer, where = m, member_at(relative(k))
        rows = features // 2
        here = half_of(i, layer, core)
        src = here if k == 3 else w_hbm[i].at[0, pl.ds(pl.multiple_of(core * rows, 16), rows)]
        return remote(src, here, wt_send.at[k - 1, i], wt_recv.at[k - 1, i], where)

    def got(k, i):
        here = half_of(i, relative(k), core)
        return remote(here, here, wt_send.at[k - 1, i], wt_recv.at[k - 1, i], sibling)

    def share(k, i):
        here = half_of(i, relative(k), core)
        return remote(here, here, ws_send.at[k - 1, i], ws_recv.at[k - 1, i], sibling)

    def shared(k, i):
        here = half_of(i, relative(k), 1 - core)
        return remote(here, here, ws_send.at[k - 1, i], ws_recv.at[k - 1, i], sibling)

    def give_gain(k):
        return remote(gains.at[m], gains.at[m], gn_send.at[k - 1], gn_recv.at[k - 1], member_at(relative(k)))

    def got_gain(k):
        here = gains.at[relative(k)]
        return remote(here, here, gn_send.at[k - 1], gn_recv.at[k - 1], sibling)

    pl.semaphore_wait(barrier, met)
    give(1, 0).start()
    give(2, 0).start()
    for load in loads:
        load.wait()
    gains[m] = jnp.broadcast_to(gain_v[...], (8, features))
    for k in (1, 2, 3):
        give_gain(k).start()

    def kept_if(col, b, tile):
        return jnp.where(jnp.full(tile.shape, col, jnp.int32) == b, tile, jnp.zeros_like(tile))

    for k in range(2):
        for r in range(2):
            tile = m2m[2 * r + k]
            for b in range(2):
                kept = kept_if(m2m_c[2 * r + k], b, tile)
                mix[r * BLOCK : (r + 1) * BLOCK, (2 * k + b) * BLOCK : (2 * k + b + 1) * BLOCK] = kept
                mix_t[b * BLOCK : (b + 1) * BLOCK, (2 * k + r) * BLOCK : (2 * k + r + 1) * BLOCK] = kept.T

    lat_load.wait()
    guest_load.wait()
    tgt_load.wait()

    @pl.when(early)
    def _():
        for t in range(4):
            for b in range(4):
                k, r = t % 2, t // 2
                kept = kept_if(g2m_c[t], b, g2m[t])
                enc[r * BLOCK : (r + 1) * BLOCK, (4 * k + b) * BLOCK : (4 * k + b + 1) * BLOCK] = kept

    @pl.when(late)
    def _():
        for t in range(8):
            tile_t = m2g[t].T
            for b in range(2):
                k, r = t % 2, t // 2
                kept = kept_if(m2g_c[t], b, m2g[t])
                pred[r * BLOCK : (r + 1) * BLOCK, (2 * k + b) * BLOCK : (2 * k + b + 1) * BLOCK] = kept
                kept = kept_if(m2g_c[t], b, tile_t)
                seed_t[b * BLOCK : (b + 1) * BLOCK, (4 * k + r) * BLOCK : (4 * k + r + 1) * BLOCK] = kept

    give(1, 0).wait_send()
    give(1, 1).start()
    give(1, 2).start()
    give(2, 0).wait_send()
    give(2, 1).start()

    span = NODES // CHUNKS

    def rows_of(c):
        return pl.ds(c * span, span)

    def hop_f(c):
        return remote(h.at[LAYERS, rows_of(c)], h.at[0, rows_of(c)], hop_send.at[0, c], hop_recv.at[0, c], hop_to)

    def hop_b(c):
        return remote(up.at[0, rows_of(c)], up.at[LAYERS, rows_of(c)], hop_send.at[1, c], hop_recv.at[1, c], hop_to)

    def hand_in(layer, kind):
        ref, at = ((h, layer), (up, layer + 1))[kind]
        return remote(
            ref.at[at], ref.at[LAYERS + 1 + j], pass_send.at[layer, kind], pass_recv.at[j, kind], member_at(layer)
        )

    def handed_in(i, kind):
        here = (h, up)[kind].at[LAYERS + 1 + i]
        return remote(here, here, pass_send.at[0, kind], pass_recv.at[i, kind], sibling)

    def forward(q, layer, at, output_at=None):
        gain = gains[layer, 0:1, :]
        for c in range(CHUNKS):
            rows = rows_of(c)
            x = h[at, rows, :].astype(F32)
            center = x - jnp.mean(x, axis=-1, keepdims=True)
            inverse = lax.rsqrt(jnp.mean(center * center, axis=-1, keepdims=True) + EPSILON)
            normed = center * inverse
            unit = (normed * gain).astype(BF16)
            normed_s[q, rows, :] = normed
            inv_s[q, rows, :] = jnp.broadcast_to(inverse, (span, 128))
            unit_s[q, rows, :] = unit
            msg_s[rows, :] = dot(unit, w[0, layer]).astype(BF16)
            up_s[rows, :] = dot(unit, w[1, layer])
        for c in range(CHUNKS):
            rows = rows_of(c)
            before = up_s[rows, :] + dot(mix[rows, :NODES], msg_s[...]) + dot(mix[rows, NODES:], msg_s[...])
            sigma = 1.0 / (1.0 + jnp.exp(-before))
            active = (before * sigma).astype(BF16)
            slope_s[q, rows, :] = sigma * (1.0 + before * (1.0 - sigma))
            act_s[q, rows, :] = active
            if output_at is not None:
                output = h[at, rows, :].astype(F32) + dot(active, w[2, layer])
                h[output_at, rows, :] = output.astype(BF16)

    guest_h = LAYERS + 1 + samples

    def guest_rows(n):
        return remote(h.at[guest_h + n], h.at[1 + n], guest_send.at[n], guest_recv.at[n], member_at(2))

    def encode(i, at):
        grid_rows = lat.shape[1]
        h[at] = (dot(enc[:, :grid_rows], lat[i]) + dot(enc[:, grid_rows:], lat[i])).astype(BF16)

    def decode():
        upstream = jnp.zeros((NODES, features), F32)
        for r in range(4):
            here = pl.ds(r * BLOCK, BLOCK)
            predicted = dot(pred[here, :NODES], h[LAYERS]) + dot(pred[here, NODES:], h[LAYERS])
            target = tgt[r * BLOCK : (r + 1) * BLOCK, :].astype(F32)
            residual = ((predicted - target) * loss_scale).astype(BF16)
            for k in range(2):
                part = seed_t[:, (4 * k + r) * BLOCK : (4 * k + r + 1) * BLOCK]
                upstream = upstream + dot(part, residual)
        up[LAYERS] = upstream.astype(BF16)

    def backward(q, layer, own):
        gain = gains[layer, 0:1, :]
        gb_s[q] = (dot_nt(up[q + 1], w[2, layer]) * slope_s[q]).astype(BF16)
        gm_s[q] = (dot(mix_t[:, :NODES], gb_s[q]) + dot(mix_t[:, NODES:], gb_s[q])).astype(BF16)
        up_s[...] = dot_nt(gb_s[q], w[1, layer]) + dot_nt(gm_s[q], w[0, layer])

        @pl.when(layer == m)
        def _():
            gacc[...] += jnp.sum((up_s[...] * normed_s[q]).reshape(NODES // 8, 8, features), axis=0)

        if own:

            @pl.when(late | (q > 0))
            def _():
                for c in range(CHUNKS):
                    rows = rows_of(c)
                    grad_normed = up_s[rows, :] * gain
                    normed = normed_s[q, rows, :]
                    inverse = inv_s[q, rows, :][:, :1]
                    grad_inputs = up[q + 1, rows, :].astype(F32) + inverse * (
                        grad_normed
                        - jnp.mean(grad_normed, axis=-1, keepdims=True)
                        - normed * jnp.mean(grad_normed * normed, axis=-1, keepdims=True)
                    )
                    up[q, rows, :] = grad_inputs.astype(BF16)

            @pl.when(late & (q == 0))
            def _():
                for c in range(CHUNKS):
                    hop_b(c).start()

    def add_weight_grads(q):
        for n, (left, right) in enumerate(((unit_s, gm_s), (unit_s, gb_s), (act_s, None))):
            rows = pl.ds(n * features, features)
            acc[rows, :] += dot(left[q].T, up[q + 1] if right is None else right[q])

    def round_of(l):
        last = 0
        for i in range(LAYERS):
            far = 2 * lax.rem(i // 2 + mx, 2) + lax.rem(i % 2 + my, 2)
            last = jnp.maximum(last, jnp.where(l >= i, far, 0))
        return jnp.where(early, jnp.where(guest, jnp.where(l < 2, LAYERS, 2), last), LAYERS - 1)

    @pl.loop(0, LAYERS * LAYERS)
    def _(t):
        e, l = t // LAYERS, lax.rem(t, LAYERS)

        @pl.when((e == 1) & (l == 0))
        def _():
            for k in (1, 2, 3):
                got_gain(k).wait_recv()
            for k, i in ((1, 0), (2, 0), (1, 1), (1, 2)):
                got(k, i).wait_recv()
                if k == 2:
                    give(3, i).start()
                share(k, i).start()
            give(2, 1).wait_send()
            give(2, 2).start()
            for i in range(3):
                shared(1, i).wait_recv()

        @pl.when((e == 2) & (l == 0))
        def _():
            for i in (1, 2):
                got(2, i).wait_recv()
                give(3, i).start()
                share(2, i).start()
            for i in range(3):
                shared(2, i).wait_recv()

        @pl.when((e == 3) & (l == 0))
        def _():
            for i in range(3):
                got(3, i).wait_recv()
                share(3, i).start()
            for i in range(3):
                shared(3, i).wait_recv()

        @pl.when(host & (l == e) & (e < 2))
        def _():
            @pl.when(e == 0)
            def _():
                encode(1, LAYERS + 1 + GUEST)

            forward(jnp.where(e == 0, LAYERS + GUEST, LAYERS + samples), e, jnp.where(e == 0, LAYERS + 1 + GUEST, guest_h), guest_h + e)

            @pl.when(e == 1)
            def _():
                guest_rows(1).start()
                guest_rows(0).start()

        @pl.when(busy & (round_of(l) == e))
        def _():
            @pl.when(early & (l == 0))
            def _():
                encode(0, 0)

            @pl.when(late & (l == 0))
            def _():
                for c in range(CHUNKS):
                    hop_f(c).wait_recv()

            @pl.when(guest & (l == 2))
            def _():
                guest_rows(1).wait_recv()

            @pl.when(late & (l != m))
            def _():
                @pl.when(l > 0)
                def _():
                    hand_in(l, 0).start()

            forward(l, l, l, l + 1)

            @pl.when(early & (l == LAYERS - 1))
            def _():
                for c in range(CHUNKS):
                    hop_f(c).start()

    @pl.when(busy & late)
    def _():
        decode()

    @pl.when(guest)
    def _():
        guest_rows(0).wait_recv()

    @pl.when(busy)
    def _():
        @pl.loop(0, LAYERS)
        def _(l):
            @pl.when((l != m) & (early | (l == 0)) & jnp.logical_not(guest & (l == 0)))
            def _():
                hand_in(l, 0).start()

        @pl.when(m != LAYERS - 1)
        def _():
            @pl.when(late)
            def _():
                hand_in(LAYERS - 1, 1).start()

    acc[...] = jnp.zeros_like(acc)
    gacc[...] = jnp.zeros_like(gacc)

    @pl.loop(0, LAYERS + samples)
    def _(t):
        other = jnp.where(early, t, t - LAYERS)
        l = LAYERS - 1 - jnp.where(early, t - samples, t)

        again = guest & (other == j)

        @pl.when((other >= 0) & (other < samples) & ((other != j) | again) & jnp.logical_not(host & (other == GUEST)))
        def _():
            @pl.when(jnp.logical_not(again))
            def _():
                handed_in(other, 0).wait_recv()

            forward(jnp.where(again, 1, LAYERS + other), jnp.where(again, 1, m), jnp.where(again, 1, LAYERS + 1 + other))

        @pl.when(busy & (l >= 0) & (l < LAYERS))
        def _():
            @pl.when(early & (l == LAYERS - 1))
            def _():
                for c in range(CHUNKS):
                    hop_b(c).wait_recv()

                @pl.when(m != LAYERS - 1)
                def _():
                    hand_in(LAYERS - 1, 1).start()

            @pl.when(late | (l > 0) | (m == 0))
            def _():
                backward(l, l, True)

            @pl.when((l > 0) & (l - 1 != m))
            def _():
                hand_in(l - 1, 1).start()

    @pl.loop(0, samples)
    def _(t):
        i = lax.rem(j + t, samples)
        mine = i == j

        @pl.when(jnp.logical_not(mine))
        def _():
            handed_in(i, 1).wait_recv()
            backward(LAYERS + i, m, False)

        add_weight_grads(jnp.where(mine, m, LAYERS + i))

    def finish_sends():
        for k in (1, 2, 3):
            give_gain(k).wait_send()
            for i in range(3):
                if (k, i) not in ((1, 0), (2, 0), (2, 1)):
                    give(k, i).wait_send()
                share(k, i).wait_send()

        @pl.when(busy)
        def _():
            for c in range(CHUNKS):

                @pl.when(early)
                def _():
                    hop_f(c).wait_send()

                @pl.when(late)
                def _():
                    hop_b(c).wait_send()

            @pl.loop(0, LAYERS)
            def _(l):
                @pl.when(l != m)
                def _():
                    @pl.when(jnp.logical_not(guest & (l == 0)))
                    def _():
                        hand_in(l, 0).wait_send()

                    hand_in(l, 1).wait_send()

        @pl.when(host)
        def _():
            for n in range(2):
                guest_rows(n).wait_send()

    if not SUM:
        finish_sends()
        return

    half = acc.shape[0] // CORES
    chunk = half // RING
    piece = chunk // STREAMS

    def toward(d):
        return dp_at(yh, z_next if d == 0 else z_prev, core)

    def owner_at(d, shift):
        return lax.rem(z + (shift if d == 0 else RING - shift), RING)

    def rows_at(c, u, owner):
        return pl.ds(pl.multiple_of(c * half + owner * chunk + u * piece, 8), piece)

    def steps(u, d):
        return FAR if u % 2 == d else FAR - 1

    pairs = [((u, 0), (u + 1, 1)) for u in range(0, STREAMS, 2)] + [((u + 1, 0), (u, 1)) for u in range(0, STREAMS, 2)]
    flows = [flow for pair in pairs for flow in pair]

    def chunk_rows(c, shift):
        return pl.ds(pl.multiple_of(c * half + lax.rem(z + shift, RING) * chunk, 8), chunk)

    def to_sib(shift):
        rows = chunk_rows(1 - core, shift)
        return remote(acc.at[rows], sib_buf.at[shift], sib_send.at[shift], sib_recv.at[shift], sibling)

    def from_sib(*shifts):
        for shift in shifts:
            to_sib(shift).wait_recv()
            acc[chunk_rows(core, shift), :] += sib_buf[shift]

    g_to_sib = remote(gacc, g_sib, gs_sem.at[0], gs_sem.at[1], sibling)
    for shift in (4, 3, 5, 2, 6, 1, 7, 0):
        to_sib(shift).start()
    g_to_sib.start()

    def rs(u, d, t):
        rows = rows_at(core, u, owner_at(d, steps(u, d) - t))
        return remote(acc.at[rows], ring_buf.at[u, d, t], rs_send.at[u, d, t], rs_recv.at[u, d, t], toward(d))

    def take(u, d, t):
        rs(u, d, t).wait_recv()
        acc[rows_at(core, u, owner_at(d, steps(u, d) - t - 1)), :] += ring_buf[u, d, t]

    def start_pair(n):
        if n > 0:
            for u, d in pairs[n - 1]:
                rs(u, d, 0).wait_send()
        for u, d in pairs[n]:
            rs(u, d, 0).start()

    from_sib(4)
    start_pair(0)
    from_sib(3, 5)
    start_pair(1)
    from_sib(2, 6)
    start_pair(2)
    from_sib(1, 7)
    start_pair(3)
    from_sib(0)
    g_to_sib.wait()
    gacc[...] += g_sib[...]
    g_to_y = remote(gacc, g_y, gy_sem.at[0], gy_sem.at[1], across)
    g_to_y.start()
    for t in range(1, FAR):
        for u, d in flows:
            if t < steps(u, d):
                take(u, d, t - 1)
                rs(u, d, t).start()

    def y_copy(u):
        return remote(acc.at[rows_at(core, u, z)], y_buf.at[u], y_send.at[u], y_recv.at[u], across)

    for u in range(STREAMS):
        for d in (1 - u % 2, u % 2):
            take(u, d, steps(u, d) - 1)
        y_copy(u).start()

    g_to_y.wait()
    g_z[z] = gacc[...] + g_y[...]

    def g_spread(d):
        return remote(g_z.at[z], g_z.at[z], gz_send.at[d - 1], gz_recv.at[d - 1], dp_at(yh, lax.rem(z + d, RING), core))

    def g_arrive(d):
        at = lax.rem(z - d + RING, RING)
        return remote(g_z.at[at], g_z.at[at], gz_send.at[d - 1], gz_recv.at[d - 1], dp_at(yh, at, core))

    for d in range(1, RING):
        g_spread(d).start()

    def spread(u, d, t):
        rows = rows_at(core, u, owner_at(1 - d, t))
        return remote(out.at[rows], out.at[rows], ag_send.at[u, d, t], ag_recv.at[u, d, t], toward(d))

    def arrive(u, d, t):
        rows = rows_at(core, u, owner_at(1 - d, t + 1))
        return remote(out.at[rows], out.at[rows], ag_send.at[u, d, t], ag_recv.at[u, d, t], toward(d))

    def hand_over(u, owner):
        rows = rows_at(core, u, owner)
        return remote(out.at[rows], out.at[rows], fw_send.at[u, owner], fw_recv.at[u, owner], sibling)

    def handed_over(u, owner):
        rows = rows_at(1 - core, u, owner)
        return remote(out.at[rows], out.at[rows], fw_send.at[u, owner], fw_recv.at[u, owner], sibling)

    for u in range(STREAMS):
        y_copy(u).wait()
        rows = rows_at(core, u, z)
        out[rows, :] = acc[rows, :] + y_buf[u]
        for d in (u % 2, 1 - u % 2):
            spread(u, d, 0).start()
        hand_over(u, z).start()

    for t in range(FAR):
        for u, d in flows:
            if t < steps(u, d):
                arrive(u, d, t).wait_recv()
                if t + 1 < steps(u, d):
                    spread(u, d, t + 1).start()
                hand_over(u, owner_at(1 - d, t + 1)).start()

    for d in range(1, RING):
        g_arrive(d).wait_recv()
    total = g_z[0]
    for i in range(1, RING):
        total = total + g_z[i]
    gain_out[...] = jnp.sum(total, axis=0, keepdims=True)

    for shift in range(RING):
        to_sib(shift).wait_send()
    for u in range(STREAMS):
        for i in range(RING):
            handed_over(u, i).wait_recv()
            hand_over(u, i).wait_send()
    for u, d in flows:
        for t in range(steps(u, d)):
            if t > 0 or (u, d) in pairs[-1]:
                rs(u, d, t).wait_send()
            spread(u, d, t).wait_send()
    for d in range(1, RING):
        g_spread(d).wait_send()
    finish_sends()


def on_device(sections, replicas, *args):
    samples, grid_rows, features = args[0].shape
    loss_scale = 1.0 / math.sqrt(samples * replicas * grid_rows)
    total_rows = 3 * features
    chunk = total_rows // CORES // RING
    piece = chunk // STREAMS
    dma = pltpu.SemaphoreType.DMA
    v = pltpu.VMEM
    tile = (BLOCK, BLOCK)
    vmem_spec = pl.BlockSpec(memory_space=pltpu.VMEM)
    out, gain_out = pl.pallas_call(
        functools.partial(step_kernel, samples, loss_scale),
        out_shape=(
            jax.ShapeDtypeStruct((total_rows, features), F32),
            jax.ShapeDtypeStruct((1, features), F32),
        ),
        in_specs=[pl.BlockSpec(memory_space=pltpu.HBM)] * 12,
        out_specs=(vmem_spec, vmem_spec),
        scratch_shapes=[
            v((2, grid_rows, features), BF16),
            v((grid_rows, features), BF16),
            v((4,) + tile, BF16),
            v((4,) + tile, BF16),
            v((8,) + tile, BF16),
            pltpu.SMEM((4,), jnp.int32),
            pltpu.SMEM((4,), jnp.int32),
            pltpu.SMEM((8,), jnp.int32),
            v((3, LAYERS, features, features), BF16),
            v((1, features), F32),
            v((LAYERS, 8, features), F32),
            v((NODES, 2 * NODES), BF16),
            v((NODES, 2 * NODES), BF16),
            v((NODES, 2 * grid_rows), BF16),
            v((grid_rows, 2 * NODES), BF16),
            v((NODES, 2 * grid_rows), BF16),
            v((LAYERS + 3 + samples, NODES, features), BF16),
            v((LAYERS + 1 + samples, NODES, features), BF16),
            v((LAYERS + 1 + samples, NODES, features), BF16),
            v((LAYERS + 1 + samples, NODES, features), BF16),
            v((LAYERS + samples, NODES, features), BF16),
            v((LAYERS + 1 + samples, NODES, features), F32),
            v((LAYERS + 1 + samples, NODES, features), F32),
            v((LAYERS + 1 + samples, NODES, 128), F32),
            v((NODES, features), BF16),
            v((NODES, features), F32),
            v((LAYERS + samples, NODES, features), BF16),
            v((total_rows, features), F32),
            v((8, features), F32),
            v((RING, chunk, features), F32),
            v((STREAMS, 2, FAR, piece, features), F32),
            v((STREAMS, piece, features), F32),
            v((8, features), F32),
            v((8, features), F32),
            v((RING, 8, features), F32),
            dma((10,)),
            dma((3,)),
            dma((3, 3)),
            dma((3, 3)),
            dma((3, 3)),
            dma((3, 3)),
            dma((3,)),
            dma((3,)),
            dma((2, CHUNKS)),
            dma((2, CHUNKS)),
            dma((2,)),
            dma((2,)),
            dma((LAYERS, 2)),
            dma((samples, 2)),
            dma((RING,)),
            dma((RING,)),
            dma((STREAMS, 2, FAR)),
            dma((STREAMS, 2, FAR)),
            dma((STREAMS,)),
            dma((STREAMS,)),
            dma((STREAMS, 2, FAR)),
            dma((STREAMS, 2, FAR)),
            dma((STREAMS, RING)),
            dma((STREAMS, RING)),
            dma((2,)),
            dma((2,)),
            dma((STEPS,)),
            dma((STEPS,)),
        ],
        compiler_params=pltpu.CompilerParams(
            collective_id=0, has_side_effects=True, vmem_limit_bytes=44 * 1024 * 1024
        ),
        name="train_step",
    )(*[pltpu.with_memory_space_constraint(a, pltpu.HBM) for a in args])
    return out.reshape(1, 3, features, features), gain_out


def solution(mesh):
    placed = (
        P("dp", None, None),
        P("dp", None, None),
        P(),
        P(),
        P(),
        P(),
        P(),
        P(),
        P("section", None, None),
        P("section", None, None),
        P("section", None, None),
        P("section", None),
    )
    return jax.shard_map(
        functools.partial(on_device, mesh.shape["section"], mesh.shape["dp"]),
        mesh=mesh,
        in_specs=placed,
        out_specs=(P("section", None, None, None), P("section", None)),
        check_vma=False,
    )
```

```python
import functools
import math

import jax
import jax.numpy as jnp
from jax import lax
from jax.experimental import pallas as pl
from jax.experimental.pallas import tpu as pltpu
from jax.sharding import PartitionSpec as P

BLOCK = 128
NODES = 256
EPSILON = 1e-05
MESH = pl.DeviceIdType.MESH
F32 = jnp.float32
BF16 = jnp.bfloat16
CHUNKS = 2
GUEST = 2
LAYERS = 4
CORES = 2
RING = 8
STEPS = RING - 1
FAR = RING // 2
STREAMS = 4
WIDE = 2
SUM = True


def dot(a, b):
    return jnp.dot(a, b, preferred_element_type=F32)


def dot_nt(a, b):
    return lax.dot_general(a, b, (((1,), (1,)), ((), ())), preferred_element_type=F32)


def step_kernel(
    samples,
    loss_scale,
    lat_hbm,
    tgt_hbm,
    g2m_hbm,
    g2m_c_hbm,
    m2m_hbm,
    m2m_c_hbm,
    m2g_hbm,
    m2g_c_hbm,
    wm_hbm,
    wu_hbm,
    wd_hbm,
    gain_hbm,
    out,
    gain_out,
    lat,
    tgt,
    g2m,
    m2m,
    m2g,
    g2m_c,
    m2m_c,
    m2g_c,
    w,
    gain_v,
    gains,
    mix,
    mix_t,
    enc,
    pred,
    seed_t,
    h,
    up,
    unit_s,
    act_s,
    gb_s,
    slope_s,
    normed_s,
    inv_s,
    msg_s,
    up_s,
    gm_s,
    acc,
    gacc,
    sib_buf,
    ring_buf,
    y_buf,
    narrow,
    g_sib,
    g_y,
    g_z,
    in_sem,
    io_sem,
    wt_send,
    wt_recv,
    ws_send,
    ws_recv,
    gn_send,
    gn_recv,
    hop_send,
    hop_recv,
    guest_send,
    guest_recv,
    pass_send,
    pass_recv,
    sib_send,
    sib_recv,
    rs_send,
    rs_recv,
    y_send,
    y_recv,
    ag_send,
    ag_recv,
    fw_send,
    fw_recv,
    gs_sem,
    gy_sem,
    gz_send,
    gz_recv,
):
    features = w.shape[-1]
    s = lax.axis_index("section")
    dp = lax.axis_index("dp")
    core = lax.rem(dp, CORES)
    z = lax.rem(dp // CORES, RING)
    yh = dp // (CORES * RING)
    stage = s // LAYERS
    m = lax.rem(s, LAYERS)
    mx, my = m // 2, lax.rem(m, 2)
    early = stage == 0
    late = stage == 1
    j = jnp.where(early, m, 2 * (1 - mx) + my)
    busy = j < samples
    host = early & (m == 0)
    guest = early & (m == 2)

    def dp_at(y_, z_, c_):
        return {"dp": (y_ * RING + z_) * CORES + c_}

    def relative(k):
        x_ = lax.rem(mx + k // 2, 2)
        y_ = lax.rem(my + k % 2, 2)
        return 2 * x_ + y_

    y_cross = lax.rem(yh + core, 2)

    def member_at(layer):
        y_ = jnp.where(lax.rem(layer, 2) == my, yh, y_cross)
        return {"section": LAYERS * stage + layer, "dp": (y_ * RING + z) * CORES + core}

    hop_to = {"section": 2 * (3 - s // 2) + lax.rem(s, 2)}
    sibling = dp_at(yh, z, 1 - core)
    across = dp_at(1 - yh, z, core)
    z_next = lax.rem(z + 1, RING)
    z_prev = lax.rem(z + RING - 1, RING)

    def remote(src, dst, send, recv, where):
        return pltpu.make_async_remote_copy(
            src_ref=src, dst_ref=dst, send_sem=send, recv_sem=recv, device_id=where, device_id_type=MESH
        )

    barrier = pltpu.get_barrier_semaphore()

    def greet(where):
        pl.semaphore_signal(barrier, inc=1, device_id=where, device_id_type=MESH)

    greet(sibling)
    for k in (1, 2, 3):
        greet(member_at(relative(k)))
    greet(hop_to)
    met = 5
    if SUM:
        greet(across)
        for d in range(1, RING):
            greet(dp_at(yh, lax.rem(z + d, RING), core))
        met += RING

    w_hbm = (wm_hbm, wu_hbm, wd_hbm)
    loads = [
        pltpu.make_async_copy(a, b, in_sem.at[i])
        for i, (a, b) in enumerate(
            [
                (g2m_c_hbm, g2m_c),
                (m2m_c_hbm, m2m_c),
                (m2g_c_hbm, m2g_c),
                (g2m_hbm, g2m),
                (m2m_hbm, m2m),
                (gain_hbm, gain_v),
                (m2g_hbm, m2g),
            ]
            + [(w_hbm[i].at[0], w.at[i, m]) for i in range(3)]
        )
    ]
    sample = jnp.minimum(j, samples - 1)
    lat_load = pltpu.make_async_copy(lat_hbm.at[sample], lat.at[0], io_sem.at[0])
    guest_load = pltpu.make_async_copy(lat_hbm.at[GUEST], lat.at[1], io_sem.at[2])
    tgt_load = pltpu.make_async_copy(tgt_hbm.at[sample], tgt, io_sem.at[1])
    for load in loads:
        load.start()
    lat_load.start()
    guest_load.start()
    tgt_load.start()

    def half_of(i, layer, c):
        rows = features // 2
        return w.at[i, layer, pl.ds(pl.multiple_of(c * rows, 16), rows)]

    def give(k, i):
        if k == 3:
            layer, where = relative(2), member_at(relative(1))
        else:
            layer, where = m, member_at(relative(k))
        rows = features // 2
        here = half_of(i, layer, core)
        src = here if k == 3 else w_hbm[i].at[0, pl.ds(pl.multiple_of(core * rows, 16), rows)]
        return remote(src, here, wt_send.at[k - 1, i], wt_recv.at[k - 1, i], where)

    def got(k, i):
        here = half_of(i, relative(k), core)
        return remote(here, here, wt_send.at[k - 1, i], wt_recv.at[k - 1, i], sibling)

    def share(k, i):
        here = half_of(i, relative(k), core)
        return remote(here, here, ws_send.at[k - 1, i], ws_recv.at[k - 1, i], sibling)

    def shared(k, i):
        here = half_of(i, relative(k), 1 - core)
        return remote(here, here, ws_send.at[k - 1, i], ws_recv.at[k - 1, i], sibling)

    def give_gain(k):
        return remote(gains.at[m], gains.at[m], gn_send.at[k - 1], gn_recv.at[k - 1], member_at(relative(k)))

    def got_gain(k):
        here = gains.at[relative(k)]
        return remote(here, here, gn_send.at[k - 1], gn_recv.at[k - 1], sibling)

    pl.semaphore_wait(barrier, met)
    give(1, 0).start()
    give(2, 0).start()
    for load in loads:
        load.wait()
    gains[m] = jnp.broadcast_to(gain_v[...], (8, features))
    for k in (1, 2, 3):
        give_gain(k).start()

    def kept_if(col, b, tile):
        return jnp.where(jnp.full(tile.shape, col, jnp.int32) == b, tile, jnp.zeros_like(tile))

    for k in range(2):
        for r in range(2):
            tile = m2m[2 * r + k]
            for b in range(2):
                kept = kept_if(m2m_c[2 * r + k], b, tile)
                mix[r * BLOCK : (r + 1) * BLOCK, (2 * k + b) * BLOCK : (2 * k + b + 1) * BLOCK] = kept
                mix_t[b * BLOCK : (b + 1) * BLOCK, (2 * k + r) * BLOCK : (2 * k + r + 1) * BLOCK] = kept.T

    lat_load.wait()
    guest_load.wait()
    tgt_load.wait()

    @pl.when(early)
    def _():
        for t in range(4):
            for b in range(4):
                k, r = t % 2, t // 2
                kept = kept_if(g2m_c[t], b, g2m[t])
                enc[r * BLOCK : (r + 1) * BLOCK, (4 * k + b) * BLOCK : (4 * k + b + 1) * BLOCK] = kept

    @pl.when(late)
    def _():
        for t in range(8):
            tile_t = m2g[t].T
            for b in range(2):
                k, r = t % 2, t // 2
                kept = kept_if(m2g_c[t], b, m2g[t])
                pred[r * BLOCK : (r + 1) * BLOCK, (2 * k + b) * BLOCK : (2 * k + b + 1) * BLOCK] = kept
                kept = kept_if(m2g_c[t], b, tile_t)
                seed_t[b * BLOCK : (b + 1) * BLOCK, (4 * k + r) * BLOCK : (4 * k + r + 1) * BLOCK] = kept

    give(1, 0).wait_send()
    give(1, 1).start()
    give(1, 2).start()
    give(2, 0).wait_send()
    give(2, 1).start()

    span = NODES // CHUNKS

    def rows_of(c):
        return pl.ds(c * span, span)

    def hop_f(c):
        return remote(h.at[LAYERS, rows_of(c)], h.at[0, rows_of(c)], hop_send.at[0, c], hop_recv.at[0, c], hop_to)

    def hop_b(c):
        return remote(up.at[0, rows_of(c)], up.at[LAYERS, rows_of(c)], hop_send.at[1, c], hop_recv.at[1, c], hop_to)

    def hand_in(layer, kind):
        ref, at = ((h, layer), (up, layer + 1))[kind]
        return remote(
            ref.at[at], ref.at[LAYERS + 1 + j], pass_send.at[layer, kind], pass_recv.at[j, kind], member_at(layer)
        )

    def handed_in(i, kind):
        here = (h, up)[kind].at[LAYERS + 1 + i]
        return remote(here, here, pass_send.at[0, kind], pass_recv.at[i, kind], sibling)

    def forward(q, layer, at, output_at=None):
        gain = gains[layer, 0:1, :]
        for c in range(CHUNKS):
            rows = rows_of(c)
            x = h[at, rows, :].astype(F32)
            center = x - jnp.mean(x, axis=-1, keepdims=True)
            inverse = lax.rsqrt(jnp.mean(center * center, axis=-1, keepdims=True) + EPSILON)
            normed = center * inverse
            unit = (normed * gain).astype(BF16)
            normed_s[q, rows, :] = normed
            inv_s[q, rows, :] = jnp.broadcast_to(inverse, (span, 128))
            unit_s[q, rows, :] = unit
            msg_s[rows, :] = dot(unit, w[0, layer]).astype(BF16)
            up_s[rows, :] = dot(unit, w[1, layer])
        for c in range(CHUNKS):
            rows = rows_of(c)
            before = up_s[rows, :] + dot(mix[rows, :NODES], msg_s[...]) + dot(mix[rows, NODES:], msg_s[...])
            sigma = 1.0 / (1.0 + jnp.exp(-before))
            active = (before * sigma).astype(BF16)
            slope_s[q, rows, :] = sigma * (1.0 + before * (1.0 - sigma))
            act_s[q, rows, :] = active
            if output_at is not None:
                output = h[at, rows, :].astype(F32) + dot(active, w[2, layer])
                h[output_at, rows, :] = output.astype(BF16)

    guest_h = LAYERS + 1 + samples

    def guest_rows(n):
        return remote(h.at[guest_h + n], h.at[1 + n], guest_send.at[n], guest_recv.at[n], member_at(2))

    def encode(i, at):
        grid_rows = lat.shape[1]
        h[at] = (dot(enc[:, :grid_rows], lat[i]) + dot(enc[:, grid_rows:], lat[i])).astype(BF16)

    def decode():
        upstream = jnp.zeros((NODES, features), F32)
        for r in range(4):
            here = pl.ds(r * BLOCK, BLOCK)
            predicted = dot(pred[here, :NODES], h[LAYERS]) + dot(pred[here, NODES:], h[LAYERS])
            target = tgt[r * BLOCK : (r + 1) * BLOCK, :].astype(F32)
            residual = ((predicted - target) * loss_scale).astype(BF16)
            for k in range(2):
                part = seed_t[:, (4 * k + r) * BLOCK : (4 * k + r + 1) * BLOCK]
                upstream = upstream + dot(part, residual)
        up[LAYERS] = upstream.astype(BF16)

    def grad_unit(q, layer):
        up_s[...] = dot_nt(gb_s[q], w[1, layer]) + dot_nt(gm_s[q], w[0, layer])

    def add_gain_grads(q):
        gacc[...] += jnp.sum((up_s[...] * normed_s[q]).reshape(NODES // 8, 8, features), axis=0)

    def backward(q, layer, own):
        gain = gains[layer, 0:1, :]
        gb_s[q] = (dot_nt(up[q + 1], w[2, layer]) * slope_s[q]).astype(BF16)
        gm_s[q] = (dot(mix_t[:, :NODES], gb_s[q]) + dot(mix_t[:, NODES:], gb_s[q])).astype(BF16)
        if own:
            grad_unit(q, layer)

            @pl.when(layer == m)
            def _():
                add_gain_grads(q)

            @pl.when(late | (q > 0))
            def _():
                for c in range(CHUNKS):
                    rows = rows_of(c)
                    grad_normed = up_s[rows, :] * gain
                    normed = normed_s[q, rows, :]
                    inverse = inv_s[q, rows, :][:, :1]
                    grad_inputs = up[q + 1, rows, :].astype(F32) + inverse * (
                        grad_normed
                        - jnp.mean(grad_normed, axis=-1, keepdims=True)
                        - normed * jnp.mean(grad_normed * normed, axis=-1, keepdims=True)
                    )
                    up[q, rows, :] = grad_inputs.astype(BF16)

            @pl.when(late & (q == 0))
            def _():
                for c in range(CHUNKS):
                    hop_b(c).start()

    def add_weight_grads(q):
        for n, (left, right) in enumerate(((unit_s, gm_s), (unit_s, gb_s), (act_s, None))):
            rows = pl.ds(n * features, features)
            acc[rows, :] += dot(left[q].T, up[q + 1] if right is None else right[q])

    def round_of(l):
        last = 0
        for i in range(LAYERS):
            far = 2 * lax.rem(i // 2 + mx, 2) + lax.rem(i % 2 + my, 2)
            last = jnp.maximum(last, jnp.where(l >= i, far, 0))
        return jnp.where(early, jnp.where(guest, jnp.where(l < 2, LAYERS, 2), last), LAYERS - 1)

    @pl.loop(0, LAYERS * LAYERS)
    def _(t):
        e, l = t // LAYERS, lax.rem(t, LAYERS)

        @pl.when((e == 1) & (l == 0))
        def _():
            for k in (1, 2, 3):
                got_gain(k).wait_recv()
            for k, i in ((1, 0), (2, 0), (1, 1), (1, 2)):
                got(k, i).wait_recv()
                if k == 2:
                    give(3, i).start()
                share(k, i).start()
            give(2, 1).wait_send()
            give(2, 2).start()
            for i in range(3):
                shared(1, i).wait_recv()

        @pl.when((e == 2) & (l == 0))
        def _():
            for i in (1, 2):
                got(2, i).wait_recv()
                give(3, i).start()
                share(2, i).start()
            for i in range(3):
                shared(2, i).wait_recv()

        @pl.when((e == 3) & (l == 0))
        def _():
            for i in range(3):
                got(3, i).wait_recv()
                share(3, i).start()
            for i in range(3):
                shared(3, i).wait_recv()

        @pl.when(host & (l == e) & (e < 2))
        def _():
            @pl.when(e == 0)
            def _():
                encode(1, LAYERS + 1 + GUEST)

            forward(jnp.where(e == 0, LAYERS + GUEST, LAYERS + samples), e, jnp.where(e == 0, LAYERS + 1 + GUEST, guest_h), guest_h + e)

            @pl.when(e == 1)
            def _():
                guest_rows(1).start()
                guest_rows(0).start()

        @pl.when(busy & (round_of(l) == e))
        def _():
            @pl.when(early & (l == 0))
            def _():
                encode(0, 0)

            @pl.when(late & (l == 0))
            def _():
                for c in range(CHUNKS):
                    hop_f(c).wait_recv()

            @pl.when(guest & (l == 2))
            def _():
                guest_rows(1).wait_recv()

            @pl.when(late & (l != m))
            def _():
                @pl.when(l > 0)
                def _():
                    hand_in(l, 0).start()

            forward(l, l, l, l + 1)

            @pl.when(early & (l == LAYERS - 1))
            def _():
                for c in range(CHUNKS):
                    hop_f(c).start()

    @pl.when(busy & late)
    def _():
        decode()

    @pl.when(guest)
    def _():
        guest_rows(0).wait_recv()

    @pl.when(busy)
    def _():
        @pl.loop(0, LAYERS)
        def _(l):
            @pl.when((l != m) & (early | (l == 0)) & jnp.logical_not(guest & (l == 0)))
            def _():
                hand_in(l, 0).start()

        @pl.when(m != LAYERS - 1)
        def _():
            @pl.when(late)
            def _():
                hand_in(LAYERS - 1, 1).start()

    acc[...] = jnp.zeros_like(acc)
    gacc[...] = jnp.zeros_like(gacc)

    @pl.loop(0, LAYERS + samples)
    def _(t):
        other = jnp.where(early, t, t - LAYERS)
        l = LAYERS - 1 - jnp.where(early, t - samples, t)

        again = guest & (other == j)

        @pl.when((other >= 0) & (other < samples) & ((other != j) | again) & jnp.logical_not(host & (other == GUEST)))
        def _():
            @pl.when(jnp.logical_not(again))
            def _():
                handed_in(other, 0).wait_recv()

            forward(jnp.where(again, 1, LAYERS + other), jnp.where(again, 1, m), jnp.where(again, 1, LAYERS + 1 + other))

        @pl.when(busy & (l >= 0) & (l < LAYERS))
        def _():
            @pl.when(early & (l == LAYERS - 1))
            def _():
                for c in range(CHUNKS):
                    hop_b(c).wait_recv()

                @pl.when(m != LAYERS - 1)
                def _():
                    hand_in(LAYERS - 1, 1).start()

            @pl.when(late | (l > 0) | (m == 0))
            def _():
                backward(l, l, True)

            @pl.when((l > 0) & (l - 1 != m))
            def _():
                hand_in(l - 1, 1).start()

    @pl.loop(0, samples)
    def _(t):
        i = lax.rem(j + t, samples)
        mine = i == j

        @pl.when(jnp.logical_not(mine))
        def _():
            handed_in(i, 1).wait_recv()
            backward(LAYERS + i, m, False)

        add_weight_grads(jnp.where(mine, m, LAYERS + i))

    def finish_sends():
        for k in (1, 2, 3):
            give_gain(k).wait_send()
            for i in range(3):
                if (k, i) not in ((1, 0), (2, 0), (2, 1)):
                    give(k, i).wait_send()
                share(k, i).wait_send()

        @pl.when(busy)
        def _():
            for c in range(CHUNKS):

                @pl.when(early)
                def _():
                    hop_f(c).wait_send()

                @pl.when(late)
                def _():
                    hop_b(c).wait_send()

            @pl.loop(0, LAYERS)
            def _(l):
                @pl.when(l != m)
                def _():
                    @pl.when(jnp.logical_not(guest & (l == 0)))
                    def _():
                        hand_in(l, 0).wait_send()

                    hand_in(l, 1).wait_send()

        @pl.when(host)
        def _():
            for n in range(2):
                guest_rows(n).wait_send()

    def other_gain_grads():
        @pl.loop(0, samples)
        def _(i):
            @pl.when(i != j)
            def _():
                grad_unit(LAYERS + i, m)
                add_gain_grads(LAYERS + i)

    if not SUM:
        other_gain_grads()
        finish_sends()
        return

    half = acc.shape[0] // CORES
    chunk = half // RING
    piece = chunk // STREAMS

    def toward(d):
        return dp_at(yh, z_next if d == 0 else z_prev, core)

    def owner_at(d, shift):
        return lax.rem(z + (shift if d == 0 else RING - shift), RING)

    def rows_at(c, u, owner):
        return pl.ds(pl.multiple_of(c * half + owner * chunk + u * piece, 8), piece)

    def steps(u, d):
        return FAR if u % 2 == d else FAR - 1

    pairs = [((u, 0), (u + 1, 1)) for u in range(0, STREAMS, 2)] + [((u + 1, 0), (u, 1)) for u in range(0, STREAMS, 2)]
    flows = [flow for pair in pairs for flow in pair]

    def chunk_rows(c, shift):
        return pl.ds(pl.multiple_of(c * half + lax.rem(z + shift, RING) * chunk, 8), chunk)

    def to_sib(shift):
        rows = chunk_rows(1 - core, shift)
        return remote(acc.at[rows], sib_buf.at[shift], sib_send.at[shift], sib_recv.at[shift], sibling)

    def from_sib(*shifts):
        for shift in shifts:
            to_sib(shift).wait_recv()
            acc[chunk_rows(core, shift), :] += sib_buf[shift]

    g_to_sib = remote(gacc, g_sib, gs_sem.at[0], gs_sem.at[1], sibling)
    for shift in (4, 3, 5, 2, 6, 1, 7, 0):
        to_sib(shift).start()

    def rs(u, d, t):
        rows = rows_at(core, u, owner_at(d, steps(u, d) - t))
        return remote(acc.at[rows], ring_buf.at[u, d, t], rs_send.at[u, d, t], rs_recv.at[u, d, t], toward(d))

    def take(u, d, t):
        rs(u, d, t).wait_recv()
        acc[rows_at(core, u, owner_at(d, steps(u, d) - t - 1)), :] += ring_buf[u, d, t]

    def start_pair(n):
        if n > 0:
            for u, d in pairs[n - 1]:
                rs(u, d, 0).wait_send()
        for u, d in pairs[n]:
            rs(u, d, 0).start()

    from_sib(4)
    start_pair(0)
    from_sib(3, 5)
    start_pair(1)
    from_sib(2, 6)
    start_pair(2)
    from_sib(1, 7)
    start_pair(3)
    from_sib(0)
    other_gain_grads()
    g_to_sib.start()
    g_to_y = remote(gacc, g_y, gy_sem.at[0], gy_sem.at[1], across)
    for t in range(1, FAR):
        if t == 2:
            g_to_sib.wait()
            gacc[...] += g_sib[...]
            g_to_y.start()
        for u, d in flows:
            if t < steps(u, d):
                take(u, d, t - 1)
                rs(u, d, t).start()

    def y_copy(u):
        return remote(acc.at[rows_at(core, u, z)], y_buf.at[u], y_send.at[u], y_recv.at[u], across)

    for u in range(STREAMS):
        for d in (1 - u % 2, u % 2):
            take(u, d, steps(u, d) - 1)
        y_copy(u).start()

    g_to_y.wait()
    g_z[z] = gacc[...] + g_y[...]

    def g_spread(d):
        return remote(g_z.at[z], g_z.at[z], gz_send.at[d - 1], gz_recv.at[d - 1], dp_at(yh, lax.rem(z + d, RING), core))

    def g_arrive(d):
        at = lax.rem(z - d + RING, RING)
        return remote(g_z.at[at], g_z.at[at], gz_send.at[d - 1], gz_recv.at[d - 1], dp_at(yh, at, core))

    for d in range(1, RING):
        g_spread(d).start()

    def finished(c, u, owner):
        return out.at[rows_at(c, u, owner)] if u < WIDE else narrow.at[c, u - WIDE, owner]

    def widen(c, u, owner):
        if u >= WIDE:
            out[rows_at(c, u, owner), :] = narrow[c, u - WIDE, owner].astype(F32)

    def spread(u, d, t):
        here = finished(core, u, owner_at(1 - d, t))
        return remote(here, here, ag_send.at[u, d, t], ag_recv.at[u, d, t], toward(d))

    def arrive(u, d, t):
        here = finished(core, u, owner_at(1 - d, t + 1))
        return remote(here, here, ag_send.at[u, d, t], ag_recv.at[u, d, t], toward(d))

    def hand_over(u, owner):
        here = finished(core, u, owner)
        return remote(here, here, fw_send.at[u, owner], fw_recv.at[u, owner], sibling)

    def handed_over(u, owner):
        here = finished(1 - core, u, owner)
        return remote(here, here, fw_send.at[u, owner], fw_recv.at[u, owner], sibling)

    for u in range(STREAMS):
        y_copy(u).wait()
        rows = rows_at(core, u, z)
        total = acc[rows, :] + y_buf[u]
        if u < WIDE:
            out[rows, :] = total
        else:
            narrow[core, u - WIDE, z] = total.astype(BF16)
        for d in (u % 2, 1 - u % 2):
            spread(u, d, 0).start()
        hand_over(u, z).start()
        widen(core, u, z)

    for t in range(FAR):
        for u, d in flows:
            if t < steps(u, d):
                arrive(u, d, t).wait_recv()
                if t + 1 < steps(u, d):
                    spread(u, d, t + 1).start()
                hand_over(u, owner_at(1 - d, t + 1)).start()
                widen(core, u, owner_at(1 - d, t + 1))

    for d in range(1, RING):
        g_arrive(d).wait_recv()
    total = g_z[0]
    for i in range(1, RING):
        total = total + g_z[i]
    gain_out[...] = jnp.sum(total, axis=0, keepdims=True)

    for shift in range(RING):
        to_sib(shift).wait_send()
    for u in range(STREAMS):
        for i in range(RING):
            handed_over(u, i).wait_recv()
            widen(1 - core, u, i)
            hand_over(u, i).wait_send()
    for u, d in flows:
        for t in range(steps(u, d)):
            if t > 0 or (u, d) in pairs[-1]:
                rs(u, d, t).wait_send()
            spread(u, d, t).wait_send()
    for d in range(1, RING):
        g_spread(d).wait_send()
    finish_sends()


def on_device(sections, replicas, *args):
    samples, grid_rows, features = args[0].shape
    loss_scale = 1.0 / math.sqrt(samples * replicas * grid_rows)
    total_rows = 3 * features
    chunk = total_rows // CORES // RING
    piece = chunk // STREAMS
    dma = pltpu.SemaphoreType.DMA
    v = pltpu.VMEM
    tile = (BLOCK, BLOCK)
    vmem_spec = pl.BlockSpec(memory_space=pltpu.VMEM)
    out, gain_out = pl.pallas_call(
        functools.partial(step_kernel, samples, loss_scale),
        out_shape=(
            jax.ShapeDtypeStruct((total_rows, features), F32),
            jax.ShapeDtypeStruct((1, features), F32),
        ),
        in_specs=[pl.BlockSpec(memory_space=pltpu.HBM)] * 12,
        out_specs=(vmem_spec, vmem_spec),
        scratch_shapes=[
            v((2, grid_rows, features), BF16),
            v((grid_rows, features), BF16),
            v((4,) + tile, BF16),
            v((4,) + tile, BF16),
            v((8,) + tile, BF16),
            pltpu.SMEM((4,), jnp.int32),
            pltpu.SMEM((4,), jnp.int32),
            pltpu.SMEM((8,), jnp.int32),
            v((3, LAYERS, features, features), BF16),
            v((1, features), F32),
            v((LAYERS, 8, features), F32),
            v((NODES, 2 * NODES), BF16),
            v((NODES, 2 * NODES), BF16),
            v((NODES, 2 * grid_rows), BF16),
            v((grid_rows, 2 * NODES), BF16),
            v((NODES, 2 * grid_rows), BF16),
            v((LAYERS + 3 + samples, NODES, features), BF16),
            v((LAYERS + 1 + samples, NODES, features), BF16),
            v((LAYERS + 1 + samples, NODES, features), BF16),
            v((LAYERS + 1 + samples, NODES, features), BF16),
            v((LAYERS + samples, NODES, features), BF16),
            v((LAYERS + 1 + samples, NODES, features), F32),
            v((LAYERS + 1 + samples, NODES, features), F32),
            v((LAYERS + 1 + samples, NODES, 128), F32),
            v((NODES, features), BF16),
            v((NODES, features), F32),
            v((LAYERS + samples, NODES, features), BF16),
            v((total_rows, features), F32),
            v((8, features), F32),
            v((RING, chunk, features), F32),
            v((STREAMS, 2, FAR, piece, features), F32),
            v((STREAMS, piece, features), F32),
            v((CORES, STREAMS - WIDE, RING, piece, features), BF16),
            v((8, features), F32),
            v((8, features), F32),
            v((RING, 8, features), F32),
            dma((10,)),
            dma((3,)),
            dma((3, 3)),
            dma((3, 3)),
            dma((3, 3)),
            dma((3, 3)),
            dma((3,)),
            dma((3,)),
            dma((2, CHUNKS)),
            dma((2, CHUNKS)),
            dma((2,)),
            dma((2,)),
            dma((LAYERS, 2)),
            dma((samples, 2)),
            dma((RING,)),
            dma((RING,)),
            dma((STREAMS, 2, FAR)),
            dma((STREAMS, 2, FAR)),
            dma((STREAMS,)),
            dma((STREAMS,)),
            dma((STREAMS, 2, FAR)),
            dma((STREAMS, 2, FAR)),
            dma((STREAMS, RING)),
            dma((STREAMS, RING)),
            dma((2,)),
            dma((2,)),
            dma((STEPS,)),
            dma((STEPS,)),
        ],
        compiler_params=pltpu.CompilerParams(
            collective_id=0, has_side_effects=True, vmem_limit_bytes=44 * 1024 * 1024
        ),
        name="train_step",
    )(*[pltpu.with_memory_space_constraint(a, pltpu.HBM) for a in args])
    return out.reshape(1, 3, features, features), gain_out


def solution(mesh):
    placed = (
        P("dp", None, None),
        P("dp", None, None),
        P(),
        P(),
        P(),
        P(),
        P(),
        P(),
        P("section", None, None),
        P("section", None, None),
        P("section", None, None),
        P("section", None),
    )
    return jax.shard_map(
        functools.partial(on_device, mesh.shape["section"], mesh.shape["dp"]),
        mesh=mesh,
        in_specs=placed,
        out_specs=(P("section", None, None, None), P("section", None)),
        check_vma=False,
    )
```

```python
import functools
import math

import jax
import jax.numpy as jnp
from jax import lax
from jax.experimental import pallas as pl
from jax.experimental.pallas import tpu as pltpu
from jax.sharding import PartitionSpec as P

BLOCK = 128
NODES = 256
EPSILON = 1e-05
MESH = pl.DeviceIdType.MESH
F32 = jnp.float32
BF16 = jnp.bfloat16
CHUNKS = 2
GUEST = 2
LAYERS = 4
CORES = 2
RING = 8
FAR = RING // 2
STREAMS = 4
WIDE = 2
SUM = True


def dot(a, b):
    return jnp.dot(a, b, preferred_element_type=F32)


def dot_nt(a, b):
    return lax.dot_general(a, b, (((1,), (1,)), ((), ())), preferred_element_type=F32)


def step_kernel(
    samples,
    loss_scale,
    lat_hbm,
    tgt_hbm,
    g2m_hbm,
    g2m_c_hbm,
    m2m_hbm,
    m2m_c_hbm,
    m2g_hbm,
    m2g_c_hbm,
    wm_hbm,
    wu_hbm,
    wd_hbm,
    gain_hbm,
    out,
    gain_out,
    lat,
    tgt,
    g2m,
    m2m,
    m2g,
    g2m_c,
    m2m_c,
    m2g_c,
    w,
    gain_v,
    gains,
    mix,
    mix_t,
    enc,
    pred,
    seed_t,
    h,
    up,
    unit_s,
    act_s,
    gb_s,
    slope_s,
    normed_s,
    inv_s,
    msg_s,
    up_s,
    gm_s,
    acc,
    gacc,
    sib_buf,
    ring_buf,
    y_buf,
    narrow,
    g_sib,
    g_y,
    g_z,
    in_sem,
    io_sem,
    wt_send,
    wt_recv,
    ws_send,
    ws_recv,
    gn_send,
    gn_recv,
    hop_send,
    hop_recv,
    guest_send,
    guest_recv,
    pass_send,
    pass_recv,
    sib_send,
    sib_recv,
    rs_send,
    rs_recv,
    y_send,
    y_recv,
    ag_send,
    ag_recv,
    fw_send,
    fw_recv,
    gs_sem,
    gy_sem,
    gz_send,
    gz_recv,
):
    features = w.shape[-1]
    s = lax.axis_index("section")
    dp = lax.axis_index("dp")
    core = lax.rem(dp, CORES)
    z = lax.rem(dp // CORES, RING)
    yh = dp // (CORES * RING)
    stage = s // LAYERS
    m = lax.rem(s, LAYERS)
    mx, my = m // 2, lax.rem(m, 2)
    early = stage == 0
    late = stage == 1
    j = jnp.where(early, m, 2 * (1 - mx) + my)
    busy = j < samples
    host = early & (m == 0)
    guest = early & (m == 2)

    def dp_at(y_, z_, c_):
        return {"dp": (y_ * RING + z_) * CORES + c_}

    def relative(k):
        x_ = lax.rem(mx + k // 2, 2)
        y_ = lax.rem(my + k % 2, 2)
        return 2 * x_ + y_

    y_cross = lax.rem(yh + core, 2)

    def member_at(layer):
        y_ = jnp.where(lax.rem(layer, 2) == my, yh, y_cross)
        return {"section": LAYERS * stage + layer, "dp": (y_ * RING + z) * CORES + core}

    hop_to = {"section": 2 * (3 - s // 2) + lax.rem(s, 2)}
    sibling = dp_at(yh, z, 1 - core)
    across = dp_at(1 - yh, z, core)
    z_next = lax.rem(z + 1, RING)
    z_prev = lax.rem(z + RING - 1, RING)

    def remote(src, dst, send, recv, where):
        return pltpu.make_async_remote_copy(
            src_ref=src, dst_ref=dst, send_sem=send, recv_sem=recv, device_id=where, device_id_type=MESH
        )

    barrier = pltpu.get_barrier_semaphore()

    def greet(where):
        pl.semaphore_signal(barrier, inc=1, device_id=where, device_id_type=MESH)

    greet(sibling)
    for k in (1, 2, 3):
        greet(member_at(relative(k)))
    greet(hop_to)
    met = 5
    if SUM:
        greet(across)
        greet(dp_at(yh, z_next, core))
        greet(dp_at(yh, z_prev, core))
        met += 3

    w_hbm = (wm_hbm, wu_hbm, wd_hbm)
    loads = [
        pltpu.make_async_copy(a, b, in_sem.at[i])
        for i, (a, b) in enumerate(
            [
                (g2m_c_hbm, g2m_c),
                (m2m_c_hbm, m2m_c),
                (m2g_c_hbm, m2g_c),
                (g2m_hbm, g2m),
                (m2m_hbm, m2m),
                (gain_hbm, gain_v),
                (m2g_hbm, m2g),
            ]
            + [(w_hbm[i].at[0], w.at[i, m]) for i in range(3)]
        )
    ]
    sample = jnp.minimum(j, samples - 1)
    lat_load = pltpu.make_async_copy(lat_hbm.at[sample], lat.at[0], io_sem.at[0])
    guest_load = pltpu.make_async_copy(lat_hbm.at[GUEST], lat.at[1], io_sem.at[2])
    tgt_load = pltpu.make_async_copy(tgt_hbm.at[sample], tgt, io_sem.at[1])
    for load in loads:
        load.start()
    lat_load.start()
    guest_load.start()
    tgt_load.start()

    def half_of(i, layer, c):
        rows = features // 2
        return w.at[i, layer, pl.ds(pl.multiple_of(c * rows, 16), rows)]

    def give(k, i):
        if k == 3:
            layer, where = relative(2), member_at(relative(1))
        else:
            layer, where = m, member_at(relative(k))
        rows = features // 2
        here = half_of(i, layer, core)
        src = here if k == 3 else w_hbm[i].at[0, pl.ds(pl.multiple_of(core * rows, 16), rows)]
        return remote(src, here, wt_send.at[k - 1, i], wt_recv.at[k - 1, i], where)

    def got(k, i):
        here = half_of(i, relative(k), core)
        return remote(here, here, wt_send.at[k - 1, i], wt_recv.at[k - 1, i], sibling)

    def share(k, i):
        here = half_of(i, relative(k), core)
        return remote(here, here, ws_send.at[k - 1, i], ws_recv.at[k - 1, i], sibling)

    def shared(k, i):
        here = half_of(i, relative(k), 1 - core)
        return remote(here, here, ws_send.at[k - 1, i], ws_recv.at[k - 1, i], sibling)

    def give_gain(k):
        return remote(gains.at[m], gains.at[m], gn_send.at[k - 1], gn_recv.at[k - 1], member_at(relative(k)))

    def got_gain(k):
        here = gains.at[relative(k)]
        return remote(here, here, gn_send.at[k - 1], gn_recv.at[k - 1], sibling)

    pl.semaphore_wait(barrier, met)
    give(1, 0).start()
    give(2, 0).start()
    for load in loads:
        load.wait()
    gains[m] = jnp.broadcast_to(gain_v[...], (8, features))
    for k in (1, 2, 3):
        give_gain(k).start()

    def kept_if(col, b, tile):
        return jnp.where(jnp.full(tile.shape, col, jnp.int32) == b, tile, jnp.zeros_like(tile))

    for k in range(2):
        for r in range(2):
            tile = m2m[2 * r + k]
            for b in range(2):
                kept = kept_if(m2m_c[2 * r + k], b, tile)
                mix[r * BLOCK : (r + 1) * BLOCK, (2 * k + b) * BLOCK : (2 * k + b + 1) * BLOCK] = kept
                mix_t[b * BLOCK : (b + 1) * BLOCK, (2 * k + r) * BLOCK : (2 * k + r + 1) * BLOCK] = kept.T

    lat_load.wait()
    guest_load.wait()
    tgt_load.wait()

    @pl.when(early)
    def _():
        for t in range(4):
            for b in range(4):
                k, r = t % 2, t // 2
                kept = kept_if(g2m_c[t], b, g2m[t])
                enc[r * BLOCK : (r + 1) * BLOCK, (4 * k + b) * BLOCK : (4 * k + b + 1) * BLOCK] = kept

    @pl.when(late)
    def _():
        for t in range(8):
            tile_t = m2g[t].T
            for b in range(2):
                k, r = t % 2, t // 2
                kept = kept_if(m2g_c[t], b, m2g[t])
                pred[r * BLOCK : (r + 1) * BLOCK, (2 * k + b) * BLOCK : (2 * k + b + 1) * BLOCK] = kept
                kept = kept_if(m2g_c[t], b, tile_t)
                seed_t[b * BLOCK : (b + 1) * BLOCK, (4 * k + r) * BLOCK : (4 * k + r + 1) * BLOCK] = kept

    give(1, 0).wait_send()
    give(1, 1).start()
    give(1, 2).start()
    give(2, 0).wait_send()
    give(2, 1).start()

    span = NODES // CHUNKS

    def rows_of(c):
        return pl.ds(c * span, span)

    def hop_f(c):
        return remote(h.at[LAYERS, rows_of(c)], h.at[0, rows_of(c)], hop_send.at[0, c], hop_recv.at[0, c], hop_to)

    def hop_b(c):
        return remote(up.at[0, rows_of(c)], up.at[LAYERS, rows_of(c)], hop_send.at[1, c], hop_recv.at[1, c], hop_to)

    def hand_in(layer, kind):
        ref, at = ((h, layer), (up, layer + 1))[kind]
        return remote(
            ref.at[at], ref.at[LAYERS + 1 + j], pass_send.at[layer, kind], pass_recv.at[j, kind], member_at(layer)
        )

    def handed_in(i, kind):
        here = (h, up)[kind].at[LAYERS + 1 + i]
        return remote(here, here, pass_send.at[0, kind], pass_recv.at[i, kind], sibling)

    def forward(q, layer, at, output_at=None):
        gain = gains[layer, 0:1, :]
        for c in range(CHUNKS):
            rows = rows_of(c)
            x = h[at, rows, :].astype(F32)
            center = x - jnp.mean(x, axis=-1, keepdims=True)
            inverse = lax.rsqrt(jnp.mean(center * center, axis=-1, keepdims=True) + EPSILON)
            normed = center * inverse
            unit = (normed * gain).astype(BF16)
            normed_s[q, rows, :] = normed
            inv_s[q, rows, :] = jnp.broadcast_to(inverse, (span, 128))
            unit_s[q, rows, :] = unit
            msg_s[rows, :] = dot(unit, w[0, layer]).astype(BF16)
            up_s[rows, :] = dot(unit, w[1, layer])
        for c in range(CHUNKS):
            rows = rows_of(c)
            before = up_s[rows, :] + dot(mix[rows, :NODES], msg_s[...]) + dot(mix[rows, NODES:], msg_s[...])
            sigma = 1.0 / (1.0 + jnp.exp(-before))
            active = (before * sigma).astype(BF16)
            slope_s[q, rows, :] = sigma * (1.0 + before * (1.0 - sigma))
            act_s[q, rows, :] = active
            if output_at is not None:
                output = h[at, rows, :].astype(F32) + dot(active, w[2, layer])
                h[output_at, rows, :] = output.astype(BF16)

    guest_h = LAYERS + 1 + samples

    def guest_rows(n):
        return remote(h.at[guest_h + n], h.at[1 + n], guest_send.at[n], guest_recv.at[n], member_at(2))

    def encode(i, at):
        grid_rows = lat.shape[1]
        h[at] = (dot(enc[:, :grid_rows], lat[i]) + dot(enc[:, grid_rows:], lat[i])).astype(BF16)

    def decode():
        upstream = jnp.zeros((NODES, features), F32)
        for r in range(4):
            here = pl.ds(r * BLOCK, BLOCK)
            predicted = dot(pred[here, :NODES], h[LAYERS]) + dot(pred[here, NODES:], h[LAYERS])
            target = tgt[r * BLOCK : (r + 1) * BLOCK, :].astype(F32)
            residual = ((predicted - target) * loss_scale).astype(BF16)
            for k in range(2):
                part = seed_t[:, (4 * k + r) * BLOCK : (4 * k + r + 1) * BLOCK]
                upstream = upstream + dot(part, residual)
        up[LAYERS] = upstream.astype(BF16)

    def grad_unit(q, layer):
        up_s[...] = dot_nt(gb_s[q], w[1, layer]) + dot_nt(gm_s[q], w[0, layer])

    def add_gain_grads(q):
        gacc[...] += jnp.sum((up_s[...] * normed_s[q]).reshape(NODES // 8, 8, features), axis=0)

    def backward(q, layer, own):
        gain = gains[layer, 0:1, :]
        gb_s[q] = (dot_nt(up[q + 1], w[2, layer]) * slope_s[q]).astype(BF16)
        gm_s[q] = (dot(mix_t[:, :NODES], gb_s[q]) + dot(mix_t[:, NODES:], gb_s[q])).astype(BF16)
        if own:
            grad_unit(q, layer)

            @pl.when(layer == m)
            def _():
                add_gain_grads(q)

            @pl.when(late | (q > 0))
            def _():
                for c in range(CHUNKS):
                    rows = rows_of(c)
                    grad_normed = up_s[rows, :] * gain
                    normed = normed_s[q, rows, :]
                    inverse = inv_s[q, rows, :][:, :1]
                    grad_inputs = up[q + 1, rows, :].astype(F32) + inverse * (
                        grad_normed
                        - jnp.mean(grad_normed, axis=-1, keepdims=True)
                        - normed * jnp.mean(grad_normed * normed, axis=-1, keepdims=True)
                    )
                    up[q, rows, :] = grad_inputs.astype(BF16)

            @pl.when(late & (q == 0))
            def _():
                for c in range(CHUNKS):
                    hop_b(c).start()

    def add_weight_grads(q):
        for n, (left, right) in enumerate(((unit_s, gm_s), (unit_s, gb_s), (act_s, None))):
            rows = pl.ds(n * features, features)
            acc[rows, :] += dot(left[q].T, up[q + 1] if right is None else right[q])

    def round_of(l):
        last = 0
        for i in range(LAYERS):
            far = 2 * lax.rem(i // 2 + mx, 2) + lax.rem(i % 2 + my, 2)
            last = jnp.maximum(last, jnp.where(l >= i, far, 0))
        return jnp.where(early, jnp.where(guest, jnp.where(l < 2, LAYERS, 2), last), LAYERS - 1)

    @pl.loop(0, LAYERS * LAYERS)
    def _(t):
        e, l = t // LAYERS, lax.rem(t, LAYERS)

        @pl.when((e == 1) & (l == 0))
        def _():
            for k in (1, 2, 3):
                got_gain(k).wait_recv()
            for k, i in ((1, 0), (2, 0), (1, 1), (1, 2)):
                got(k, i).wait_recv()
                if k == 2:
                    give(3, i).start()
                share(k, i).start()
            give(2, 1).wait_send()
            give(2, 2).start()
            for i in range(3):
                shared(1, i).wait_recv()

        @pl.when((e == 2) & (l == 0))
        def _():
            for i in (1, 2):
                got(2, i).wait_recv()
                give(3, i).start()
                share(2, i).start()
            for i in range(3):
                shared(2, i).wait_recv()

        @pl.when((e == 3) & (l == 0))
        def _():
            for i in range(3):
                got(3, i).wait_recv()
                share(3, i).start()
            for i in range(3):
                shared(3, i).wait_recv()

        @pl.when(host & (l == e) & (e < 2))
        def _():
            @pl.when(e == 0)
            def _():
                encode(1, LAYERS + 1 + GUEST)

            forward(jnp.where(e == 0, LAYERS + GUEST, LAYERS + samples), e, jnp.where(e == 0, LAYERS + 1 + GUEST, guest_h), guest_h + e)

            @pl.when(e == 1)
            def _():
                guest_rows(1).start()
                guest_rows(0).start()

        @pl.when(busy & (round_of(l) == e))
        def _():
            @pl.when(early & (l == 0))
            def _():
                encode(0, 0)

            @pl.when(late & (l == 0))
            def _():
                for c in range(CHUNKS):
                    hop_f(c).wait_recv()

            @pl.when(guest & (l == 2))
            def _():
                guest_rows(1).wait_recv()

            @pl.when(late & (l != m))
            def _():
                @pl.when(l > 0)
                def _():
                    hand_in(l, 0).start()

            forward(l, l, l, l + 1)

            @pl.when(early & (l == LAYERS - 1))
            def _():
                for c in range(CHUNKS):
                    hop_f(c).start()

    @pl.when(busy & late)
    def _():
        decode()

    @pl.when(guest)
    def _():
        guest_rows(0).wait_recv()

    @pl.when(busy)
    def _():
        @pl.loop(0, LAYERS)
        def _(l):
            @pl.when((l != m) & (early | (l == 0)) & jnp.logical_not(guest & (l == 0)))
            def _():
                hand_in(l, 0).start()

        @pl.when(m != LAYERS - 1)
        def _():
            @pl.when(late)
            def _():
                hand_in(LAYERS - 1, 1).start()

    acc[...] = jnp.zeros_like(acc)
    gacc[...] = jnp.zeros_like(gacc)

    @pl.loop(0, LAYERS + samples)
    def _(t):
        other = jnp.where(early, t, t - LAYERS)
        l = LAYERS - 1 - jnp.where(early, t - samples, t)

        again = guest & (other == j)

        @pl.when((other >= 0) & (other < samples) & ((other != j) | again) & jnp.logical_not(host & (other == GUEST)))
        def _():
            @pl.when(jnp.logical_not(again))
            def _():
                handed_in(other, 0).wait_recv()

            forward(jnp.where(again, 1, LAYERS + other), jnp.where(again, 1, m), jnp.where(again, 1, LAYERS + 1 + other))

        @pl.when(busy & (l >= 0) & (l < LAYERS))
        def _():
            @pl.when(early & (l == LAYERS - 1))
            def _():
                for c in range(CHUNKS):
                    hop_b(c).wait_recv()

                @pl.when(m != LAYERS - 1)
                def _():
                    hand_in(LAYERS - 1, 1).start()

            @pl.when(late | (l > 0) | (m == 0))
            def _():
                backward(l, l, True)

            @pl.when((l > 0) & (l - 1 != m))
            def _():
                hand_in(l - 1, 1).start()

    @pl.loop(0, samples)
    def _(t):
        i = lax.rem(j + t, samples)
        mine = i == j

        @pl.when(jnp.logical_not(mine))
        def _():
            handed_in(i, 1).wait_recv()
            backward(LAYERS + i, m, False)

        add_weight_grads(jnp.where(mine, m, LAYERS + i))

    def finish_sends():
        for k in (1, 2, 3):
            give_gain(k).wait_send()
            for i in range(3):
                if (k, i) not in ((1, 0), (2, 0), (2, 1)):
                    give(k, i).wait_send()
                share(k, i).wait_send()

        @pl.when(busy)
        def _():
            for c in range(CHUNKS):

                @pl.when(early)
                def _():
                    hop_f(c).wait_send()

                @pl.when(late)
                def _():
                    hop_b(c).wait_send()

            @pl.loop(0, LAYERS)
            def _(l):
                @pl.when(l != m)
                def _():
                    @pl.when(jnp.logical_not(guest & (l == 0)))
                    def _():
                        hand_in(l, 0).wait_send()

                    hand_in(l, 1).wait_send()

        @pl.when(host)
        def _():
            for n in range(2):
                guest_rows(n).wait_send()

    def other_gain_grads():
        @pl.loop(0, samples)
        def _(i):
            @pl.when(i != j)
            def _():
                grad_unit(LAYERS + i, m)
                add_gain_grads(LAYERS + i)

    if not SUM:
        other_gain_grads()
        finish_sends()
        return

    half = acc.shape[0] // CORES
    chunk = half // RING
    piece = chunk // STREAMS

    def toward(d):
        return dp_at(yh, z_next if d == 0 else z_prev, core)

    def owner_at(d, shift):
        return lax.rem(z + (shift if d == 0 else RING - shift), RING)

    def rows_at(c, u, owner):
        return pl.ds(pl.multiple_of(c * half + owner * chunk + u * piece, 8), piece)

    def steps(u, d):
        return FAR if u % 2 == d else FAR - 1

    pairs = [((u, 0), (u + 1, 1)) for u in range(0, STREAMS, 2)] + [((u + 1, 0), (u, 1)) for u in range(0, STREAMS, 2)]
    flows = [flow for pair in pairs for flow in pair]

    def chunk_rows(c, shift):
        return pl.ds(pl.multiple_of(c * half + lax.rem(z + shift, RING) * chunk, 8), chunk)

    def to_sib(shift):
        rows = chunk_rows(1 - core, shift)
        return remote(acc.at[rows], sib_buf.at[shift], sib_send.at[shift], sib_recv.at[shift], sibling)

    def from_sib(*shifts):
        for shift in shifts:
            to_sib(shift).wait_recv()
            acc[chunk_rows(core, shift), :] += sib_buf[shift]

    g_to_sib = remote(gacc, g_sib, gs_sem.at[0], gs_sem.at[1], sibling)
    for shift in (4, 3, 5, 2, 6, 1, 7, 0):
        to_sib(shift).start()

    def rs(u, d, t):
        rows = rows_at(core, u, owner_at(d, steps(u, d) - t))
        return remote(acc.at[rows], ring_buf.at[u, d, t], rs_send.at[u, d, t], rs_recv.at[u, d, t], toward(d))

    def take(u, d, t):
        rs(u, d, t).wait_recv()
        acc[rows_at(core, u, owner_at(d, steps(u, d) - t - 1)), :] += ring_buf[u, d, t]

    def start_pair(n):
        if n > 0:
            for u, d in pairs[n - 1]:
                rs(u, d, 0).wait_send()
        for u, d in pairs[n]:
            rs(u, d, 0).start()

    from_sib(4)
    start_pair(0)
    from_sib(3, 5)
    start_pair(1)
    from_sib(2, 6)
    start_pair(2)
    from_sib(1, 7)
    start_pair(3)
    from_sib(0)
    other_gain_grads()
    g_to_sib.start()
    g_to_y = remote(gacc, g_y, gy_sem.at[0], gy_sem.at[1], across)
    for t in range(1, FAR):
        if t == 2:
            g_to_sib.wait()
            gacc[...] += g_sib[...]
            g_to_y.start()
        for u, d in flows:
            if t < steps(u, d):
                take(u, d, t - 1)
                rs(u, d, t).start()

    def y_copy(u):
        return remote(acc.at[rows_at(core, u, z)], y_buf.at[u], y_send.at[u], y_recv.at[u], across)

    for u in range(STREAMS):
        for d in (1 - u % 2, u % 2):
            take(u, d, steps(u, d) - 1)
        y_copy(u).start()

    g_to_y.wait()
    g_z[z] = gacc[...] + g_y[...]

    def g_pass(d, t):
        here = g_z.at[owner_at(1 - d, t)]
        return remote(here, here, gz_send.at[d, t], gz_recv.at[d, t], toward(d))

    def g_arrive(d, t):
        here = g_z.at[owner_at(1 - d, t + 1)]
        return remote(here, here, gz_send.at[d, t], gz_recv.at[d, t], toward(d))

    for d in range(2):
        g_pass(d, 0).start()

    def finished(c, u, owner):
        return out.at[rows_at(c, u, owner)] if u < WIDE else narrow.at[c, u - WIDE, owner]

    def widen(c, u, owner):
        if u >= WIDE:
            out[rows_at(c, u, owner), :] = narrow[c, u - WIDE, owner].astype(F32)

    def spread(u, d, t):
        here = finished(core, u, owner_at(1 - d, t))
        return remote(here, here, ag_send.at[u, d, t], ag_recv.at[u, d, t], toward(d))

    def arrive(u, d, t):
        here = finished(core, u, owner_at(1 - d, t + 1))
        return remote(here, here, ag_send.at[u, d, t], ag_recv.at[u, d, t], toward(d))

    def hand_over(u, owner):
        here = finished(core, u, owner)
        return remote(here, here, fw_send.at[u, owner], fw_recv.at[u, owner], sibling)

    def handed_over(u, owner):
        here = finished(1 - core, u, owner)
        return remote(here, here, fw_send.at[u, owner], fw_recv.at[u, owner], sibling)

    for u in range(STREAMS):
        y_copy(u).wait()
        rows = rows_at(core, u, z)
        total = acc[rows, :] + y_buf[u]
        if u < WIDE:
            out[rows, :] = total
        else:
            narrow[core, u - WIDE, z] = total.astype(BF16)
        for d in (u % 2, 1 - u % 2):
            spread(u, d, 0).start()
        hand_over(u, z).start()
        widen(core, u, z)

    for t in range(FAR):
        for u, d in flows:
            if t < steps(u, d):
                arrive(u, d, t).wait_recv()
                if t + 1 < steps(u, d):
                    spread(u, d, t + 1).start()
                hand_over(u, owner_at(1 - d, t + 1)).start()
                widen(core, u, owner_at(1 - d, t + 1))
                if u == d and t < FAR - d:
                    g_arrive(d, t).wait_recv()
                    if t + 1 < FAR - d:
                        g_pass(d, t + 1).start()

    total = g_z[0]
    for i in range(1, RING):
        total = total + g_z[i]
    gain_out[...] = jnp.sum(total, axis=0, keepdims=True)

    for shift in range(RING):
        to_sib(shift).wait_send()
    for u in range(STREAMS):
        for i in range(RING):
            handed_over(u, i).wait_recv()
            widen(1 - core, u, i)
            hand_over(u, i).wait_send()
    for u, d in flows:
        for t in range(steps(u, d)):
            if t > 0 or (u, d) in pairs[-1]:
                rs(u, d, t).wait_send()
            spread(u, d, t).wait_send()
    for d in range(2):
        for t in range(FAR - d):
            g_pass(d, t).wait_send()
    finish_sends()


def on_device(sections, replicas, *args):
    samples, grid_rows, features = args[0].shape
    loss_scale = 1.0 / math.sqrt(samples * replicas * grid_rows)
    total_rows = 3 * features
    chunk = total_rows // CORES // RING
    piece = chunk // STREAMS
    dma = pltpu.SemaphoreType.DMA
    v = pltpu.VMEM
    tile = (BLOCK, BLOCK)
    vmem_spec = pl.BlockSpec(memory_space=pltpu.VMEM)
    out, gain_out = pl.pallas_call(
        functools.partial(step_kernel, samples, loss_scale),
        out_shape=(
            jax.ShapeDtypeStruct((total_rows, features), F32),
            jax.ShapeDtypeStruct((1, features), F32),
        ),
        in_specs=[pl.BlockSpec(memory_space=pltpu.HBM)] * 12,
        out_specs=(vmem_spec, vmem_spec),
        scratch_shapes=[
            v((2, grid_rows, features), BF16),
            v((grid_rows, features), BF16),
            v((4,) + tile, BF16),
            v((4,) + tile, BF16),
            v((8,) + tile, BF16),
            pltpu.SMEM((4,), jnp.int32),
            pltpu.SMEM((4,), jnp.int32),
            pltpu.SMEM((8,), jnp.int32),
            v((3, LAYERS, features, features), BF16),
            v((1, features), F32),
            v((LAYERS, 8, features), F32),
            v((NODES, 2 * NODES), BF16),
            v((NODES, 2 * NODES), BF16),
            v((NODES, 2 * grid_rows), BF16),
            v((grid_rows, 2 * NODES), BF16),
            v((NODES, 2 * grid_rows), BF16),
            v((LAYERS + 3 + samples, NODES, features), BF16),
            v((LAYERS + 1 + samples, NODES, features), BF16),
            v((LAYERS + 1 + samples, NODES, features), BF16),
            v((LAYERS + 1 + samples, NODES, features), BF16),
            v((LAYERS + samples, NODES, features), BF16),
            v((LAYERS + 1 + samples, NODES, features), F32),
            v((LAYERS + 1 + samples, NODES, features), F32),
            v((LAYERS + 1 + samples, NODES, 128), F32),
            v((NODES, features), BF16),
            v((NODES, features), F32),
            v((LAYERS + samples, NODES, features), BF16),
            v((total_rows, features), F32),
            v((8, features), F32),
            v((RING, chunk, features), F32),
            v((STREAMS, 2, FAR, piece, features), F32),
            v((STREAMS, piece, features), F32),
            v((CORES, STREAMS - WIDE, RING, piece, features), BF16),
            v((8, features), F32),
            v((8, features), F32),
            v((RING, 8, features), F32),
            dma((10,)),
            dma((3,)),
            dma((3, 3)),
            dma((3, 3)),
            dma((3, 3)),
            dma((3, 3)),
            dma((3,)),
            dma((3,)),
            dma((2, CHUNKS)),
            dma((2, CHUNKS)),
            dma((2,)),
            dma((2,)),
            dma((LAYERS, 2)),
            dma((samples, 2)),
            dma((RING,)),
            dma((RING,)),
            dma((STREAMS, 2, FAR)),
            dma((STREAMS, 2, FAR)),
            dma((STREAMS,)),
            dma((STREAMS,)),
            dma((STREAMS, 2, FAR)),
            dma((STREAMS, 2, FAR)),
            dma((STREAMS, RING)),
            dma((STREAMS, RING)),
            dma((2,)),
            dma((2,)),
            dma((2, FAR)),
            dma((2, FAR)),
        ],
        compiler_params=pltpu.CompilerParams(
            collective_id=0, has_side_effects=True, vmem_limit_bytes=44 * 1024 * 1024
        ),
        name="train_step",
    )(*[pltpu.with_memory_space_constraint(a, pltpu.HBM) for a in args])
    return out.reshape(1, 3, features, features), gain_out


def solution(mesh):
    placed = (
        P("dp", None, None),
        P("dp", None, None),
        P(),
        P(),
        P(),
        P(),
        P(),
        P(),
        P("section", None, None),
        P("section", None, None),
        P("section", None, None),
        P("section", None),
    )
    return jax.shard_map(
        functools.partial(on_device, mesh.shape["section"], mesh.shape["dp"]),
        mesh=mesh,
        in_specs=placed,
        out_specs=(P("section", None, None, None), P("section", None)),
        check_vma=False,
    )
```

```python
import functools
import math

import jax
import jax.numpy as jnp
from jax import lax
from jax.experimental import pallas as pl
from jax.experimental.pallas import tpu as pltpu
from jax.sharding import PartitionSpec as P

BLOCK = 128
NODES = 256
EPSILON = 1e-05
MESH = pl.DeviceIdType.MESH
F32 = jnp.float32
BF16 = jnp.bfloat16
CHUNKS = 2
GUEST = 2
LAYERS = 4
CORES = 2
RING = 8
FAR = RING // 2
STREAMS = 4
WIDE = 2
SUM = True


def dot(a, b):
    return jnp.dot(a, b, preferred_element_type=F32)


def dot_nt(a, b):
    return lax.dot_general(a, b, (((1,), (1,)), ((), ())), preferred_element_type=F32)


def step_kernel(
    samples,
    loss_scale,
    lat_hbm,
    tgt_hbm,
    g2m_hbm,
    g2m_c_hbm,
    m2m_hbm,
    m2m_c_hbm,
    m2g_hbm,
    m2g_c_hbm,
    wm_hbm,
    wu_hbm,
    wd_hbm,
    gain_hbm,
    out,
    gain_out,
    lat,
    tgt,
    g2m,
    m2m,
    m2g,
    g2m_c,
    m2m_c,
    m2g_c,
    w,
    gain_v,
    gains,
    mix,
    mix_t,
    enc,
    pred,
    seed_t,
    h,
    up,
    unit_s,
    act_s,
    gb_s,
    slope_s,
    normed_s,
    inv_s,
    msg_s,
    up_s,
    gm_s,
    acc,
    gacc,
    sib_buf,
    ring_buf,
    y_buf,
    narrow,
    g_sib,
    g_y,
    g_z,
    in_sem,
    io_sem,
    wt_send,
    wt_recv,
    ws_send,
    ws_recv,
    gn_send,
    gn_recv,
    hop_send,
    hop_recv,
    guest_send,
    guest_recv,
    pass_send,
    pass_recv,
    sib_send,
    sib_recv,
    rs_send,
    rs_recv,
    y_send,
    y_recv,
    ag_send,
    ag_recv,
    fw_send,
    fw_recv,
    gs_sem,
    gy_sem,
    gz_send,
    gz_recv,
):
    features = w.shape[-1]
    s = lax.axis_index("section")
    dp = lax.axis_index("dp")
    core = lax.rem(dp, CORES)
    z = lax.rem(dp // CORES, RING)
    yh = dp // (CORES * RING)
    stage = s // LAYERS
    m = lax.rem(s, LAYERS)
    mx, my = m // 2, lax.rem(m, 2)
    early = stage == 0
    late = stage == 1
    j = jnp.where(early, m, 2 * (1 - mx) + my)
    busy = j < samples
    host = early & (m == 0)
    guest = early & (m == 2)

    def dp_at(y_, z_, c_):
        return {"dp": (y_ * RING + z_) * CORES + c_}

    def relative(k):
        x_ = lax.rem(mx + k // 2, 2)
        y_ = lax.rem(my + k % 2, 2)
        return 2 * x_ + y_

    y_cross = lax.rem(yh + core, 2)

    def member_at(layer):
        y_ = jnp.where(lax.rem(layer, 2) == my, yh, y_cross)
        return {"section": LAYERS * stage + layer, "dp": (y_ * RING + z) * CORES + core}

    hop_to = {"section": 2 * (3 - s // 2) + lax.rem(s, 2)}
    sibling = dp_at(yh, z, 1 - core)
    across = dp_at(1 - yh, z, core)
    z_next = lax.rem(z + 1, RING)
    z_prev = lax.rem(z + RING - 1, RING)

    def remote(src, dst, send, recv, where):
        return pltpu.make_async_remote_copy(
            src_ref=src, dst_ref=dst, send_sem=send, recv_sem=recv, device_id=where, device_id_type=MESH
        )

    barrier = pltpu.get_barrier_semaphore()

    def greet(where):
        pl.semaphore_signal(barrier, inc=1, device_id=where, device_id_type=MESH)

    greet(sibling)
    for k in (1, 2, 3):
        greet(member_at(relative(k)))
    greet(hop_to)
    met = 5
    if SUM:
        greet(across)
        greet(dp_at(yh, z_next, core))
        greet(dp_at(yh, z_prev, core))
        met += 3

    w_hbm = (wm_hbm, wu_hbm, wd_hbm)
    loads = [
        pltpu.make_async_copy(a, b, in_sem.at[i])
        for i, (a, b) in enumerate(
            [
                (g2m_c_hbm, g2m_c),
                (m2m_c_hbm, m2m_c),
                (m2g_c_hbm, m2g_c),
                (g2m_hbm, g2m),
                (m2m_hbm, m2m),
                (gain_hbm, gain_v),
                (m2g_hbm, m2g),
            ]
            + [(w_hbm[i].at[0], w.at[i, m]) for i in range(3)]
        )
    ]
    sample = jnp.minimum(j, samples - 1)
    lat_load = pltpu.make_async_copy(lat_hbm.at[sample], lat.at[0], io_sem.at[0])
    guest_load = pltpu.make_async_copy(lat_hbm.at[GUEST], lat.at[1], io_sem.at[2])
    tgt_load = pltpu.make_async_copy(tgt_hbm.at[sample], tgt, io_sem.at[1])
    for load in loads:
        load.start()
    lat_load.start()
    guest_load.start()
    tgt_load.start()

    def half_of(i, layer, c):
        rows = features // 2
        return w.at[i, layer, pl.ds(pl.multiple_of(c * rows, 16), rows)]

    def give(k, i):
        if k == 3:
            layer, where = relative(2), member_at(relative(1))
        else:
            layer, where = m, member_at(relative(k))
        rows = features // 2
        here = half_of(i, layer, core)
        src = here if k == 3 else w_hbm[i].at[0, pl.ds(pl.multiple_of(core * rows, 16), rows)]
        return remote(src, here, wt_send.at[k - 1, i], wt_recv.at[k - 1, i], where)

    def got(k, i):
        here = half_of(i, relative(k), core)
        return remote(here, here, wt_send.at[k - 1, i], wt_recv.at[k - 1, i], sibling)

    def share(k, i):
        here = half_of(i, relative(k), core)
        return remote(here, here, ws_send.at[k - 1, i], ws_recv.at[k - 1, i], sibling)

    def shared(k, i):
        here = half_of(i, relative(k), 1 - core)
        return remote(here, here, ws_send.at[k - 1, i], ws_recv.at[k - 1, i], sibling)

    def give_gain(k):
        return remote(gains.at[m], gains.at[m], gn_send.at[k - 1], gn_recv.at[k - 1], member_at(relative(k)))

    def got_gain(k):
        here = gains.at[relative(k)]
        return remote(here, here, gn_send.at[k - 1], gn_recv.at[k - 1], sibling)

    pl.semaphore_wait(barrier, met)
    give(1, 0).start()
    give(2, 0).start()
    for load in loads:
        load.wait()
    gains[m] = jnp.broadcast_to(gain_v[...], (8, features))
    for k in (1, 2, 3):
        give_gain(k).start()

    def kept_if(col, b, tile):
        return jnp.where(jnp.full(tile.shape, col, jnp.int32) == b, tile, jnp.zeros_like(tile))

    for k in range(2):
        for r in range(2):
            tile = m2m[2 * r + k]
            for b in range(2):
                kept = kept_if(m2m_c[2 * r + k], b, tile)
                mix[r * BLOCK : (r + 1) * BLOCK, (2 * k + b) * BLOCK : (2 * k + b + 1) * BLOCK] = kept
                mix_t[b * BLOCK : (b + 1) * BLOCK, (2 * k + r) * BLOCK : (2 * k + r + 1) * BLOCK] = kept.T

    lat_load.wait()
    guest_load.wait()
    tgt_load.wait()

    @pl.when(early)
    def _():
        for t in range(4):
            for b in range(4):
                k, r = t % 2, t // 2
                kept = kept_if(g2m_c[t], b, g2m[t])
                enc[r * BLOCK : (r + 1) * BLOCK, (4 * k + b) * BLOCK : (4 * k + b + 1) * BLOCK] = kept

    @pl.when(late)
    def _():
        for t in range(8):
            tile_t = m2g[t].T
            for b in range(2):
                k, r = t % 2, t // 2
                kept = kept_if(m2g_c[t], b, m2g[t])
                pred[r * BLOCK : (r + 1) * BLOCK, (2 * k + b) * BLOCK : (2 * k + b + 1) * BLOCK] = kept
                kept = kept_if(m2g_c[t], b, tile_t)
                seed_t[b * BLOCK : (b + 1) * BLOCK, (4 * k + r) * BLOCK : (4 * k + r + 1) * BLOCK] = kept

    give(1, 0).wait_send()
    give(1, 1).start()
    give(1, 2).start()
    give(2, 0).wait_send()
    give(2, 1).start()
    give(2, 2).start()

    span = NODES // CHUNKS

    def rows_of(c):
        return pl.ds(c * span, span)

    def hop_f(c):
        return remote(h.at[LAYERS, rows_of(c)], h.at[0, rows_of(c)], hop_send.at[0, c], hop_recv.at[0, c], hop_to)

    def hop_b(c):
        return remote(up.at[0, rows_of(c)], up.at[LAYERS, rows_of(c)], hop_send.at[1, c], hop_recv.at[1, c], hop_to)

    def hand_in(layer, kind):
        ref, at = ((h, layer), (up, layer + 1))[kind]
        return remote(
            ref.at[at], ref.at[LAYERS + 1 + j], pass_send.at[layer, kind], pass_recv.at[j, kind], member_at(layer)
        )

    def handed_in(i, kind):
        here = (h, up)[kind].at[LAYERS + 1 + i]
        return remote(here, here, pass_send.at[0, kind], pass_recv.at[i, kind], sibling)

    def forward(q, layer, at, output_at=None):
        gain = gains[layer, 0:1, :]
        for c in range(CHUNKS):
            rows = rows_of(c)
            x = h[at, rows, :].astype(F32)
            center = x - jnp.mean(x, axis=-1, keepdims=True)
            inverse = lax.rsqrt(jnp.mean(center * center, axis=-1, keepdims=True) + EPSILON)
            normed = center * inverse
            unit = (normed * gain).astype(BF16)
            normed_s[q, rows, :] = normed
            inv_s[q, rows, :] = jnp.broadcast_to(inverse, (span, 128))
            unit_s[q, rows, :] = unit
            msg_s[rows, :] = dot(unit, w[0, layer]).astype(BF16)
            up_s[rows, :] = dot(unit, w[1, layer])
        for c in range(CHUNKS):
            rows = rows_of(c)
            before = up_s[rows, :] + dot(mix[rows, :NODES], msg_s[...]) + dot(mix[rows, NODES:], msg_s[...])
            sigma = 1.0 / (1.0 + jnp.exp(-before))
            active = (before * sigma).astype(BF16)
            slope_s[q, rows, :] = sigma * (1.0 + before * (1.0 - sigma))
            act_s[q, rows, :] = active
            if output_at is not None:
                output = h[at, rows, :].astype(F32) + dot(active, w[2, layer])
                h[output_at, rows, :] = output.astype(BF16)

    guest_h = LAYERS + 1 + samples

    def guest_rows(n):
        return remote(h.at[guest_h + n], h.at[1 + n], guest_send.at[n], guest_recv.at[n], member_at(2))

    def encode(i, at):
        grid_rows = lat.shape[1]
        h[at] = (dot(enc[:, :grid_rows], lat[i]) + dot(enc[:, grid_rows:], lat[i])).astype(BF16)

    def decode():
        upstream = jnp.zeros((NODES, features), F32)
        for r in range(4):
            here = pl.ds(r * BLOCK, BLOCK)
            predicted = dot(pred[here, :NODES], h[LAYERS]) + dot(pred[here, NODES:], h[LAYERS])
            target = tgt[r * BLOCK : (r + 1) * BLOCK, :].astype(F32)
            residual = ((predicted - target) * loss_scale).astype(BF16)
            for k in range(2):
                part = seed_t[:, (4 * k + r) * BLOCK : (4 * k + r + 1) * BLOCK]
                upstream = upstream + dot(part, residual)
        up[LAYERS] = upstream.astype(BF16)

    def grad_unit(q, layer):
        up_s[...] = dot_nt(gb_s[q], w[1, layer]) + dot_nt(gm_s[q], w[0, layer])

    def add_gain_grads(q):
        gacc[...] += jnp.sum((up_s[...] * normed_s[q]).reshape(NODES // 8, 8, features), axis=0)

    def backward(q, layer, own):
        gain = gains[layer, 0:1, :]
        gb_s[q] = (dot_nt(up[q + 1], w[2, layer]) * slope_s[q]).astype(BF16)
        gm_s[q] = (dot(mix_t[:, :NODES], gb_s[q]) + dot(mix_t[:, NODES:], gb_s[q])).astype(BF16)
        if own:
            grad_unit(q, layer)

            @pl.when(layer == m)
            def _():
                add_gain_grads(q)

            @pl.when(late | (q > 0))
            def _():
                for c in range(CHUNKS):
                    rows = rows_of(c)
                    grad_normed = up_s[rows, :] * gain
                    normed = normed_s[q, rows, :]
                    inverse = inv_s[q, rows, :][:, :1]
                    grad_inputs = up[q + 1, rows, :].astype(F32) + inverse * (
                        grad_normed
                        - jnp.mean(grad_normed, axis=-1, keepdims=True)
                        - normed * jnp.mean(grad_normed * normed, axis=-1, keepdims=True)
                    )
                    up[q, rows, :] = grad_inputs.astype(BF16)

            @pl.when(late & (q == 0))
            def _():
                for c in range(CHUNKS):
                    hop_b(c).start()

    def add_weight_grads(q):
        for n, (left, right) in enumerate(((unit_s, gm_s), (unit_s, gb_s), (act_s, None))):
            rows = pl.ds(n * features, features)
            acc[rows, :] += dot(left[q].T, up[q + 1] if right is None else right[q])

    def round_of(l):
        last = 0
        for i in range(LAYERS):
            far = 2 * lax.rem(i // 2 + mx, 2) + lax.rem(i % 2 + my, 2)
            last = jnp.maximum(last, jnp.where(l >= i, far, 0))
        return jnp.where(early, jnp.where(guest, jnp.where(l < 2, LAYERS, 2), last), LAYERS - 1)

    @pl.loop(0, LAYERS * LAYERS)
    def _(t):
        e, l = t // LAYERS, lax.rem(t, LAYERS)

        @pl.when((e == 1) & (l == 0))
        def _():
            for k in (1, 2, 3):
                got_gain(k).wait_recv()
            for k, i in ((1, 0), (2, 0), (1, 1), (1, 2)):
                got(k, i).wait_recv()
                if k == 2:
                    give(3, i).start()
                share(k, i).start()
            for i in range(3):
                shared(1, i).wait_recv()

        @pl.when((e == 2) & (l == 0))
        def _():
            for i in (1, 2):
                got(2, i).wait_recv()
                give(3, i).start()
                share(2, i).start()
            for i in range(3):
                shared(2, i).wait_recv()

        @pl.when((e == 3) & (l == 0))
        def _():
            for i in range(3):
                got(3, i).wait_recv()
                share(3, i).start()
            for i in range(3):
                shared(3, i).wait_recv()

        @pl.when(host & (l == e) & (e < 2))
        def _():
            @pl.when(e == 0)
            def _():
                encode(1, LAYERS + 1 + GUEST)

            forward(jnp.where(e == 0, LAYERS + GUEST, LAYERS + samples), e, jnp.where(e == 0, LAYERS + 1 + GUEST, guest_h), guest_h + e)

            @pl.when(e == 1)
            def _():
                guest_rows(1).start()
                guest_rows(0).start()

        @pl.when(busy & (round_of(l) == e))
        def _():
            @pl.when(early & (l == 0))
            def _():
                encode(0, 0)

            @pl.when(late & (l == 0))
            def _():
                for c in range(CHUNKS):
                    hop_f(c).wait_recv()

            @pl.when(guest & (l == 2))
            def _():
                guest_rows(1).wait_recv()

            @pl.when(late & (l != m))
            def _():
                @pl.when(l > 0)
                def _():
                    hand_in(l, 0).start()

            forward(l, l, l, l + 1)

            @pl.when(early & (l == LAYERS - 1))
            def _():
                for c in range(CHUNKS):
                    hop_f(c).start()

    @pl.when(busy & late)
    def _():
        decode()

    @pl.when(guest)
    def _():
        guest_rows(0).wait_recv()

    @pl.when(busy)
    def _():
        @pl.loop(0, LAYERS)
        def _(l):
            @pl.when((l != m) & (early | (l == 0)) & jnp.logical_not(guest & (l == 0)))
            def _():
                hand_in(l, 0).start()

        @pl.when(m != LAYERS - 1)
        def _():
            @pl.when(late)
            def _():
                hand_in(LAYERS - 1, 1).start()

    acc[...] = jnp.zeros_like(acc)
    gacc[...] = jnp.zeros_like(gacc)

    @pl.loop(0, LAYERS + samples)
    def _(t):
        other = jnp.where(early, t, t - LAYERS)
        l = LAYERS - 1 - jnp.where(early, t - samples, t)

        again = guest & (other == j)

        @pl.when((other >= 0) & (other < samples) & ((other != j) | again) & jnp.logical_not(host & (other == GUEST)))
        def _():
            @pl.when(jnp.logical_not(again))
            def _():
                handed_in(other, 0).wait_recv()

            forward(jnp.where(again, 1, LAYERS + other), jnp.where(again, 1, m), jnp.where(again, 1, LAYERS + 1 + other))

        @pl.when(busy & (l >= 0) & (l < LAYERS))
        def _():
            @pl.when(early & (l == LAYERS - 1))
            def _():
                for c in range(CHUNKS):
                    hop_b(c).wait_recv()

                @pl.when(m != LAYERS - 1)
                def _():
                    hand_in(LAYERS - 1, 1).start()

            @pl.when(late | (l > 0) | (m == 0))
            def _():
                backward(l, l, True)

            @pl.when((l > 0) & (l - 1 != m))
            def _():
                hand_in(l - 1, 1).start()

    @pl.loop(0, samples)
    def _(t):
        i = lax.rem(j + jnp.where(host, samples - t, t), samples)
        mine = i == j

        @pl.when(jnp.logical_not(mine))
        def _():
            handed_in(i, 1).wait_recv()
            backward(LAYERS + i, m, False)

        add_weight_grads(jnp.where(mine, m, LAYERS + i))

    def finish_sends():
        for k in (1, 2, 3):
            give_gain(k).wait_send()
            for i in range(3):
                if (k, i) not in ((1, 0), (2, 0)):
                    give(k, i).wait_send()
                share(k, i).wait_send()

        @pl.when(busy)
        def _():
            for c in range(CHUNKS):

                @pl.when(early)
                def _():
                    hop_f(c).wait_send()

                @pl.when(late)
                def _():
                    hop_b(c).wait_send()

            @pl.loop(0, LAYERS)
            def _(l):
                @pl.when(l != m)
                def _():
                    @pl.when(jnp.logical_not(guest & (l == 0)))
                    def _():
                        hand_in(l, 0).wait_send()

                    hand_in(l, 1).wait_send()

        @pl.when(host)
        def _():
            for n in range(2):
                guest_rows(n).wait_send()

    def other_gain_grads():
        @pl.loop(0, samples)
        def _(i):
            @pl.when(i != j)
            def _():
                grad_unit(LAYERS + i, m)
                add_gain_grads(LAYERS + i)

    if not SUM:
        other_gain_grads()
        finish_sends()
        return

    half = acc.shape[0] // CORES
    chunk = half // RING
    piece = chunk // STREAMS

    def toward(d):
        return dp_at(yh, z_next if d == 0 else z_prev, core)

    def owner_at(d, shift):
        return lax.rem(z + (shift if d == 0 else RING - shift), RING)

    def rows_at(c, u, owner):
        return pl.ds(pl.multiple_of(c * half + owner * chunk + u * piece, 8), piece)

    def steps(u, d):
        return FAR if u % 2 == d else FAR - 1

    pairs = [((u, 0), (u + 1, 1)) for u in range(0, STREAMS, 2)] + [((u + 1, 0), (u, 1)) for u in range(0, STREAMS, 2)]
    flows = [flow for pair in pairs for flow in pair]

    def chunk_rows(c, shift):
        return pl.ds(pl.multiple_of(c * half + lax.rem(z + shift, RING) * chunk, 8), chunk)

    def to_sib(shift):
        rows = chunk_rows(1 - core, shift)
        return remote(acc.at[rows], sib_buf.at[shift], sib_send.at[shift], sib_recv.at[shift], sibling)

    def from_sib(*shifts):
        for shift in shifts:
            to_sib(shift).wait_recv()
            acc[chunk_rows(core, shift), :] += sib_buf[shift]

    g_to_sib = remote(gacc, g_sib, gs_sem.at[0], gs_sem.at[1], sibling)
    for shift in (4, 3, 5, 2, 6, 1, 7, 0):
        to_sib(shift).start()

    def rs(u, d, t):
        rows = rows_at(core, u, owner_at(d, steps(u, d) - t))
        return remote(acc.at[rows], ring_buf.at[u, d, t], rs_send.at[u, d, t], rs_recv.at[u, d, t], toward(d))

    def take(u, d, t):
        rs(u, d, t).wait_recv()
        acc[rows_at(core, u, owner_at(d, steps(u, d) - t - 1)), :] += ring_buf[u, d, t]

    def start_pair(n):
        if n > 0:
            for u, d in pairs[n - 1]:
                rs(u, d, 0).wait_send()
        for u, d in pairs[n]:
            rs(u, d, 0).start()

    from_sib(4)
    start_pair(0)
    from_sib(3, 5)
    start_pair(1)
    from_sib(2, 6)
    start_pair(2)
    from_sib(1, 7)
    start_pair(3)
    from_sib(0)
    other_gain_grads()
    g_to_sib.start()
    g_to_y = remote(gacc, g_y, gy_sem.at[0], gy_sem.at[1], across)
    for t in range(1, FAR):
        if t == 2:
            g_to_sib.wait()
            gacc[...] += g_sib[...]
            g_to_y.start()
        for u, d in flows:
            if t < steps(u, d):
                take(u, d, t - 1)
                rs(u, d, t).start()

    def y_copy(u):
        return remote(acc.at[rows_at(core, u, z)], y_buf.at[u], y_send.at[u], y_recv.at[u], across)

    for u in range(STREAMS):
        for d in (1 - u % 2, u % 2):
            take(u, d, steps(u, d) - 1)
        y_copy(u).start()

    g_to_y.wait()
    g_z[z] = gacc[...] + g_y[...]

    def g_pass(d, t):
        here = g_z.at[owner_at(1 - d, t)]
        return remote(here, here, gz_send.at[d, t], gz_recv.at[d, t], toward(d))

    def g_arrive(d, t):
        here = g_z.at[owner_at(1 - d, t + 1)]
        return remote(here, here, gz_send.at[d, t], gz_recv.at[d, t], toward(d))

    for d in range(2):
        g_pass(d, 0).start()

    def finished(c, u, owner):
        return out.at[rows_at(c, u, owner)] if u < WIDE else narrow.at[c, u - WIDE, owner]

    def widen(c, u, owner):
        if u >= WIDE:
            out[rows_at(c, u, owner), :] = narrow[c, u - WIDE, owner].astype(F32)

    def spread(u, d, t):
        here = finished(core, u, owner_at(1 - d, t))
        return remote(here, here, ag_send.at[u, d, t], ag_recv.at[u, d, t], toward(d))

    def arrive(u, d, t):
        here = finished(core, u, owner_at(1 - d, t + 1))
        return remote(here, here, ag_send.at[u, d, t], ag_recv.at[u, d, t], toward(d))

    def hand_over(u, owner):
        here = finished(core, u, owner)
        return remote(here, here, fw_send.at[u, owner], fw_recv.at[u, owner], sibling)

    def handed_over(u, owner):
        here = finished(1 - core, u, owner)
        return remote(here, here, fw_send.at[u, owner], fw_recv.at[u, owner], sibling)

    for u in range(STREAMS):
        y_copy(u).wait()
        rows = rows_at(core, u, z)
        total = acc[rows, :] + y_buf[u]
        if u < WIDE:
            out[rows, :] = total
        else:
            narrow[core, u - WIDE, z] = total.astype(BF16)
        for d in (u % 2, 1 - u % 2):
            spread(u, d, 0).start()
        hand_over(u, z).start()
        widen(core, u, z)

    for t in range(FAR):
        for u, d in flows:
            if t < steps(u, d):
                arrive(u, d, t).wait_recv()
                if t + 1 < steps(u, d):
                    spread(u, d, t + 1).start()
                hand_over(u, owner_at(1 - d, t + 1)).start()
                widen(core, u, owner_at(1 - d, t + 1))
                if u == d and t < FAR - d:
                    g_arrive(d, t).wait_recv()
                    if t + 1 < FAR - d:
                        g_pass(d, t + 1).start()

    total = g_z[0]
    for i in range(1, RING):
        total = total + g_z[i]
    gain_out[...] = jnp.sum(total, axis=0, keepdims=True)

    for shift in range(RING):
        to_sib(shift).wait_send()
    for u in range(STREAMS):
        for i in range(RING):
            handed_over(u, i).wait_recv()
            widen(1 - core, u, i)
            hand_over(u, i).wait_send()
    for u, d in flows:
        for t in range(steps(u, d)):
            if t > 0 or (u, d) in pairs[-1]:
                rs(u, d, t).wait_send()
            spread(u, d, t).wait_send()
    for d in range(2):
        for t in range(FAR - d):
            g_pass(d, t).wait_send()
    finish_sends()


def on_device(sections, replicas, *args):
    samples, grid_rows, features = args[0].shape
    loss_scale = 1.0 / math.sqrt(samples * replicas * grid_rows)
    total_rows = 3 * features
    chunk = total_rows // CORES // RING
    piece = chunk // STREAMS
    dma = pltpu.SemaphoreType.DMA
    v = pltpu.VMEM
    tile = (BLOCK, BLOCK)
    vmem_spec = pl.BlockSpec(memory_space=pltpu.VMEM)
    out, gain_out = pl.pallas_call(
        functools.partial(step_kernel, samples, loss_scale),
        out_shape=(
            jax.ShapeDtypeStruct((total_rows, features), F32),
            jax.ShapeDtypeStruct((1, features), F32),
        ),
        in_specs=[pl.BlockSpec(memory_space=pltpu.HBM)] * 12,
        out_specs=(vmem_spec, vmem_spec),
        scratch_shapes=[
            v((2, grid_rows, features), BF16),
            v((grid_rows, features), BF16),
            v((4,) + tile, BF16),
            v((4,) + tile, BF16),
            v((8,) + tile, BF16),
            pltpu.SMEM((4,), jnp.int32),
            pltpu.SMEM((4,), jnp.int32),
            pltpu.SMEM((8,), jnp.int32),
            v((3, LAYERS, features, features), BF16),
            v((1, features), F32),
            v((LAYERS, 8, features), F32),
            v((NODES, 2 * NODES), BF16),
            v((NODES, 2 * NODES), BF16),
            v((NODES, 2 * grid_rows), BF16),
            v((grid_rows, 2 * NODES), BF16),
            v((NODES, 2 * grid_rows), BF16),
            v((LAYERS + 3 + samples, NODES, features), BF16),
            v((LAYERS + 1 + samples, NODES, features), BF16),
            v((LAYERS + 1 + samples, NODES, features), BF16),
            v((LAYERS + 1 + samples, NODES, features), BF16),
            v((LAYERS + samples, NODES, features), BF16),
            v((LAYERS + 1 + samples, NODES, features), F32),
            v((LAYERS + 1 + samples, NODES, features), F32),
            v((LAYERS + 1 + samples, NODES, 128), F32),
            v((NODES, features), BF16),
            v((NODES, features), F32),
            v((LAYERS + samples, NODES, features), BF16),
            v((total_rows, features), F32),
            v((8, features), F32),
            v((RING, chunk, features), F32),
            v((STREAMS, 2, FAR, piece, features), F32),
            v((STREAMS, piece, features), F32),
            v((CORES, STREAMS - WIDE, RING, piece, features), BF16),
            v((8, features), F32),
            v((8, features), F32),
            v((RING, 8, features), F32),
            dma((10,)),
            dma((3,)),
            dma((3, 3)),
            dma((3, 3)),
            dma((3, 3)),
            dma((3, 3)),
            dma((3,)),
            dma((3,)),
            dma((2, CHUNKS)),
            dma((2, CHUNKS)),
            dma((2,)),
            dma((2,)),
            dma((LAYERS, 2)),
            dma((samples, 2)),
            dma((RING,)),
            dma((RING,)),
            dma((STREAMS, 2, FAR)),
            dma((STREAMS, 2, FAR)),
            dma((STREAMS,)),
            dma((STREAMS,)),
            dma((STREAMS, 2, FAR)),
            dma((STREAMS, 2, FAR)),
            dma((STREAMS, RING)),
            dma((STREAMS, RING)),
            dma((2,)),
            dma((2,)),
            dma((2, FAR)),
            dma((2, FAR)),
        ],
        compiler_params=pltpu.CompilerParams(
            collective_id=0, has_side_effects=True, vmem_limit_bytes=44 * 1024 * 1024
        ),
        name="train_step",
    )(*[pltpu.with_memory_space_constraint(a, pltpu.HBM) for a in args])
    return out.reshape(1, 3, features, features), gain_out


def solution(mesh):
    placed = (
        P("dp", None, None),
        P("dp", None, None),
        P(),
        P(),
        P(),
        P(),
        P(),
        P(),
        P("section", None, None),
        P("section", None, None),
        P("section", None, None),
        P("section", None),
    )
    return jax.shard_map(
        functools.partial(on_device, mesh.shape["section"], mesh.shape["dp"]),
        mesh=mesh,
        in_specs=placed,
        out_specs=(P("section", None, None, None), P("section", None)),
        check_vma=False,
    )
```
